256 devices in a mesh: grp: 8 (over x, core), dev: 32 (over y, z).
Axes of the slice: x: 4, y: 4, z: 8, core: 2. Of those that a mesh axis runs over, the one named last changes fastest.
Arguments:
- energies: bfloat16 [32768, 32768], P(('grp', 'dev')), may hold values from -48 to 48
- triples: int32 [32768, 3], P(('grp', 'dev')), may hold values from 0 to 113, as said below
- pair_surfaces: float32 [8192, 1024], P('dev'), may hold values from -24 to 24
- pair_slot: int32 [114, 114], replicated, may hold values from 0 to 8191, as said below
- single_surfaces: float32 [128, 32], P('dev'), may hold values from -12 to 12
- modals: float32 [128, 512], P('dev'), may hold values from -1 to 1
- mode_slot: int32 [114], replicated, may hold values from 0 to 127, as said below
Outputs:
- coefficients: bfloat16 [32768, 4096], P(('grp', 'dev'))
- triple_energy: float32 [32768], P(('grp', 'dev'))
- mean_field: float32 [128, 256], P('dev')
The draws below stay inside these ranges and needn't reach their ends.
Inputs may be any that keep to these rules, and one draw needn't show every extreme that they name: The three modes of a row are distinct. Rows come in blocks of 128, one block to each device in the order of the triples' placement; all rows of a block share their first mode m, and m * (number of groups along grp) // 114 is the block's index along grp. Counting one need for each row and each of its three pairs, the rows of one block need exactly 12 surfaces from each owner along dev, the owner of pair_slot row q being q // 256. `pair_slot`: Symmetric; for two distinct modes it names the row of pair_surfaces that holds their surface, distinct pairs naming distinct rows; the diagonal is 0. `mode_slot`: distinct modes name distinct rows.
All inputs are finite; a program needn't handle non-finite values.
Results may differ from the reference program's by a relative error of at most 0.001.
Values sent between devices are 32-bit elements; how exact they have to be, the bound alone decides.
No kernel may reach another device: no remote copies, remote signals or barrier semaphores. Data moves between devices by JAX's collectives and lax.ppermute only.
A program may use at most 128 MiB of HBM per device.

```python
import jax
import jax.numpy as jnp
from jax import lax

M = 114
G = 32
KEEP = 16
S = 16
TRI_DEV = 128
TRIPLES = 32768
MODE_DEV = 4
MODE_SLOTS = 128
PAIR_DEV = 256
PAIR_SLOTS = 8192
N_GRP = 8
N_DEV = 32


def mode_layout(key):
    mode_order = jax.random.permutation(jax.random.fold_in(key, 11), M).astype(jnp.int32)
    ranking = jnp.zeros((M,), jnp.int32).at[mode_order].set(jnp.arange(M, dtype=jnp.int32))
    return (mode_order, ranking)


def draw_mode_slot(key, part):
    mode_order, ranking = mode_layout(key)
    return ranking % N_DEV * MODE_DEV + ranking // N_DEV


def draw_pair_slot(key, part):
    mode_order, ranking = mode_layout(key)
    owner_of = ranking % N_DEV
    cell_count = M * M
    mode_ids = jnp.arange(M, dtype=jnp.int32)
    above = mode_ids[:, None] < mode_ids[None, :]
    pair_owner = (owner_of[:, None] + owner_of[None, :]) % N_DEV
    priority = jax.random.permutation(jax.random.fold_in(key, 23), cell_count).astype(jnp.int32).reshape(M, M)
    sort_keys = jnp.where(above, pair_owner * cell_count + priority, N_DEV * cell_count + priority).reshape(cell_count)
    sorted_cells = jnp.argsort(sort_keys)
    position = jnp.zeros((cell_count,), jnp.int32).at[sorted_cells].set(jnp.arange(cell_count, dtype=jnp.int32))
    flat_owner = pair_owner.reshape(cell_count)
    flat_above = above.reshape(cell_count)
    owner_ids = jnp.arange(N_DEV, dtype=jnp.int32)
    per_owner = jnp.sum(((flat_owner[:, None] == owner_ids[None, :]) & flat_above[:, None]).astype(jnp.int32), axis=0)
    starts = jnp.cumsum(per_owner) - per_owner
    slot_ids = flat_owner * PAIR_DEV + position - starts[flat_owner]
    slot_table = jnp.where(flat_above, slot_ids, 0).reshape(M, M)
    return slot_table + slot_table.T


def pick_member(member_key, classes, avoid_first, avoid_second, mode_order):
    places = jnp.arange(MODE_DEV, dtype=jnp.int32)
    rank_grid = classes[:, None] + places[None, :] * N_DEV
    members = mode_order[jnp.minimum(rank_grid, M - 1)]
    usable = (rank_grid < M) & (members != avoid_first[:, None]) & (members != avoid_second[:, None])
    scores = jax.random.randint(member_key, rank_grid.shape, 0, 1 << 20) * MODE_DEV + places[None, :]
    scores = jnp.where(usable, scores, -1)
    chosen = jnp.argmax(scores, axis=1)
    return jnp.take_along_axis(members, chosen[:, None], axis=1)[:, 0]


def draw_triples(key, part):
    mode_order, ranking = mode_layout(key)

    def one_block(block_index):
        block_key = jax.random.fold_in(jax.random.fold_in(key, 37), block_index)
        group_id = block_index // N_DEV
        lowest = (group_id * M + N_GRP - 1) // N_GRP
        beyond = ((group_id + 1) * M + N_GRP - 1) // N_GRP
        leading = lowest + jax.random.randint(jax.random.fold_in(block_key, 1), (), 0, 1 << 20) % (beyond - lowest)
        row_ids = jnp.arange(TRI_DEV, dtype=jnp.int32)
        class_second = row_ids % N_DEV
        class_third = (class_second + row_ids // N_DEV % N_DEV) % N_DEV
        lead_column = jnp.zeros((TRI_DEV,), jnp.int32) + leading
        second = pick_member(jax.random.fold_in(block_key, 2), class_second, lead_column, lead_column, mode_order)
        third_mode = pick_member(jax.random.fold_in(block_key, 3), class_third, lead_column, second, mode_order)
        return jnp.stack([lead_column, second, third_mode], axis=1).astype(jnp.int32)
    blocks = jax.vmap(one_block)(jnp.arange(N_GRP * N_DEV, dtype=jnp.int32))
    return blocks.reshape(TRIPLES, 3)


def shard_levels(key, shape, shards, smallest, high):
    factor_of, own = 1.0, jax.random.fold_in(key, 6)
    for axis_at, blocks in shards:
        steps = jnp.exp(jax.random.uniform(jax.random.fold_in(own, axis_at), (blocks,), jnp.float32, smallest / len(shards), high / len(shards)))
        factor_of = factor_of * jnp.repeat(steps, shape[axis_at] // blocks).reshape([-1 if axis == axis_at else 1 for axis in range(len(shape))])
    return factor_of


def gaussian(rng, extent, deviation, bound, shards=(), kind=jnp.bfloat16):
    array = jax.random.normal(rng, extent, jnp.float32) * deviation
    if len(shards) > 0:
        array = shard_levels(rng, extent, shards, -0.22, 0.18) * array
    return jnp.clip(array, min=-bound, max=bound).astype(kind)


def setup_inputs(seed: int = 0) -> dict:
    key_list = jax.random.split(jax.random.key(seed), 8)
    energies = gaussian(key_list[0], (TRIPLES, G * G * G), 8.0, 48.0, ((0, 256),))
    triples = draw_triples(jax.random.fold_in(key_list[7], 71), 0)
    pair_surfaces = gaussian(key_list[2], (PAIR_SLOTS, G * G), 4.0, 24.0, ((0, 32),), jnp.float32)
    pair_slot = draw_pair_slot(jax.random.fold_in(key_list[7], 71), 0)
    single_surfaces = gaussian(key_list[4], (MODE_SLOTS, G), 2.0, 12.0, ((0, 32),), jnp.float32)
    modals = gaussian(key_list[5], (MODE_SLOTS, G * S), G ** -0.5, 1.0, ((0, 32),), jnp.float32)
    mode_slot = draw_mode_slot(jax.random.fold_in(key_list[7], 71), 0)
    return dict(energies=energies, triples=triples, pair_surfaces=pair_surfaces, pair_slot=pair_slot, single_surfaces=single_surfaces, modals=modals, mode_slot=mode_slot)


highest = lax.Precision.HIGHEST


def tables():
    orders = jnp.arange(KEEP, dtype=jnp.float32)
    points = jnp.arange(G, dtype=jnp.float32) + 0.5
    cosines = jnp.cos(jnp.pi * orders[:, None] * points[None, :] / G)
    weights = jnp.where(orders == 0, 1.0, 2.0) / G
    return cosines, weights[:, None] * cosines


def chebyshev_fit(values, fitter):
    number = values.shape[0]
    section_one = jnp.einsum('cg,bgx->bcx', fitter, values.reshape(number, G, G * G), precision=highest)
    section_one = section_one.reshape(number, KEEP, G, G)
    section_two = jnp.einsum('dh,bchl->bcdl', fitter, section_one, precision=highest)
    return jnp.einsum('el,bcdl->bcde', fitter, section_two, precision=highest)


def oriented(picked, lower_ends, upper_ends, width):
    square = picked.reshape(-1, width, width)
    return jnp.where((lower_ends < upper_ends)[:, None, None], square, jnp.swapaxes(square, 1, 2))


def reference(energies, triples, pair_surfaces, pair_slot, single_surfaces, modals, mode_slot):
    cosines, fitter = tables()
    shaped = modals.reshape(MODE_SLOTS, G, S)
    ground = jnp.einsum('mg,cg->mc', shaped[:, :, 0] ** 2, cosines, precision=highest)
    blocks = TRIPLES // TRI_DEV
    slot_range = jnp.arange(MODE_SLOTS, dtype=jnp.int32)

    def advance(totals, inputs):
        energy, mode_rows = inputs
        lead_mode = mode_rows[:, 0]
        second = mode_rows[:, 1]
        third_mode = mode_rows[:, 2]
        pair_first = oriented(pair_surfaces[pair_slot[lead_mode, second]], lead_mode, second, G)
        pair_second = oriented(pair_surfaces[pair_slot[lead_mode, third_mode]], lead_mode, third_mode, G)
        pair_third = oriented(pair_surfaces[pair_slot[second, third_mode]], second, third_mode, G)
        slot_first = mode_slot[lead_mode]
        slot_second = mode_slot[second]
        slot_third = mode_slot[third_mode]
        single_first = single_surfaces[slot_first]
        single_second = single_surfaces[slot_second]
        single_third = single_surfaces[slot_third]
        values = (energy.astype(jnp.float32).reshape(-1, G, G, G)
                  - pair_first[:, :, :, None] - pair_second[:, :, None, :] - pair_third[:, None, :, :]
                  - single_first[:, :, None, None] - single_second[:, None, :, None] - single_third[:, None, None, :])
        fitted = chebyshev_fit(values, fitter)
        ground_first = ground[slot_first]
        ground_second = ground[slot_second]
        ground_third = ground[slot_third]
        field_first = jnp.einsum('bcde,bd,be->bc', fitted, ground_second, ground_third, precision=highest)
        field_second = jnp.einsum('bcde,bc,be->bd', fitted, ground_first, ground_third, precision=highest)
        field_third = jnp.einsum('bcde,bc,bd->be', fitted, ground_first, ground_second, precision=highest)
        energy_out = jnp.sum(field_first * ground_first, axis=1)
        slot_ids = jnp.concatenate([slot_first, slot_second, slot_third])
        onehot = (slot_range[:, None] == slot_ids[None, :]).astype(jnp.float32)
        fields = jnp.concatenate([field_first, field_second, field_third], axis=0)
        totals = totals + jnp.dot(onehot, fields, precision=highest)
        return totals, (fitted.reshape(-1, KEEP * KEEP * KEEP).astype(jnp.bfloat16), energy_out)

    moments, (coefficients, triple_energy) = lax.scan(
        advance, jnp.zeros((MODE_SLOTS, KEEP), jnp.float32),
        (energies.reshape(blocks, TRI_DEV, G * G * G), triples.reshape(blocks, TRI_DEV, 3)))
    weighted = jnp.dot(moments, cosines, precision=highest)
    mean_field = jnp.einsum('mga,mg,mgb->mab', shaped, weighted, shaped, precision=highest).reshape(MODE_SLOTS, S * S)
    return coefficients.reshape(TRIPLES, KEEP * KEEP * KEEP), triple_energy.reshape(TRIPLES), mean_field
```

```python
import numpy as np
import jax
import jax.numpy as jnp
from jax import lax
from jax.experimental import pallas as pl
from jax.experimental.pallas import tpu as pltpu
from jax.sharding import PartitionSpec as P

G = 32
KEEP = 16
S = 16
F32 = jnp.float32
BF16 = jnp.bfloat16
HIGHEST = lax.Precision.HIGHEST
VMEM_LIMIT = 56 * 2**20


def tables():
    orders = np.arange(KEEP, dtype=np.float64)
    points = np.arange(G, dtype=np.float64) + 0.5
    cosines = np.cos(np.pi * orders[:, None] * points[None, :] / G)
    weights = np.where(orders == 0, 1.0, 2.0) / G
    return cosines, weights[:, None] * cosines


COSINES, FITTER = tables()


def halves(a):
    hi = a.astype(BF16)
    return hi, (a - hi.astype(F32)).astype(BF16)


def halves_np(a):
    a = a.astype(np.float32)
    hi = a.astype(jnp.bfloat16)
    return hi, (a - hi.astype(np.float32)).astype(jnp.bfloat16)


def dot(a, b):
    return jnp.dot(a, b, preferred_element_type=F32)


def dot_exact(a, b):
    return jnp.dot(a, b, preferred_element_type=F32, precision=HIGHEST)


def iota(shape, dim):
    return lax.broadcasted_iota(jnp.int32, shape, dim)


def lane_sum(a):
    return jnp.sum(a, axis=1, keepdims=True)


def ask_kernel(tri_ref, pair_ref, slot_ref, modal_ref, single_ref, cos_ref, fit_ref, out_ref, meta_ref):
    modes = slot_ref.shape[1]
    tri = tri_ref[...]
    first, second, third = tri[:, 0:1], tri[:, 1:2], tri[:, 2:3]
    lower = jnp.concatenate([first, first, second], axis=0)
    upper = jnp.concatenate([second, third, third], axis=0)
    each = jnp.concatenate([first, second, third], axis=0)
    rows = lower.shape[0]
    lane = iota((rows, modes), 1)
    pair = pair_ref[...]
    high = (pair >> 8).astype(F32).astype(BF16)
    low = (pair & 255).astype(F32).astype(BF16)
    pick = (lane == lower).astype(F32).astype(BF16)
    at = lane == upper
    owner = lane_sum(jnp.where(at, dot(pick, high), 0.0))
    local = lane_sum(jnp.where(at, dot(pick, low), 0.0))
    slot = lane_sum(jnp.where(lane == each, slot_ref[...].astype(F32), 0.0))
    wide = iota((rows, 128), 1)
    wide_f = wide.astype(F32)
    hit = wide_f == owner
    hit_f = hit.astype(F32)
    hit_b = hit_f.astype(BF16)
    earlier = (iota((rows, rows), 1) < iota((rows, rows), 0)).astype(F32).astype(BF16)
    rank = lane_sum(jnp.where(hit, dot(earlier, hit_b), 0.0))
    ordered = lower < upper
    is_first = iota((rows, 1), 0) < rows // 3
    turned = jnp.where(is_first, ordered.astype(F32), 1.0 - ordered.astype(F32))
    said = jnp.where(wide_f == rank, local, 0.0) + jnp.where(wide_f == rank + 16.0, turned, 0.0)
    asked = lax.dot_general(hit_b, said.astype(BF16), (((0,), (0,)), ((), ())), preferred_element_type=F32)
    square = modal_ref[...] * modal_ref[...]
    mine = dot_exact(square, cos_ref[...]) + dot_exact(single_ref[...], fit_ref[...])
    four = mine.shape
    mine = jnp.sum(jnp.where((iota(four, 1) >> 5) == iota(four, 0), mine, 0.0), axis=0, keepdims=True)
    peers = out_ref.shape[0]
    out_ref[:, 0, :] = jnp.broadcast_to(mine, (peers, 128))
    out_ref[:, 1, :] = asked[:peers]
    meta_ref[...] = jnp.where(wide == 0, owner * 24.0 + rank, jnp.where(wide == 1, slot, 0.0))


def table_kernel(pair_ref, hi_ref, lo_ref, modal_ref, cosine_ref, table_ref, integral_ref):
    a_hi, a_lo = halves(pair_ref[...])
    k_hi, k_lo = hi_ref[...], lo_ref[...]
    terms = dot(a_hi, k_hi) + dot(a_hi, k_lo) + dot(a_lo, k_hi)
    square = (256, 256)
    i, j = iota(square, 0), iota(square, 1)
    turn = (((i & 15) == (j >> 4)) & ((i >> 4) == (j & 15))).astype(F32).astype(BF16)
    t_hi, t_lo = halves(terms)
    table_ref[:, :256] = terms
    table_ref[:, 256:] = dot(t_hi, turn) + dot(t_lo, turn)
    modal = modal_ref[...]
    own = modal.shape[0]
    row = iota((own * G, G * S), 0)
    lane = iota((own * G, G * S), 1)
    spread = jnp.zeros((own * G, G * S), F32)
    for m in range(own):
        spread = jnp.where((row >> 5) == m, modal[m : m + 1, :], spread)
    spread = jnp.where((lane >> 4) == (row & 31), spread, 0.0)
    k, n = iota((G * S, 256), 0), iota((G * S, 256), 1)
    left = dot_exact(spread, ((k & 15) == (n >> 4)).astype(F32))
    right = dot_exact(spread, ((k & 15) == (n & 15)).astype(F32))
    integral_ref[...] = dot_exact(cosine_ref[...], left * right)


def answer_kernel(came_ref, table_ref, out_ref):
    asked = came_ref[:, 1, :].astype(BF16)
    rows = out_ref.shape[0]
    peers = asked.shape[0]
    at = iota((rows, 1), 0).astype(F32)
    peer = jnp.floor((at + 0.5) * (1.0 / 24.0))
    rest = at - 24.0 * peer
    late = rest >= 12.0
    rank = rest - jnp.where(late, 12.0, 0.0)
    pick = (iota((rows, peers), 1).astype(F32) == peer).astype(F32).astype(BF16)
    wide = iota((rows, 128), 1).astype(F32)
    seen = dot(pick, asked)
    local = lane_sum(jnp.where(wide == rank, seen, 0.0))
    turned = lane_sum(jnp.where(wide == rank + 16.0, seen, 0.0))
    pick = (iota((rows, 256), 1).astype(F32) == local).astype(F32).astype(BF16)
    hi, lo = halves(table_ref[...])
    both = dot(pick, hi) + dot(pick, lo)
    terms = jnp.where(turned > 0.5, both[:, 256:], both[:, :256])
    out_ref[...] = jnp.where(late, terms[:, 128:], terms[:, :128])


def fit_kernel(fit_ref, front_ref, back_ref, hi_ref, lo_ref, out_ref):
    step = pl.program_id(0)
    number = front_ref.shape[0]
    cells = G * G
    per = front_ref.shape[1] // cells
    parts = []
    for j in range(per):
        parts.append(front_ref[:, j * cells : (j + 1) * cells])
    for j in range(per):
        parts.append(back_ref[:, (per - 1 - j) * cells : (per - j) * cells])
    stacked = jnp.concatenate(parts, axis=0)
    two = dot(stacked, hi_ref[...]) + dot(stacked, lo_ref[...])
    evens, odds = [], []
    for j in range(per):
        a = two[j * number : (j + 1) * number]
        b = two[(per + j) * number : (per + j + 1) * number]
        evens.append(a + b)
        odds.append(a - b)

    def add(fresh):
        for c in range(KEEP):
            chosen = odds if c % 2 else evens
            total = chosen[0] * fit_ref[c, step * per]
            for j in range(1, per):
                total = total + chosen[j] * fit_ref[c, step * per + j]
            where = slice(c * 256, (c + 1) * 256)
            if fresh:
                out_ref[:, where] = total
            else:
                out_ref[:, where] += total

    @pl.when(step == 0)
    def _():
        add(True)

    @pl.when(step > 0)
    def _():
        add(False)


def field_kernel(fit_ref, came_ref, ground_ref, meta_ref, coef_ref, energy_ref, part_ref):
    number = fit_ref.shape[0]
    rows = meta_ref.shape[0]
    peers = ground_ref.shape[0]
    place = meta_ref[:, 0:1]
    slot = meta_ref[:, 1:2]
    home = jnp.floor((slot + 0.5) * 0.25)
    sub = slot - 4.0 * home
    lane = iota((rows, 128), 1)
    pick = (iota((rows, peers), 1).astype(F32) == home).astype(F32)
    known = dot_exact(pick, ground_ref[:, 0, :])
    known = jnp.where((lane >> 5).astype(F32) == sub, known, 0.0)
    known = known + pltpu.roll(known, 64, 1)
    known = known + pltpu.roll(known, 32, 1)
    one, two, three = (known[p * number : (p + 1) * number] for p in range(3))
    hi, lo = halves(came_ref[...])
    slots = came_ref.shape[0]
    where = iota((rows, slots), 1).astype(F32)
    got = []
    for h in range(2):
        choose = (where == place + 12.0 * h).astype(F32).astype(BF16)
        got.append(dot(choose, hi) + dot(choose, lo))
    lane = iota((number, 128), 1)
    k, n = iota((128, 256), 0), iota((128, 256), 1)
    two_wide = dot_exact(two, (k == (n >> 4)).astype(F32))
    two_single = dot_exact(two, ((k == (n >> 4) + 16) & ((n & 15) == 0)).astype(F32))
    three_low = jnp.where((lane & 31) < 16, three, 0.0)
    three_wide = three_low + pltpu.roll(three_low, 16, 1)
    start = lane < 16
    first_pair = [g[:number] for g in got]
    first_pair[0] = first_pair[0] + jnp.where(start, pltpu.roll(one, 112, 1), 0.0)
    second_pair = [g[number : 2 * number] for g in got]
    third_pair = [g[2 * number :] for g in got]
    third_pair[0] = third_pair[0] + jnp.where(start, pltpu.roll(three, 112, 1), 0.0)
    third_pair = [t + two_single[:, h * 128 : (h + 1) * 128] for h, t in enumerate(third_pair)]
    twos = [two_wide[:, :128], two_wide[:, 128:]]
    both = [w * three_wide for w in twos]
    spaced = (lane & 15) == 0
    field_first = jnp.zeros((number, 128), F32)
    lead = [jnp.zeros((number, 128), F32), jnp.zeros((number, 128), F32)]
    for c in range(KEEP):
        at_c = one[:, c : c + 1]
        along = jnp.zeros((number, 128), F32)
        for h in range(2):
            cols = slice(c * 256 + h * 128, c * 256 + (h + 1) * 128)
            moved = pltpu.roll(first_pair[h], 128 - c, 1) if c else first_pair[h]
            value = fit_ref[:, cols] - jnp.where(spaced, moved, 0.0)
            if h == 0:
                shift = (c % 8) * 16
                moved = second_pair[c // 8]
                moved = pltpu.roll(moved, 128 - shift, 1) if shift else moved
                value = value - jnp.where(start, moved, 0.0)
            if c == 0:
                value = value - third_pair[h]
            coef_ref[:, cols] = value.astype(BF16)
            along = along + value * both[h]
            lead[h] = lead[h] + at_c * value
        field_first = field_first + jnp.where(lane == c, lane_sum(along), 0.0)
    field_second = jnp.zeros((number, 128), F32)
    field_third = jnp.zeros((number, 128), F32)
    k, n = iota((128, 128), 0), iota((128, 128), 1)
    for h in range(2):
        to_second = ((k >> 4) + 8 * h == n).astype(F32)
        to_third = ((k & 15) == n).astype(F32)
        field_second = field_second + dot_exact(lead[h] * three_wide, to_second)
        field_third = field_third + dot_exact(lead[h] * twos[h], to_third)
    ones = jnp.full((8, 128), 1.0, F32)
    energy = lax.dot_general(
        ones, field_first * one, (((1,), (1,)), ((), ())), preferred_element_type=F32, precision=HIGHEST
    )
    energy_ref[...] = energy[0:1]
    fields = jnp.concatenate([field_first, field_second, field_third], axis=0)
    fields = fields + pltpu.roll(fields, 16, 1)
    fields = fields + pltpu.roll(fields, 32, 1)
    fields = jnp.where((iota((rows, 128), 1) >> 4).astype(F32) == sub, fields, 0.0)
    part = lax.dot_general(
        pick, fields, (((0,), (0,)), ((), ())), preferred_element_type=F32, precision=HIGHEST
    )
    for g in range(part_ref.shape[0]):
        part_ref[g] = part


def integral_kernel(parts_ref, integral_ref, out_ref):
    total = jnp.sum(parts_ref[...], axis=0, keepdims=True)
    shape = (out_ref.shape[0], 128)
    total = jnp.where((iota(shape, 1) >> 4) == iota(shape, 0), total, 0.0)
    out_ref[...] = dot_exact(total, integral_ref[...])


def call(kernel, outs, *args, name, smem=(), flops=0):
    vm = pl.BlockSpec(memory_space=pltpu.VMEM)
    moved = sum(int(np.prod(a.shape)) * a.dtype.itemsize for a in args) + sum(
        int(np.prod(o.shape)) * o.dtype.itemsize for o in outs
    )
    return pl.pallas_call(
        kernel,
        out_shape=outs,
        in_specs=[vm] * len(args),
        out_specs=[vm] * len(outs),
        compiler_params=pltpu.CompilerParams(vmem_limit_bytes=VMEM_LIMIT),
        cost_estimate=pl.CostEstimate(flops=flops, bytes_accessed=moved, transcendentals=0),
        name=name,
    )(*args)


def shaped(shape, dtype=F32):
    return jax.ShapeDtypeStruct(shape, dtype)


def body(energies, triples, pair_surfaces, pair_slot, single_surfaces, modals, mode_slot):
    devices = lax.axis_size("dev")
    groups = lax.axis_size("grp")
    number = triples.shape[0]
    own = modals.shape[0]
    capacity = 3 * number // devices
    cos_wide = np.zeros((G * S, 128), np.float32)
    fit_wide = np.zeros((G, 128), np.float32)
    cos_block = np.zeros((128, own * G), np.float32)
    for m in range(own):
        cos_wide[::S, m * 32 : m * 32 + KEEP] = COSINES.T
        fit_wide[:, m * 32 + KEEP : m * 32 + 2 * KEEP] = FITTER.T
        cos_block[m * KEEP : (m + 1) * KEEP, m * G : (m + 1) * G] = COSINES
    kron = np.einsum("dh,el->hlde", FITTER, FITTER).reshape(G * G, KEEP * KEEP)
    hi, lo = (jnp.asarray(x) for x in halves_np(kron))
    send, meta = call(
        ask_kernel,
        [shaped((devices, 2, 128)), shaped((3 * number, 128))],
        triples,
        pair_slot,
        mode_slot.reshape(1, -1),
        modals,
        single_surfaces,
        jnp.asarray(cos_wide),
        jnp.asarray(fit_wide),
        name="ask",
    )
    came = lax.all_to_all(send, "dev", 0, 0, tiled=True)
    table, integral = call(
        table_kernel,
        [shaped((pair_surfaces.shape[0], 512)), shaped((128, S * S))],
        pair_surfaces,
        hi,
        lo,
        modals,
        jnp.asarray(cos_block),
        name="table",
        flops=10**9,
    )
    (answer,) = call(
        answer_kernel, [shaped((devices * 2 * capacity, 128))], came, table, name="answer"
    )
    terms = lax.all_to_all(
        answer.reshape(devices, 2 * capacity, 128), "dev", 0, 0, tiled=True
    ).reshape(devices * 2 * capacity, 128)
    per = 2
    steps = G // (2 * per)
    block = per * G * G
    fitted = pl.pallas_call(
        fit_kernel,
        grid=(steps,),
        out_shape=shaped((number, KEEP**3)),
        in_specs=[
            pl.BlockSpec(memory_space=pltpu.SMEM),
            pl.BlockSpec((number, block), lambda i: (0, i)),
            pl.BlockSpec((number, block), lambda i: (0, 2 * steps - 1 - i)),
            pl.BlockSpec((G * G, 256), lambda i: (0, 0)),
            pl.BlockSpec((G * G, 256), lambda i: (0, 0)),
        ],
        out_specs=pl.BlockSpec((number, KEEP**3), lambda i: (0, 0)),
        compiler_params=pltpu.CompilerParams(vmem_limit_bytes=VMEM_LIMIT),
        cost_estimate=pl.CostEstimate(flops=5 * 10**9, bytes_accessed=11 * 2**20, transcendentals=0),
        name="fit",
    )(jnp.asarray(FITTER.astype(np.float32)), energies, energies, hi, lo)
    coefficients, energy, part = call(
        field_kernel,
        [shaped((number, KEEP**3), BF16), shaped((1, number)), shaped((groups, devices, 128))],
        fitted,
        terms,
        came,
        meta,
        name="fields",
        flops=10**9,
    )
    parts = lax.all_to_all(
        part.reshape(groups * devices, 1, 128), ("grp", "dev"), 0, 0, tiled=True
    )
    (mean_field,) = call(
        integral_kernel,
        [shaped((own, S * S))],
        parts.reshape(groups * devices, 128),
        integral,
        name="integrals",
    )
    return coefficients, energy.reshape(number), mean_field


def solution(mesh):
    in_specs = (
        P(("grp", "dev"), None),
        P(("grp", "dev"), None),
        P("dev", None),
        P(),
        P("dev", None),
        P("dev", None),
        P(),
    )
    out_specs = (P(("grp", "dev"), None), P(("grp", "dev")), P("dev", None))
    return jax.shard_map(body, mesh=mesh, in_specs=in_specs, out_specs=out_specs, check_vma=False)
```

```python
import numpy as np
import jax
import jax.numpy as jnp
from jax import lax
from jax.experimental import pallas as pl
from jax.experimental.pallas import tpu as pltpu
from jax.sharding import PartitionSpec as P

G = 32
KEEP = 16
S = 16
F32 = jnp.float32
BF16 = jnp.bfloat16
HIGHEST = lax.Precision.HIGHEST
VMEM_LIMIT = 56 * 2**20


def tables():
    orders = np.arange(KEEP, dtype=np.float64)
    points = np.arange(G, dtype=np.float64) + 0.5
    cosines = np.cos(np.pi * orders[:, None] * points[None, :] / G)
    weights = np.where(orders == 0, 1.0, 2.0) / G
    return cosines, weights[:, None] * cosines


COSINES, FITTER = tables()


def halves(a):
    hi = a.astype(BF16)
    return hi, (a - hi.astype(F32)).astype(BF16)


def halves_np(a):
    a = a.astype(np.float32)
    hi = a.astype(jnp.bfloat16)
    return hi, (a - hi.astype(np.float32)).astype(jnp.bfloat16)


def dot(a, b):
    return jnp.dot(a, b, preferred_element_type=F32)


def dot_exact(a, b):
    return jnp.dot(a, b, preferred_element_type=F32, precision=HIGHEST)


def iota(shape, dim):
    return lax.broadcasted_iota(jnp.int32, shape, dim)


def lane_sum(a):
    return jnp.sum(a, axis=1, keepdims=True)


def column(row):
    n = row.shape[1]
    return lane_sum(jnp.where(iota((n, n), 0) == iota((n, n), 1), row, 0.0))


def one_hot(column_f, width):
    return (iota((column_f.shape[0], width), 1).astype(F32) == column_f).astype(F32).astype(BF16)


def dot_two(a, b):
    hi, lo = halves(a)
    return dot(hi, b) + dot(lo, b)


def pick_two(pick, hi, lo):
    return dot(pick, hi) + dot(pick, lo)


def place_of(slot):
    home = jnp.floor((slot + 0.5) * 0.25)
    return home, slot - 4.0 * home


def ask_kernel(tri_ref, pair_ref, slot_ref, modal_ref, single_ref, cos_ref, fit_ref, out_ref, meta_ref):
    modes = slot_ref.shape[1]
    tri = tri_ref[...].astype(F32)
    first, second, third = (column(tri[p : p + 1]) for p in range(3))
    lower = jnp.concatenate([first, first, second], axis=0)
    upper = jnp.concatenate([second, third, third], axis=0)
    each = jnp.concatenate([first, second, third], axis=0)
    rows = lower.shape[0]
    number = rows // 3
    lane = iota((rows, modes), 1).astype(F32)
    pair = pair_ref[...]
    high = (pair >> 8).astype(F32).astype(BF16)
    low = (pair & 255).astype(F32).astype(BF16)
    pick = (lane == lower).astype(F32).astype(BF16)
    at = lane == upper
    owner = lane_sum(jnp.where(at, dot(pick, high), 0.0))
    local = lane_sum(jnp.where(at, dot(pick, low), 0.0))
    slot = lane_sum(jnp.where(lane == each, slot_ref[...].astype(F32), 0.0))
    wide = iota((rows, 128), 1)
    wide_f = wide.astype(F32)
    hit = wide_f == owner
    hit_b = hit.astype(F32).astype(BF16)
    earlier = (iota((rows, rows), 1) < iota((rows, rows), 0)).astype(F32).astype(BF16)
    rank = lane_sum(jnp.where(hit, dot(earlier, hit_b), 0.0))
    ordered = lower < upper
    is_first = iota((rows, 1), 0) < number
    turned = jnp.where(is_first, ordered.astype(F32), 1.0 - ordered.astype(F32))
    s1, s2, s3 = (slot[p * number : (p + 1) * number] for p in range(3))
    left = jnp.concatenate([s1, s1, s2], axis=0)
    right = jnp.concatenate([s2, s3, s3], axis=0)
    other = jnp.concatenate([s3, s2, s1], axis=0)
    small = jnp.where(ordered, left, right)
    large = jnp.where(ordered, right, left)
    off = wide_f - rank
    said = jnp.where(off == 0.0, local, 0.0)
    for k, value in enumerate((turned, small, large, other)):
        said = said + jnp.where(off == 16.0 * (k + 1), value, 0.0)
    asked = lax.dot_general(hit_b, said.astype(BF16), (((0,), (0,)), ((), ())), preferred_element_type=F32)
    square = modal_ref[...] * modal_ref[...]
    mine = dot_exact(square, cos_ref[...]) + dot_exact(single_ref[...], fit_ref[...])
    four = mine.shape
    mine = jnp.sum(jnp.where((iota(four, 1) >> 5) == iota(four, 0), mine, 0.0), axis=0, keepdims=True)
    peers = out_ref.shape[0]
    out_ref[:, 0, :] = jnp.broadcast_to(mine, (peers, 128))
    out_ref[:, 1, :] = asked[:peers]
    meta_ref[...] = jnp.where(wide == 0, owner * 25.0 + rank, jnp.where(wide == 1, slot, 0.0))


def table_kernel(pair_ref, hi_ref, lo_ref, table_hi_ref, table_lo_ref):
    a_hi, a_lo = halves(pair_ref[...])
    k_hi, k_lo = hi_ref[...], lo_ref[...]
    terms = dot(a_hi, k_hi) + dot(a_hi, k_lo) + dot(a_lo, k_hi)
    square = (256, 256)
    i, j = iota(square, 0), iota(square, 1)
    turn = (((i & 15) == (j >> 4)) & ((i >> 4) == (j & 15))).astype(F32).astype(BF16)
    t_hi, t_lo = halves(terms)
    table_hi_ref[:, :256] = t_hi
    table_lo_ref[:, :256] = t_lo
    table_hi_ref[:, 256:] = dot(t_hi, turn).astype(BF16)
    table_lo_ref[:, 256:] = dot(t_lo, turn).astype(BF16)


def unit_kernel(modal_ref, cosine_ref, integral_ref):
    modal = modal_ref[...]
    own = modal.shape[0]
    row = iota((own * G, G * S), 0)
    lane = iota((own * G, G * S), 1)
    spread = jnp.zeros((own * G, G * S), F32)
    for m in range(own):
        spread = jnp.where((row >> 5) == m, modal[m : m + 1, :], spread)
    spread = jnp.where((lane >> 4) == (row & 31), spread, 0.0)
    k, n = iota((G * S, 256), 0), iota((G * S, 256), 1)
    hi, lo = halves(spread)
    to_left = ((k & 15) == (n >> 4)).astype(F32).astype(BF16)
    to_right = ((k & 15) == (n & 15)).astype(F32).astype(BF16)
    left = dot(hi, to_left) + dot(lo, to_left)
    right = dot(hi, to_right) + dot(lo, to_right)
    integral_ref[...] = dot_exact(cosine_ref[...], left * right)


def fit_kernel(fit_ref, front_ref, back_ref, hi_ref, lo_ref, out_ref, two_ref):
    step = pl.program_id(0)
    number = front_ref.shape[0]
    cells = G * G
    per = front_ref.shape[1] // cells
    parts = [front_ref[:, j * cells : (j + 1) * cells] for j in range(per)]
    parts += [back_ref[:, (per - 1 - j) * cells : (per - j) * cells] for j in range(per)]
    stacked = jnp.concatenate(parts, axis=0)
    two = dot(stacked, hi_ref[...]) + dot(stacked, lo_ref[...])
    for j in range(per):
        a = two[j * number : (j + 1) * number]
        b = two[(per + j) * number : (per + j + 1) * number]
        two_ref[0, j] = a + b
        two_ref[1, j] = a - b

    @pl.when(step == 0)
    def _():
        out_ref[...] = jnp.zeros_like(out_ref)

    def add(q, carry):
        for parity in range(2):
            c = 2 * q + parity
            total = two_ref[parity, 0] * fit_ref[c, step * per]
            for j in range(1, per):
                total = total + two_ref[parity, j] * fit_ref[c, step * per + j]
            out_ref[c] += total
        return carry

    lax.fori_loop(0, KEEP // 2, add, 0)


def share_kernel(came_ref, hi_ref, lo_ref, fit_ref, meta_ref, out_ref, known_ref):
    peers = came_ref.shape[0]
    number = fit_ref.shape[1]
    rows = 3 * number
    asked = came_ref[:, 1, :].astype(BF16)
    per = float(rows // peers)
    at = iota((rows, 1), 0).astype(F32)
    peer = jnp.floor((at + 0.5) * (1.0 / per))
    rank = at - per * peer
    seen = dot(one_hot(peer, peers), asked)
    off = iota((rows, 128), 1).astype(F32) - rank
    local, small, large, other = (
        lane_sum(jnp.where(off == 16.0 * k, seen, 0.0)) for k in (0, 2, 3, 4)
    )
    slot = jnp.concatenate([meta_ref[:, 1:2], small, large, other], axis=0)
    home, sub = place_of(slot)
    pick = one_hot(home, peers)
    g_hi, g_lo = halves(came_ref[:, 0, :])
    lane = iota((4 * rows, 128), 1)
    known = pick_two(pick, g_hi, g_lo)
    known = jnp.where((lane >> 5).astype(F32) == sub, known, 0.0)
    known = known + pltpu.roll(known, 64, 1)
    known = known + pltpu.roll(known, 32, 1)
    known_ref[...] = known[:rows]
    k, n = iota((128, 256), 0), iota((128, 256), 1)
    widen = (k == (n >> 4)).astype(F32).astype(BF16)
    widen_single = ((k == (n >> 4) + 16) & ((n & 15) == 0)).astype(F32).astype(BF16)
    k, n = iota((256, 128), 0), iota((256, 128), 1)
    to_high = ((k >> 4) == n).astype(F32).astype(BF16)
    to_low = ((k & 15) == n).astype(F32).astype(BF16)

    def repeated(a):
        part = jnp.where((iota(a.shape, 1) & 31) < 16, a, 0.0)
        return part + pltpu.roll(part, 16, 1)

    def twice(a):
        return jnp.concatenate([a, a], axis=1)

    terms = pick_two(one_hot(local, 256), hi_ref[:, :256], lo_ref[:, :256])
    g_small, g_large, g_other = (known[p * rows : (p + 1) * rows] for p in (1, 2, 3))
    of_small = dot_two(terms * twice(repeated(g_large)), to_high)
    of_large = dot_two(terms * dot_two(g_small, widen), to_low)
    norm = g_other[:, 0:1]
    of_other = lane_sum(of_small * g_small)
    lane = iota((rows, 128), 1)
    shares = [-norm * of_small, -norm * of_large, jnp.where(lane == 0, -of_other, 0.0)]
    one, two, three = (known[p * number : (p + 1) * number] for p in range(3))
    two_wide = dot_two(two, widen)
    three_wide = twice(repeated(three))
    both = two_wide * three_wide
    lane = iota((number, 256), 1)
    single = dot_two(two, widen_single) + jnp.where(
        lane < 16, twice(pltpu.roll(three, 112, 1)), 0.0
    )
    thin = iota((number, 128), 1)
    field_first = jnp.zeros((number, 128), F32)
    lead = jnp.zeros((number, 256), F32)
    for c in range(KEEP):
        value = fit_ref[c] - jnp.where(lane == 0, one[:, 16 + c : 17 + c], 0.0)
        if c == 0:
            value = value - single
        along = value * both
        field_first = field_first + jnp.where(thin == c, lane_sum(along[:, :128] + along[:, 128:]), 0.0)
        lead = lead + one[:, c : c + 1] * value
    field_second = dot_two(lead * three_wide, to_high)
    field_third = dot_two(lead * two_wide, to_low)
    fields = jnp.concatenate([field_first, field_second, field_third] + shares, axis=0)
    fields = fields + pltpu.roll(fields, 16, 1)
    fields = fields + pltpu.roll(fields, 32, 1)
    fields = jnp.where((iota(fields.shape, 1) >> 4).astype(F32) == sub, fields, 0.0)
    f_hi, f_lo = halves(fields)
    dims = (((0,), (0,)), ((), ()))
    part = lax.dot_general(pick, f_hi, dims, preferred_element_type=F32) + lax.dot_general(
        pick, f_lo, dims, preferred_element_type=F32
    )
    slots = out_ref.shape[0]
    each = float(slots // peers)
    at = iota((slots, 1), 0).astype(F32)
    peer = jnp.floor((at + 0.5) * (1.0 / each))
    rest = at - each * peer
    late = rest >= per
    rank = rest - jnp.where(late, per, 0.0)
    from_peer = one_hot(peer, peers)
    seen = dot(from_peer, asked)
    off = iota((slots, 128), 1).astype(F32) - rank
    local = lane_sum(jnp.where(off == 0.0, seen, 0.0))
    turned = lane_sum(jnp.where(off == 16.0, seen, 0.0))
    terms = pick_two(one_hot(local, 256), hi_ref[...], lo_ref[...])
    terms = jnp.where(turned > 0.5, terms[:, 256:], terms[:, :256])
    terms = jnp.where(late, terms[:, 128:], terms[:, :128])
    p_hi, p_lo = halves(part)
    out_ref[...] = jnp.where(rest == 2.0 * per, pick_two(from_peer, p_hi, p_lo), terms)


def own_kernel(came_ref, out_ref):
    peers = came_ref.shape[0] // 25
    each = 25
    rows = came_ref[pl.ds(each - 1, peers, stride=each), :]
    total = jnp.sum(rows, axis=0, keepdims=True)
    out_ref[...] = jnp.broadcast_to(total, out_ref.shape)


def face_kernel(fit_ref, came_ref, known_ref, meta_ref, coef_ref, energy_ref):
    number = fit_ref.shape[1]
    place = meta_ref[:, 0:1]
    known = known_ref[...]
    one, two, three = (known[p * number : (p + 1) * number] for p in range(3))
    hi, lo = halves(came_ref[...])
    slots = came_ref.shape[0]
    got = [pick_two(one_hot(place + 12.0 * h, slots), hi, lo) for h in range(2)]
    lane = iota((number, 128), 1)
    k, n = iota((128, 256), 0), iota((128, 256), 1)
    two_wide = dot_two(two, (k == (n >> 4)).astype(F32).astype(BF16))
    two_single = dot_two(two, ((k == (n >> 4) + 16) & ((n & 15) == 0)).astype(F32).astype(BF16))
    three_low = jnp.where((lane & 31) < 16, three, 0.0)
    three_wide = three_low + pltpu.roll(three_low, 16, 1)
    start = lane < 16
    first_pair = [g[:number] for g in got]
    first_pair[0] = first_pair[0] + jnp.where(start, pltpu.roll(one, 112, 1), 0.0)
    second_pair = [g[number : 2 * number] for g in got]
    third_pair = [g[2 * number :] for g in got]
    third_pair[0] = third_pair[0] + jnp.where(start, pltpu.roll(three, 112, 1), 0.0)
    third_pair = [t + two_single[:, h * 128 : (h + 1) * 128] for h, t in enumerate(third_pair)]
    both = [two_wide[:, h * 128 : (h + 1) * 128] * three_wide for h in range(2)]
    spaced = (lane & 15) == 0
    energy = jnp.zeros((number, 128), F32)
    for c in range(KEEP):
        along = jnp.zeros((number, 128), F32)
        for h in range(2):
            moved = pltpu.roll(first_pair[h], 128 - c, 1) if c else first_pair[h]
            value = fit_ref[c, :, h * 128 : (h + 1) * 128] - jnp.where(spaced, moved, 0.0)
            if h == 0:
                shift = (c % 8) * 16
                moved = second_pair[c // 8]
                moved = pltpu.roll(moved, 128 - shift, 1) if shift else moved
                value = value - jnp.where(start, moved, 0.0)
            if c == 0:
                value = value - third_pair[h]
            coef_ref[:, c * 256 + h * 128 : c * 256 + (h + 1) * 128] = value.astype(BF16)
            along = along + value * both[h]
        energy = energy + one[:, c : c + 1] * along
    energy_ref[...] = lax.dot_general(
        jnp.full((8, 128), 1.0, F32), energy, (((1,), (1,)), ((), ())), preferred_element_type=F32, precision=HIGHEST
    )[0:1]


def integral_kernel(parts_ref, integral_ref, out_ref):
    total = jnp.sum(parts_ref[...], axis=0, keepdims=True)
    shape = (out_ref.shape[0], 128)
    total = jnp.where((iota(shape, 1) >> 4) == iota(shape, 0), total, 0.0)
    out_ref[...] = dot_exact(total, integral_ref[...])


def call(kernel, outs, *args, name, smem=(), flops=0):
    vm = pl.BlockSpec(memory_space=pltpu.VMEM)
    moved = sum(int(np.prod(a.shape)) * a.dtype.itemsize for a in args) + sum(
        int(np.prod(o.shape)) * o.dtype.itemsize for o in outs
    )
    return pl.pallas_call(
        kernel,
        out_shape=outs,
        in_specs=[vm] * len(args),
        out_specs=[vm] * len(outs),
        compiler_params=pltpu.CompilerParams(vmem_limit_bytes=VMEM_LIMIT),
        cost_estimate=pl.CostEstimate(flops=flops, bytes_accessed=moved, transcendentals=0),
        name=name,
    )(*args)


def shaped(shape, dtype=F32):
    return jax.ShapeDtypeStruct(shape, dtype)


def body(energies, triples, pair_surfaces, pair_slot, single_surfaces, modals, mode_slot):
    devices = lax.axis_size("dev")
    groups = lax.axis_size("grp")
    number = triples.shape[0]
    own = modals.shape[0]
    capacity = 3 * number // devices
    cos_wide = np.zeros((G * S, 128), np.float32)
    fit_wide = np.zeros((G, 128), np.float32)
    cos_block = np.zeros((128, own * G), np.float32)
    for m in range(own):
        cos_wide[::S, m * 32 : m * 32 + KEEP] = COSINES.T
        fit_wide[:, m * 32 + KEEP : m * 32 + 2 * KEEP] = FITTER.T
        cos_block[m * KEEP : (m + 1) * KEEP, m * G : (m + 1) * G] = COSINES
    kron = np.einsum("dh,el->hlde", FITTER, FITTER).reshape(G * G, KEEP * KEEP)
    hi, lo = (jnp.asarray(x) for x in halves_np(kron))
    send, meta = call(
        ask_kernel,
        [shaped((devices, 2, 128)), shaped((3 * number, 128))],
        triples.T,
        pair_slot,
        mode_slot.reshape(1, -1),
        modals,
        single_surfaces,
        jnp.asarray(cos_wide),
        jnp.asarray(fit_wide),
        name="ask",
    )
    came = lax.all_to_all(send, "dev", 0, 0, tiled=True)
    table = shaped((pair_surfaces.shape[0], 512), BF16)
    table_hi, table_lo = call(
        table_kernel, [table, table], pair_surfaces, hi, lo, name="table", flops=5 * 10**8
    )
    per = 4
    steps = G // (2 * per)
    block = per * G * G
    fitted = pl.pallas_call(
        fit_kernel,
        grid=(steps,),
        out_shape=shaped((KEEP, number, KEEP**2)),
        in_specs=[
            pl.BlockSpec(memory_space=pltpu.SMEM),
            pl.BlockSpec((number, block), lambda i: (0, i)),
            pl.BlockSpec((number, block), lambda i: (0, 2 * steps - 1 - i)),
            pl.BlockSpec((G * G, 256), lambda i: (0, 0)),
            pl.BlockSpec((G * G, 256), lambda i: (0, 0)),
        ],
        out_specs=pl.BlockSpec((KEEP, number, KEEP**2), lambda i: (0, 0, 0)),
        scratch_shapes=[pltpu.VMEM((2, per, number, 256), F32)],
        compiler_params=pltpu.CompilerParams(vmem_limit_bytes=VMEM_LIMIT),
        cost_estimate=pl.CostEstimate(flops=5 * 10**9, bytes_accessed=11 * 2**20, transcendentals=0),
        name="fit",
    )(jnp.asarray(FITTER.astype(np.float32)), energies, energies, hi, lo)
    each = 2 * capacity + 1
    answer, known = call(
        share_kernel,
        [shaped((devices * each, 128)), shaped((3 * number, 128))],
        came,
        table_hi,
        table_lo,
        fitted,
        meta,
        name="share",
        flops=10**9,
    )
    terms = lax.all_to_all(
        answer.reshape(devices, each, 1, 128), "dev", 0, 0, tiled=True
    ).reshape(devices * each, 128)
    (integral,) = call(
        unit_kernel, [shaped((128, S * S))], modals, jnp.asarray(cos_block), name="unit", flops=10**9
    )
    (mine,) = call(own_kernel, [shaped((groups, 128))], terms, name="own")
    parts = lax.all_to_all(mine.reshape(groups, 1, 128), "grp", 0, 0, tiled=True)
    coefficients, energy = call(
        face_kernel,
        [shaped((number, KEEP**3), BF16), shaped((1, number))],
        fitted,
        terms,
        known,
        meta,
        name="faces",
        flops=10**9,
    )
    (mean_field,) = call(
        integral_kernel,
        [shaped((own, S * S))],
        parts.reshape(groups, 128),
        integral,
        name="integrals",
    )
    return coefficients, energy.reshape(number), mean_field


def solution(mesh):
    in_specs = (
        P(("grp", "dev"), None),
        P(("grp", "dev"), None),
        P("dev", None),
        P(),
        P("dev", None),
        P("dev", None),
        P(),
    )
    out_specs = (P(("grp", "dev"), None), P(("grp", "dev")), P("dev", None))
    return jax.shard_map(body, mesh=mesh, in_specs=in_specs, out_specs=out_specs, check_vma=False)
```

```python
import numpy as np
import jax
import jax.numpy as jnp
from jax import lax
from jax.experimental import pallas as pl
from jax.experimental.pallas import tpu as pltpu
from jax.sharding import PartitionSpec as P

G = 32
KEEP = 16
S = 16
F32 = jnp.float32
BF16 = jnp.bfloat16
HIGHEST = lax.Precision.HIGHEST
VMEM_LIMIT = 24 * 2**20
LARGE_LIMIT = 52 * 2**20


def tables():
    orders = np.arange(KEEP, dtype=np.float64)
    points = np.arange(G, dtype=np.float64) + 0.5
    cosines = np.cos(np.pi * orders[:, None] * points[None, :] / G)
    weights = np.where(orders == 0, 1.0, 2.0) / G
    return cosines, weights[:, None] * cosines


COSINES, FITTER = tables()


def halves(a):
    hi = a.astype(BF16)
    return hi, (a - hi.astype(F32)).astype(BF16)


def halves_np(a):
    a = a.astype(np.float32)
    hi = a.astype(jnp.bfloat16)
    return hi, (a - hi.astype(np.float32)).astype(jnp.bfloat16)


def dot(a, b):
    return jnp.dot(a, b, preferred_element_type=F32)


def dot_exact(a, b):
    return jnp.dot(a, b, preferred_element_type=F32, precision=HIGHEST)


def iota(shape, dim):
    return lax.broadcasted_iota(jnp.int32, shape, dim)


def lane_sum(a):
    return jnp.sum(a, axis=1, keepdims=True)


def column(row):
    n = row.shape[1]
    return lane_sum(jnp.where(iota((n, n), 0) == iota((n, n), 1), row, 0.0))


def one_hot(column_f, width):
    return (iota((column_f.shape[0], width), 1).astype(F32) == column_f).astype(F32).astype(BF16)


def dot_two(a, b):
    hi, lo = halves(a)
    return dot(hi, b) + dot(lo, b)


def pick_two(pick, hi, lo):
    return dot(pick, hi) + dot(pick, lo)


def place_of(slot):
    home = jnp.floor((slot + 0.5) * 0.25)
    return home, slot - 4.0 * home


def ask_kernel(tri_ref, pair_ref, slot_ref, modal_ref, single_ref, cos_ref, fit_ref, out_ref, meta_ref):
    modes = slot_ref.shape[1]
    tri = tri_ref[...].astype(F32)
    first, second, third = (column(tri[p : p + 1]) for p in range(3))
    lower = jnp.concatenate([first, first, second], axis=0)
    upper = jnp.concatenate([second, third, third], axis=0)
    each = jnp.concatenate([first, second, third], axis=0)
    rows = lower.shape[0]
    number = rows // 3
    lane = iota((rows, modes), 1).astype(F32)
    pair = pair_ref[...]
    high = (pair >> 8).astype(F32).astype(BF16)
    low = (pair & 255).astype(F32).astype(BF16)
    pick = (lane == lower).astype(F32).astype(BF16)
    at = lane == upper
    owner = lane_sum(jnp.where(at, dot(pick, high), 0.0))
    local = lane_sum(jnp.where(at, dot(pick, low), 0.0))
    slot = lane_sum(jnp.where(lane == each, slot_ref[...].astype(F32), 0.0))
    wide = iota((rows, 128), 1)
    wide_f = wide.astype(F32)
    hit = wide_f == owner
    hit_b = hit.astype(F32).astype(BF16)
    earlier = (iota((rows, rows), 1) < iota((rows, rows), 0)).astype(F32).astype(BF16)
    rank = lane_sum(jnp.where(hit, dot(earlier, hit_b), 0.0))
    ordered = lower < upper
    is_first = iota((rows, 1), 0) < number
    turned = jnp.where(is_first, ordered.astype(F32), 1.0 - ordered.astype(F32))
    s1, s2, s3 = (slot[p * number : (p + 1) * number] for p in range(3))
    left = jnp.concatenate([s1, s1, s2], axis=0)
    right = jnp.concatenate([s2, s3, s3], axis=0)
    other = jnp.concatenate([s3, s2, s1], axis=0)
    small = jnp.where(ordered, left, right)
    large = jnp.where(ordered, right, left)
    off = wide_f - rank
    said = jnp.where(off == 0.0, local, 0.0)
    for k, value in enumerate((turned, small, large, other)):
        said = said + jnp.where(off == 16.0 * (k + 1), value, 0.0)
    asked = lax.dot_general(hit_b, said.astype(BF16), (((0,), (0,)), ((), ())), preferred_element_type=F32)
    square = modal_ref[...] * modal_ref[...]
    mine = dot_exact(square, cos_ref[...]) + dot_exact(single_ref[...], fit_ref[...])
    four = mine.shape
    mine = jnp.sum(jnp.where((iota(four, 1) >> 5) == iota(four, 0), mine, 0.0), axis=0, keepdims=True)
    peers = out_ref.shape[0]
    out_ref[:, 0, :] = jnp.broadcast_to(mine, (peers, 128))
    out_ref[:, 1, :] = asked[:peers]
    meta_ref[...] = jnp.where(wide == 0, owner * 25.0 + rank, jnp.where(wide == 1, slot, 0.0))


def table_kernel(pair_ref, hi_ref, lo_ref, table_hi_ref, table_lo_ref):
    a_hi, a_lo = halves(pair_ref[...])
    k_hi, k_lo = hi_ref[...], lo_ref[...]
    terms = dot(a_hi, k_hi) + dot(a_hi, k_lo) + dot(a_lo, k_hi)
    square = (256, 256)
    i, j = iota(square, 0), iota(square, 1)
    turn = (((i & 15) == (j >> 4)) & ((i >> 4) == (j & 15))).astype(F32).astype(BF16)
    t_hi, t_lo = halves(terms)
    table_hi_ref[:, :256] = t_hi
    table_lo_ref[:, :256] = t_lo
    table_hi_ref[:, 256:] = dot(t_hi, turn).astype(BF16)
    table_lo_ref[:, 256:] = dot(t_lo, turn).astype(BF16)


def unit_kernel(modal_ref, cosine_ref, integral_ref):
    modal = modal_ref[...]
    own = modal.shape[0]
    row = iota((own * G, G * S), 0)
    lane = iota((own * G, G * S), 1)
    spread = jnp.zeros((own * G, G * S), F32)
    for m in range(own):
        spread = jnp.where((row >> 5) == m, modal[m : m + 1, :], spread)
    spread = jnp.where((lane >> 4) == (row & 31), spread, 0.0)
    k, n = iota((G * S, 256), 0), iota((G * S, 256), 1)
    hi, lo = halves(spread)
    to_left = ((k & 15) == (n >> 4)).astype(F32).astype(BF16)
    to_right = ((k & 15) == (n & 15)).astype(F32).astype(BF16)
    left = dot(hi, to_left) + dot(lo, to_left)
    right = dot(hi, to_right) + dot(lo, to_right)
    integral_ref[...] = dot_exact(cosine_ref[...], left * right)


def fit_kernel(fit_ref, source_ref, hi_ref, lo_ref, out_ref, two_ref, energy_ref, sems):
    number = energy_ref.shape[0]
    cells = G * G
    per = two_ref.shape[1]
    steps = G // (2 * per)

    def copies(step):
        for end, block in enumerate((step, 2 * steps - 1 - step)):
            cols = pl.ds(pl.multiple_of(block * per * cells, cells), per * cells)
            yield pltpu.make_async_copy(source_ref.at[:, cols], energy_ref.at[:, cols], sems.at[step, end])

    for step in range(steps):
        for copy in copies(step):
            copy.start()
    out_ref[...] = jnp.zeros_like(out_ref)

    def step_of(step, carry):
        for copy in copies(step):
            copy.wait()
        front = pl.multiple_of(step * per * cells, cells)
        back = pl.multiple_of((2 * steps - 1 - step) * per * cells, cells)
        front = energy_ref[:, pl.ds(front, per * cells)]
        back = energy_ref[:, pl.ds(back, per * cells)]
        parts = [front[:, j * cells : (j + 1) * cells] for j in range(per)]
        parts += [back[:, (per - 1 - j) * cells : (per - j) * cells] for j in range(per)]
        stacked = jnp.concatenate(parts, axis=0)
        two = dot(stacked, hi_ref[...]) + dot(stacked, lo_ref[...])
        for j in range(per):
            a = two[j * number : (j + 1) * number]
            b = two[(per + j) * number : (per + j + 1) * number]
            two_ref[0, j] = a + b
            two_ref[1, j] = a - b

        def add(q, carry):
            for parity in range(2):
                c = 2 * q + parity
                total = two_ref[parity, 0] * fit_ref[c, step * per]
                for j in range(1, per):
                    total = total + two_ref[parity, j] * fit_ref[c, step * per + j]
                out_ref[c] += total
            return carry

        return lax.fori_loop(0, KEEP // 2, add, carry)

    lax.fori_loop(0, steps, step_of, 0)


def share_kernel(
    came_ref,
    hi_ref,
    lo_ref,
    source_ref,
    meta_ref,
    fit_ref,
    wide_ref,
    out_ref,
    known_ref,
    w1_ref,
    w23_ref,
    lead_ref,
    v_ref,
    energy_ref,
    sems,
):
    tile = 16

    def copy(r):
        rows_r = pl.ds(pl.multiple_of(r * tile, tile), tile)
        return pltpu.make_async_copy(source_ref.at[rows_r], energy_ref.at[rows_r], sems.at[r])

    for r in range(energy_ref.shape[0] // tile):
        copy(r).start()
    peers = came_ref.shape[0]
    number = energy_ref.shape[0]
    rows = 3 * number
    asked = came_ref[:, 1, :].astype(BF16)
    per = float(rows // peers)
    at = iota((rows, 1), 0).astype(F32)
    peer = jnp.floor((at + 0.5) * (1.0 / per))
    rank = at - per * peer
    seen = dot(one_hot(peer, peers), asked)
    off = iota((rows, 128), 1).astype(F32) - rank
    local, small, large, other = (
        lane_sum(jnp.where(off == 16.0 * k, seen, 0.0)) for k in (0, 2, 3, 4)
    )
    slot = jnp.concatenate([meta_ref[:, 1:2], small, large, other], axis=0)
    home, sub = place_of(slot)
    pick = one_hot(home, peers)
    g_hi, g_lo = halves(came_ref[:, 0, :])
    lane = iota((4 * rows, 128), 1)
    known = pick_two(pick, g_hi, g_lo)
    known = jnp.where((lane >> 5).astype(F32) == sub, known, 0.0)
    known = known + pltpu.roll(known, 64, 1)
    known = known + pltpu.roll(known, 32, 1)
    known_ref[...] = known[:rows]
    k, n = iota((128, 256), 0), iota((128, 256), 1)
    widen = (k == (n >> 4)).astype(F32).astype(BF16)
    k, n = iota((256, 128), 0), iota((256, 128), 1)
    to_high = ((k >> 4) == n).astype(F32).astype(BF16)
    to_low = ((k & 15) == n).astype(F32).astype(BF16)

    def repeated(a):
        part = jnp.where((iota(a.shape, 1) & 31) < 16, a, 0.0)
        return part + pltpu.roll(part, 16, 1)

    def twice(a):
        return jnp.concatenate([a, a], axis=1)

    terms = pick_two(one_hot(local, 256), hi_ref[:, :256], lo_ref[:, :256])
    g_small, g_large, g_other = (known[p * rows : (p + 1) * rows] for p in (1, 2, 3))
    of_small = dot_two(terms * twice(repeated(g_large)), to_high)
    of_large = dot_two(terms * dot_two(g_small, widen), to_low)
    norm = g_other[:, 0:1]
    of_other = lane_sum(of_small * g_small)
    lane = iota((rows, 128), 1)
    shares = [-norm * of_small, -norm * of_large, jnp.where(lane == 0, -of_other, 0.0)]
    one, two, three = (known[p * number : (p + 1) * number] for p in range(3))
    cells = G * G
    w1_ref[...] = jnp.broadcast_to(lane_sum(fit_ref[...] * one[0:1]), w1_ref.shape)
    ways = [wide_ref[p] for p in range(4)]

    def weights(a, hi, lo):
        a_hi, a_lo = halves(a[:, :32])
        return dot(a_hi, hi) + dot(a_hi, lo) + dot(a_lo, hi)

    w2 = weights(two, ways[0], ways[1])
    w3 = weights(three, ways[2], ways[3])
    w23_ref[...] = w2 * w3
    lanes = cells // 128

    def over_rows(r, carry):
        copy(r).wait()
        rows_r = pl.ds(pl.multiple_of(r * tile, tile), tile)
        w23 = [w23_ref[rows_r, k * 128 : (k + 1) * 128] for k in range(lanes)]
        thin = iota((tile, 128), 1)

        def over_points(g, state):
            v, lead = state
            x = energy_ref[rows_r, pl.ds(pl.multiple_of(g * cells, cells), cells)].astype(F32)
            w1 = w1_ref[pl.ds(g, 1), :]
            fresh, along = [], None
            for k in range(lanes):
                part = x[:, k * 128 : (k + 1) * 128]
                fresh.append(lead[k] + w1 * part)
                term = part * w23[k]
                along = term if along is None else along + term
            return v + jnp.where(thin == g, lane_sum(along), 0.0), tuple(fresh)

        none = jnp.zeros((tile, 128), F32)
        v, lead = lax.fori_loop(0, G, over_points, (none, (none,) * lanes), unroll=2)
        v_ref[rows_r, :] = v
        for k in range(lanes):
            lead_ref[rows_r, k * 128 : (k + 1) * 128] = lead[k]
        return carry

    lax.fori_loop(0, number // tile, over_rows, 0)

    def back(a, hi, lo):
        a_hi, a_lo = halves(a)
        dims = (((1,), (1,)), ((), ()))
        total = lax.dot_general(a_hi, hi, dims, preferred_element_type=F32)
        total = total + lax.dot_general(a_hi, lo, dims, preferred_element_type=F32)
        total = total + lax.dot_general(a_lo, hi, dims, preferred_element_type=F32)
        return jnp.concatenate([total, jnp.zeros((number, 96), F32)], axis=1)

    field_first = dot_exact(v_ref[:, :G], fit_ref[...])
    field_second = back(lead_ref[...] * w3, ways[0], ways[1])
    field_third = back(lead_ref[...] * w2, ways[2], ways[3])
    own = known[:rows]
    lane = iota((rows, 128), 1)
    single = jnp.where(lane < 16, pltpu.roll(own, 112, 1), 0.0)
    along = lane_sum(single * own)
    norms = own[:, 0:1]
    n1, n2, n3 = (norms[p * number : (p + 1) * number] for p in range(3))
    q1, q2, q3 = (along[p * number : (p + 1) * number] for p in range(3))
    scale = jnp.concatenate([n2 * n3, n1 * n3, n1 * n2], axis=0)
    shift = jnp.concatenate([n3 * q2 + n2 * q3, n3 * q1 + n1 * q3, n2 * q1 + n1 * q2], axis=0)
    from_grid = jnp.concatenate([field_first, field_second, field_third], axis=0)
    from_grid = from_grid - scale * single - jnp.where(lane == 0, shift, 0.0)
    fields = jnp.concatenate([from_grid] + shares, axis=0)
    fields = fields + pltpu.roll(fields, 16, 1)
    fields = fields + pltpu.roll(fields, 32, 1)
    fields = jnp.where((iota(fields.shape, 1) >> 4).astype(F32) == sub, fields, 0.0)
    f_hi, f_lo = halves(fields)
    dims = (((0,), (0,)), ((), ()))
    part = lax.dot_general(pick, f_hi, dims, preferred_element_type=F32) + lax.dot_general(
        pick, f_lo, dims, preferred_element_type=F32
    )
    slots = out_ref.shape[0]
    each = float(slots // peers)
    at = iota((slots, 1), 0).astype(F32)
    peer = jnp.floor((at + 0.5) * (1.0 / each))
    rest = at - each * peer
    late = rest >= per
    rank = rest - jnp.where(late, per, 0.0)
    from_peer = one_hot(peer, peers)
    seen = dot(from_peer, asked)
    off = iota((slots, 128), 1).astype(F32) - rank
    local = lane_sum(jnp.where(off == 0.0, seen, 0.0))
    turned = lane_sum(jnp.where(off == 16.0, seen, 0.0))
    terms = pick_two(one_hot(local, 256), hi_ref[...], lo_ref[...])
    terms = jnp.where(turned > 0.5, terms[:, 256:], terms[:, :256])
    terms = jnp.where(late, terms[:, 128:], terms[:, :128])
    p_hi, p_lo = halves(part)
    out_ref[...] = jnp.where(rest == 2.0 * per, pick_two(from_peer, p_hi, p_lo), terms)


def own_kernel(came_ref, out_ref):
    peers = came_ref.shape[0] // 25
    each = 25
    rows = came_ref[pl.ds(each - 1, peers, stride=each), :]
    total = jnp.sum(rows, axis=0, keepdims=True)
    out_ref[...] = jnp.broadcast_to(total, out_ref.shape)


def face_kernel(fit_ref, came_ref, known_ref, meta_ref, coef_ref, energy_ref):
    number = fit_ref.shape[1]
    place = meta_ref[:, 0:1]
    known = known_ref[...]
    one, two, three = (known[p * number : (p + 1) * number] for p in range(3))
    hi, lo = halves(came_ref[...])
    slots = came_ref.shape[0]
    got = [pick_two(one_hot(place + 12.0 * h, slots), hi, lo) for h in range(2)]
    lane = iota((number, 128), 1)
    k, n = iota((128, 256), 0), iota((128, 256), 1)
    two_wide = dot_two(two, (k == (n >> 4)).astype(F32).astype(BF16))
    two_single = dot_two(two, ((k == (n >> 4) + 16) & ((n & 15) == 0)).astype(F32).astype(BF16))
    three_low = jnp.where((lane & 31) < 16, three, 0.0)
    three_wide = three_low + pltpu.roll(three_low, 16, 1)
    start = lane < 16
    first_pair = [g[:number] for g in got]
    first_pair[0] = first_pair[0] + jnp.where(start, pltpu.roll(one, 112, 1), 0.0)
    second_pair = [g[number : 2 * number] for g in got]
    third_pair = [g[2 * number :] for g in got]
    third_pair[0] = third_pair[0] + jnp.where(start, pltpu.roll(three, 112, 1), 0.0)
    third_pair = [t + two_single[:, h * 128 : (h + 1) * 128] for h, t in enumerate(third_pair)]
    both = [two_wide[:, h * 128 : (h + 1) * 128] * three_wide for h in range(2)]
    spaced = (lane & 15) == 0
    energy = jnp.zeros((number, 128), F32)
    for c in range(KEEP):
        along = jnp.zeros((number, 128), F32)
        for h in range(2):
            moved = pltpu.roll(first_pair[h], 128 - c, 1) if c else first_pair[h]
            value = fit_ref[c, :, h * 128 : (h + 1) * 128] - jnp.where(spaced, moved, 0.0)
            if h == 0:
                shift = (c % 8) * 16
                moved = second_pair[c // 8]
                moved = pltpu.roll(moved, 128 - shift, 1) if shift else moved
                value = value - jnp.where(start, moved, 0.0)
            if c == 0:
                value = value - third_pair[h]
            coef_ref[:, c * 256 + h * 128 : c * 256 + (h + 1) * 128] = value.astype(BF16)
            along = along + value * both[h]
        energy = energy + one[:, c : c + 1] * along
    energy_ref[...] = lax.dot_general(
        jnp.full((8, 128), 1.0, F32), energy, (((1,), (1,)), ((), ())), preferred_element_type=F32, precision=HIGHEST
    )[0:1]


def integral_kernel(parts_ref, integral_ref, out_ref):
    total = jnp.sum(parts_ref[...], axis=0, keepdims=True)
    shape = (out_ref.shape[0], 128)
    total = jnp.where((iota(shape, 1) >> 4) == iota(shape, 0), total, 0.0)
    out_ref[...] = dot_exact(total, integral_ref[...])


def call(kernel, outs, *args, name, smem=(), apart=(), flops=0, scratch=(), room=VMEM_LIMIT):
    vm = pl.BlockSpec(memory_space=pltpu.VMEM)
    moved = sum(int(np.prod(a.shape)) * a.dtype.itemsize for a in args) + sum(
        int(np.prod(o.shape)) * o.dtype.itemsize for o in outs
    )
    return pl.pallas_call(
        kernel,
        out_shape=outs,
        in_specs=[
            pl.BlockSpec(memory_space=pltpu.SMEM if i in smem else pltpu.HBM if i in apart else pltpu.VMEM)
            for i in range(len(args))
        ],
        out_specs=[vm] * len(outs),
        scratch_shapes=list(scratch),
        compiler_params=pltpu.CompilerParams(vmem_limit_bytes=room),
        cost_estimate=pl.CostEstimate(flops=flops, bytes_accessed=moved, transcendentals=0),
        name=name,
    )(*args)


def shaped(shape, dtype=F32):
    return jax.ShapeDtypeStruct(shape, dtype)


def body(energies, triples, pair_surfaces, pair_slot, single_surfaces, modals, mode_slot):
    devices = lax.axis_size("dev")
    groups = lax.axis_size("grp")
    number = triples.shape[0]
    own = modals.shape[0]
    capacity = 3 * number // devices
    cos_wide = np.zeros((G * S, 128), np.float32)
    fit_wide = np.zeros((G, 128), np.float32)
    cos_block = np.zeros((128, own * G), np.float32)
    for m in range(own):
        cos_wide[::S, m * 32 : m * 32 + KEEP] = COSINES.T
        fit_wide[:, m * 32 + KEEP : m * 32 + 2 * KEEP] = FITTER.T
        cos_block[m * KEEP : (m + 1) * KEEP, m * G : (m + 1) * G] = COSINES
    kron = np.einsum("dh,el->hlde", FITTER, FITTER).reshape(G * G, KEEP * KEEP)
    hi, lo = (jnp.asarray(x) for x in halves_np(kron))
    fit_rows = np.zeros((G, 128), np.float32)
    fit_rows[:, :KEEP] = FITTER.T
    wide = np.zeros((2, 32, G, G))
    wide[0, :KEEP] = FITTER[:, :, None]
    wide[1, :KEEP] = FITTER[:, None, :]
    wide = jnp.asarray(np.stack([h[p] for p in range(2) for h in halves_np(wide.reshape(2, 32, G * G))]))
    send, meta = call(
        ask_kernel,
        [shaped((devices, 2, 128)), shaped((3 * number, 128))],
        triples.T,
        pair_slot,
        mode_slot.reshape(1, -1),
        modals,
        single_surfaces,
        jnp.asarray(cos_wide),
        jnp.asarray(fit_wide),
        name="ask",
    )
    came = lax.all_to_all(send, "dev", 0, 0, tiled=True)
    table = shaped((pair_surfaces.shape[0], 512), BF16)
    table_hi, table_lo = call(
        table_kernel, [table, table], pair_surfaces, hi, lo, name="table", flops=5 * 10**8
    )
    each = 2 * capacity + 1
    answer, known = call(
        share_kernel,
        [shaped((devices * each, 128)), shaped((3 * number, 128))],
        came,
        table_hi,
        table_lo,
        energies,
        meta,
        jnp.asarray(fit_rows),
        wide,
        apart=(3,),
        room=LARGE_LIMIT,
        name="share",
        flops=10**9,
        scratch=[
            pltpu.VMEM((G, 128), F32),
            pltpu.VMEM((number, G * G), F32),
            pltpu.VMEM((number, G * G), F32),
            pltpu.VMEM((number, 128), F32),
            pltpu.VMEM(energies.shape, BF16),
            pltpu.SemaphoreType.DMA((number // 16,)),
        ],
    )
    terms = lax.all_to_all(
        answer.reshape(devices, each, 1, 128), "dev", 0, 0, tiled=True
    ).reshape(devices * each, 128)
    per = 4
    (fitted,) = call(
        fit_kernel,
        [shaped((KEEP, number, KEEP**2))],
        jnp.asarray(FITTER.astype(np.float32)),
        energies,
        hi,
        lo,
        name="fit",
        flops=5 * 10**9,
        smem=(0,),
        apart=(1,),
        room=LARGE_LIMIT,
        scratch=[
            pltpu.VMEM((2, per, number, 256), F32),
            pltpu.VMEM(energies.shape, BF16),
            pltpu.SemaphoreType.DMA((G // (2 * per), 2)),
        ],
    )
    (integral,) = call(
        unit_kernel, [shaped((128, S * S))], modals, jnp.asarray(cos_block), name="unit", flops=10**9
    )
    (mine,) = call(own_kernel, [shaped((groups, 128))], terms, name="own")
    parts = lax.all_to_all(mine.reshape(groups, 1, 128), "grp", 0, 0, tiled=True)
    coefficients, energy = call(
        face_kernel,
        [shaped((number, KEEP**3), BF16), shaped((1, number))],
        fitted,
        terms,
        known,
        meta,
        name="faces",
        flops=10**9,
    )
    (mean_field,) = call(
        integral_kernel,
        [shaped((own, S * S))],
        parts.reshape(groups, 128),
        integral,
        name="integrals",
    )
    return coefficients, energy.reshape(number), mean_field


def solution(mesh):
    in_specs = (
        P(("grp", "dev"), None),
        P(("grp", "dev"), None),
        P("dev", None),
        P(),
        P("dev", None),
        P("dev", None),
        P(),
    )
    out_specs = (P(("grp", "dev"), None), P(("grp", "dev")), P("dev", None))
    return jax.shard_map(body, mesh=mesh, in_specs=in_specs, out_specs=out_specs, check_vma=False)
```

```python
import numpy as np
import jax
import jax.numpy as jnp
from jax import lax
from jax.experimental import pallas as pl
from jax.experimental.pallas import tpu as pltpu
from jax.sharding import PartitionSpec as P

G = 32
KEEP = 16
S = 16
F32 = jnp.float32
BF16 = jnp.bfloat16
HIGHEST = lax.Precision.HIGHEST
VMEM_LIMIT = 24 * 2**20


def tables():
    orders = np.arange(KEEP, dtype=np.float64)
    points = np.arange(G, dtype=np.float64) + 0.5
    cosines = np.cos(np.pi * orders[:, None] * points[None, :] / G)
    weights = np.where(orders == 0, 1.0, 2.0) / G
    return cosines, weights[:, None] * cosines


COSINES, FITTER = tables()


def halves(a):
    hi = a.astype(BF16)
    return hi, (a - hi.astype(F32)).astype(BF16)


def halves_np(a):
    a = a.astype(np.float32)
    hi = a.astype(jnp.bfloat16)
    return hi, (a - hi.astype(np.float32)).astype(jnp.bfloat16)


def dot(a, b):
    return jnp.dot(a, b, preferred_element_type=F32)


def dot_exact(a, b):
    return jnp.dot(a, b, preferred_element_type=F32, precision=HIGHEST)


def iota(shape, dim):
    return lax.broadcasted_iota(jnp.int32, shape, dim)


def lane_sum(a):
    return jnp.sum(a, axis=1, keepdims=True)


def column(row):
    n = row.shape[1]
    return lane_sum(jnp.where(iota((n, n), 0) == iota((n, n), 1), row, 0.0))


def one_hot(column_f, width):
    return (iota((column_f.shape[0], width), 1).astype(F32) == column_f).astype(F32).astype(BF16)


def dot_two(a, b):
    hi, lo = halves(a)
    return dot(hi, b) + dot(lo, b)


def pick_two(pick, hi, lo):
    return dot(pick, hi) + dot(pick, lo)


def place_of(slot):
    home = jnp.floor((slot + 0.5) * 0.25)
    return home, slot - 4.0 * home


def ask_kernel(tri_ref, pair_ref, slot_ref, modal_ref, single_ref, cos_ref, fit_ref, out_ref, meta_ref):
    modes = slot_ref.shape[1]
    tri = tri_ref[...].astype(F32)
    first, second, third = (column(tri[p : p + 1]) for p in range(3))
    lower = jnp.concatenate([first, first, second], axis=0)
    upper = jnp.concatenate([second, third, third], axis=0)
    each = jnp.concatenate([first, second, third], axis=0)
    rows = lower.shape[0]
    number = rows // 3
    lane = iota((rows, modes), 1).astype(F32)
    pair = pair_ref[...]
    high = (pair >> 8).astype(F32).astype(BF16)
    low = (pair & 255).astype(F32).astype(BF16)
    pick = (lane == lower).astype(F32).astype(BF16)
    at = lane == upper
    owner = lane_sum(jnp.where(at, dot(pick, high), 0.0))
    local = lane_sum(jnp.where(at, dot(pick, low), 0.0))
    slot = lane_sum(jnp.where(lane == each, slot_ref[...].astype(F32), 0.0))
    wide = iota((rows, 128), 1)
    wide_f = wide.astype(F32)
    hit = wide_f == owner
    hit_b = hit.astype(F32).astype(BF16)
    earlier = (iota((rows, rows), 1) < iota((rows, rows), 0)).astype(F32).astype(BF16)
    rank = lane_sum(jnp.where(hit, dot(earlier, hit_b), 0.0))
    ordered = lower < upper
    is_first = iota((rows, 1), 0) < number
    turned = jnp.where(is_first, ordered.astype(F32), 1.0 - ordered.astype(F32))
    s1, s2, s3 = (slot[p * number : (p + 1) * number] for p in range(3))
    left = jnp.concatenate([s1, s1, s2], axis=0)
    right = jnp.concatenate([s2, s3, s3], axis=0)
    other = jnp.concatenate([s3, s2, s1], axis=0)
    small = jnp.where(ordered, left, right)
    large = jnp.where(ordered, right, left)
    off = wide_f - rank
    said = jnp.where(off == 0.0, local, 0.0)
    for k, value in enumerate((turned, small, large, other)):
        said = said + jnp.where(off == 16.0 * (k + 1), value, 0.0)
    asked = lax.dot_general(hit_b, said.astype(BF16), (((0,), (0,)), ((), ())), preferred_element_type=F32)
    square = modal_ref[...] * modal_ref[...]
    mine = dot_exact(square, cos_ref[...]) + dot_exact(single_ref[...], fit_ref[...])
    four = mine.shape
    mine = jnp.sum(jnp.where((iota(four, 1) >> 5) == iota(four, 0), mine, 0.0), axis=0, keepdims=True)
    peers = out_ref.shape[0]
    out_ref[:, 0, :] = jnp.broadcast_to(mine, (peers, 128))
    out_ref[:, 1, :] = asked[:peers]
    meta_ref[...] = jnp.where(wide == 0, owner * 25.0 + rank, jnp.where(wide == 1, slot, 0.0))


def table_kernel(pair_ref, hi_ref, lo_ref, table_hi_ref, table_lo_ref):
    a_hi, a_lo = halves(pair_ref[...])
    k_hi, k_lo = hi_ref[...], lo_ref[...]
    terms = dot(a_hi, k_hi) + dot(a_hi, k_lo) + dot(a_lo, k_hi)
    square = (256, 256)
    i, j = iota(square, 0), iota(square, 1)
    turn = (((i & 15) == (j >> 4)) & ((i >> 4) == (j & 15))).astype(F32).astype(BF16)
    t_hi, t_lo = halves(terms)
    table_hi_ref[:, :256] = t_hi
    table_lo_ref[:, :256] = t_lo
    table_hi_ref[:, 256:] = dot(t_hi, turn).astype(BF16)
    table_lo_ref[:, 256:] = dot(t_lo, turn).astype(BF16)


def unit_kernel(modal_ref, cosine_ref, integral_ref):
    modal = modal_ref[...]
    own = modal.shape[0]
    row = iota((own * G, G * S), 0)
    lane = iota((own * G, G * S), 1)
    spread = jnp.zeros((own * G, G * S), F32)
    for m in range(own):
        spread = jnp.where((row >> 5) == m, modal[m : m + 1, :], spread)
    spread = jnp.where((lane >> 4) == (row & 31), spread, 0.0)
    k, n = iota((G * S, 256), 0), iota((G * S, 256), 1)
    hi, lo = halves(spread)
    to_left = ((k & 15) == (n >> 4)).astype(F32).astype(BF16)
    to_right = ((k & 15) == (n & 15)).astype(F32).astype(BF16)
    left = dot(hi, to_left) + dot(lo, to_left)
    right = dot(hi, to_right) + dot(lo, to_right)
    integral_ref[...] = dot_exact(cosine_ref[...], left * right)


def fit_kernel(
    source_ref, hi_ref, lo_ref, first_hi_ref, first_lo_ref, far_ref, energy_ref, out_ref, sems, out_sems
):
    number = energy_ref.shape[0]
    cells = G * G
    tile, few = 32, 8
    tiles = number // tile

    def copy(r):
        rows = pl.ds(pl.multiple_of(r * tile, tile), tile)
        return pltpu.make_async_copy(source_ref.at[rows], energy_ref.at[rows], sems.at[r])

    def copy_out(r):
        rows = pl.ds(pl.multiple_of(r * tile, tile), tile)
        return pltpu.make_async_copy(out_ref.at[:, rows], far_ref.at[:, rows], out_sems.at[r])

    for r in range(tiles):
        copy(r).start()

    def over_rows(r, carry):
        copy(r).wait()
        rows = pl.ds(pl.multiple_of(r * tile, tile), tile)
        stacked = jnp.concatenate([energy_ref[rows, g * cells : (g + 1) * cells] for g in range(G)], axis=0)
        two = dot(stacked, hi_ref[...]) + dot(stacked, lo_ref[...])
        for h in range(tile // few):
            part = jnp.concatenate(
                [two[g * tile + h * few : g * tile + (h + 1) * few] for g in range(G)], axis=0
            )
            p_hi, p_lo = halves(part)
            all_three = dot(first_hi_ref[...], p_hi) + dot(first_hi_ref[...], p_lo) + dot(first_lo_ref[...], p_hi)
            at = pl.ds(pl.multiple_of(r * tile + h * few, few), few)
            for c in range(KEEP):
                out_ref[c, at, :] = all_three[c * few : (c + 1) * few]
        copy_out(r).start()
        return carry

    lax.fori_loop(0, tiles, over_rows, 0)
    for r in range(tiles):
        copy_out(r).wait()


def share_kernel(
    came_ref,
    hi_ref,
    lo_ref,
    source_ref,
    meta_ref,
    fit_in,
    wide_in,
    out_ref,
    known_ref,
    w1_ref,
    w23_ref,
    lead_ref,
    along_ref,
    energy_ref,
    fit_ref,
    wide_ref,
    sems,
    more_sems,
):
    tile = 16
    tables_in = [
        pltpu.make_async_copy(fit_in, fit_ref, more_sems.at[0]),
        pltpu.make_async_copy(wide_in, wide_ref, more_sems.at[1]),
    ]
    for part in tables_in:
        part.start()

    def copy(r):
        rows_r = pl.ds(pl.multiple_of(r * tile, tile), tile)
        return pltpu.make_async_copy(source_ref.at[rows_r], energy_ref.at[rows_r], sems.at[r])

    for r in range(energy_ref.shape[0] // tile):
        copy(r).start()
    peers = came_ref.shape[0]
    number = energy_ref.shape[0]
    rows = 3 * number
    asked = came_ref[:, 1, :].astype(BF16)
    per = float(rows // peers)
    at = iota((rows, 1), 0).astype(F32)
    peer = jnp.floor((at + 0.5) * (1.0 / per))
    rank = at - per * peer
    seen = dot(one_hot(peer, peers), asked)
    off = iota((rows, 128), 1).astype(F32) - rank
    local, small, large, other = (
        lane_sum(jnp.where(off == 16.0 * k, seen, 0.0)) for k in (0, 2, 3, 4)
    )
    slot = jnp.concatenate([meta_ref[:, 1:2], small, large, other], axis=0)
    home, sub = place_of(slot)
    pick = one_hot(home, peers)
    g_hi, g_lo = halves(came_ref[:, 0, :])
    lane = iota((4 * rows, 128), 1)
    known = pick_two(pick, g_hi, g_lo)
    known = jnp.where((lane >> 5).astype(F32) == sub, known, 0.0)
    known = known + pltpu.roll(known, 64, 1)
    known = known + pltpu.roll(known, 32, 1)
    known_ref[...] = known[:rows]
    k, n = iota((128, 256), 0), iota((128, 256), 1)
    widen = (k == (n >> 4)).astype(F32).astype(BF16)
    k, n = iota((256, 128), 0), iota((256, 128), 1)
    to_high = ((k >> 4) == n).astype(F32).astype(BF16)
    to_low = ((k & 15) == n).astype(F32).astype(BF16)

    def repeated(a):
        part = jnp.where((iota(a.shape, 1) & 31) < 16, a, 0.0)
        return part + pltpu.roll(part, 16, 1)

    def twice(a):
        return jnp.concatenate([a, a], axis=1)

    terms = pick_two(one_hot(local, 256), hi_ref[:, :256], lo_ref[:, :256])
    g_small, g_large, g_other = (known[p * rows : (p + 1) * rows] for p in (1, 2, 3))
    of_small = dot_two(terms * twice(repeated(g_large)), to_high)
    of_large = dot_two(terms * dot_two(g_small, widen), to_low)
    norm = g_other[:, 0:1]
    of_other = lane_sum(of_small * g_small)
    lane = iota((rows, 128), 1)
    shares = [-norm * of_small, -norm * of_large, jnp.where(lane == 0, -of_other, 0.0)]
    one, two, three = (known[p * number : (p + 1) * number] for p in range(3))
    cells = G * G
    for part in tables_in:
        part.wait()
    w1_ref[...] = jnp.broadcast_to(lane_sum(fit_ref[...] * one[0:1]), w1_ref.shape)
    ways = [wide_ref[p] for p in range(4)]

    def weights(a, hi, lo):
        a_hi, a_lo = halves(a[:, :32])
        return dot(a_hi, hi) + dot(a_hi, lo) + dot(a_lo, hi)

    w2 = weights(two, ways[0], ways[1])
    w3 = weights(three, ways[2], ways[3])
    w23_ref[...] = w2 * w3
    lanes = cells // 128

    def over_rows(r, carry):
        copy(r).wait()
        rows_r = pl.ds(pl.multiple_of(r * tile, tile), tile)
        w23 = [w23_ref[rows_r, k * 128 : (k + 1) * 128] for k in range(lanes)]

        def over_points(g, lead):
            x = energy_ref[rows_r, pl.ds(pl.multiple_of(g * cells, cells), cells)].astype(F32)
            w1 = w1_ref[pl.ds(g, 1), :]
            fresh, along = [], None
            for k in range(lanes):
                part = x[:, k * 128 : (k + 1) * 128]
                fresh.append(lead[k] + w1 * part)
                term = part * w23[k]
                along = term if along is None else along + term
            along_ref[g, rows_r, :] = along
            return tuple(fresh)

        none = jnp.zeros((tile, 128), F32)
        lead = lax.fori_loop(0, G, over_points, (none,) * lanes, unroll=8)
        for k in range(lanes):
            lead_ref[rows_r, k * 128 : (k + 1) * 128] = lead[k]
        return carry

    lax.fori_loop(0, number // tile, over_rows, 0)

    def back(a, hi, lo):
        a_hi, a_lo = halves(a)
        dims = (((1,), (1,)), ((), ()))
        total = lax.dot_general(a_hi, hi, dims, preferred_element_type=F32)
        total = total + lax.dot_general(a_hi, lo, dims, preferred_element_type=F32)
        total = total + lax.dot_general(a_lo, hi, dims, preferred_element_type=F32)
        return jnp.concatenate([total, jnp.zeros((number, 96), F32)], axis=1)

    thin = iota((number, 128), 1)
    v = jnp.zeros((number, 128), F32)
    for g in range(G):
        v = v + jnp.where(thin == g, lane_sum(along_ref[g]), 0.0)
    field_first = dot_exact(v[:, :G], fit_ref[...])
    field_second = back(lead_ref[...] * w3, ways[0], ways[1])
    field_third = back(lead_ref[...] * w2, ways[2], ways[3])
    own = known[:rows]
    lane = iota((rows, 128), 1)
    single = jnp.where(lane < 16, pltpu.roll(own, 112, 1), 0.0)
    along = lane_sum(single * own)
    norms = own[:, 0:1]
    n1, n2, n3 = (norms[p * number : (p + 1) * number] for p in range(3))
    q1, q2, q3 = (along[p * number : (p + 1) * number] for p in range(3))
    scale = jnp.concatenate([n2 * n3, n1 * n3, n1 * n2], axis=0)
    shift = jnp.concatenate([n3 * q2 + n2 * q3, n3 * q1 + n1 * q3, n2 * q1 + n1 * q2], axis=0)
    from_grid = jnp.concatenate([field_first, field_second, field_third], axis=0)
    from_grid = from_grid - scale * single - jnp.where(lane == 0, shift, 0.0)
    fields = jnp.concatenate([from_grid] + shares, axis=0)
    fields = fields + pltpu.roll(fields, 16, 1)
    fields = fields + pltpu.roll(fields, 32, 1)
    fields = jnp.where((iota(fields.shape, 1) >> 4).astype(F32) == sub, fields, 0.0)
    f_hi, f_lo = halves(fields)
    dims = (((0,), (0,)), ((), ()))
    part = lax.dot_general(pick, f_hi, dims, preferred_element_type=F32) + lax.dot_general(
        pick, f_lo, dims, preferred_element_type=F32
    )
    slots = out_ref.shape[0]
    each = float(slots // peers)
    at = iota((slots, 1), 0).astype(F32)
    peer = jnp.floor((at + 0.5) * (1.0 / each))
    rest = at - each * peer
    late = rest >= per
    rank = rest - jnp.where(late, per, 0.0)
    from_peer = one_hot(peer, peers)
    seen = dot(from_peer, asked)
    off = iota((slots, 128), 1).astype(F32) - rank
    local = lane_sum(jnp.where(off == 0.0, seen, 0.0))
    turned = lane_sum(jnp.where(off == 16.0, seen, 0.0))
    terms = pick_two(one_hot(local, 256), hi_ref[...], lo_ref[...])
    terms = jnp.where(turned > 0.5, terms[:, 256:], terms[:, :256])
    terms = jnp.where(late, terms[:, 128:], terms[:, :128])
    p_hi, p_lo = halves(part)
    out_ref[...] = jnp.where(rest == 2.0 * per, pick_two(from_peer, p_hi, p_lo), terms)


def own_kernel(came_ref, out_ref):
    peers = came_ref.shape[0] // 25
    each = 25
    rows = came_ref[pl.ds(each - 1, peers, stride=each), :]
    total = jnp.sum(rows, axis=0, keepdims=True)
    out_ref[...] = jnp.broadcast_to(total, out_ref.shape)


def face_kernel(far_ref, came_ref, known_ref, meta_ref, coef_ref, energy_ref, fit_ref, sems):
    number = fit_ref.shape[1]
    some = 4
    copies = [
        pltpu.make_async_copy(far_ref.at[c : c + some], fit_ref.at[c : c + some], sems.at[c // some])
        for c in range(0, KEEP, some)
    ]
    for copy in copies:
        copy.start()
    place = meta_ref[:, 0:1]
    known = known_ref[...]
    one, two, three = (known[p * number : (p + 1) * number] for p in range(3))
    hi, lo = halves(came_ref[...])
    slots = came_ref.shape[0]
    got = [pick_two(one_hot(place + 12.0 * h, slots), hi, lo) for h in range(2)]
    lane = iota((number, 128), 1)
    k, n = iota((128, 256), 0), iota((128, 256), 1)
    two_wide = dot_two(two, (k == (n >> 4)).astype(F32).astype(BF16))
    two_single = dot_two(two, ((k == (n >> 4) + 16) & ((n & 15) == 0)).astype(F32).astype(BF16))
    three_low = jnp.where((lane & 31) < 16, three, 0.0)
    three_wide = three_low + pltpu.roll(three_low, 16, 1)
    start = lane < 16
    first_pair = [g[:number] for g in got]
    first_pair[0] = first_pair[0] + jnp.where(start, pltpu.roll(one, 112, 1), 0.0)
    second_pair = [g[number : 2 * number] for g in got]
    third_pair = [g[2 * number :] for g in got]
    third_pair[0] = third_pair[0] + jnp.where(start, pltpu.roll(three, 112, 1), 0.0)
    third_pair = [t + two_single[:, h * 128 : (h + 1) * 128] for h, t in enumerate(third_pair)]
    both = [two_wide[:, h * 128 : (h + 1) * 128] * three_wide for h in range(2)]
    spaced = (lane & 15) == 0
    energy = jnp.zeros((number, 128), F32)
    for c in range(KEEP):
        if c % some == 0:
            copies[c // some].wait()
        along = jnp.zeros((number, 128), F32)
        for h in range(2):
            moved = pltpu.roll(first_pair[h], 128 - c, 1) if c else first_pair[h]
            value = fit_ref[c, :, h * 128 : (h + 1) * 128] - jnp.where(spaced, moved, 0.0)
            if h == 0:
                shift = (c % 8) * 16
                moved = second_pair[c // 8]
                moved = pltpu.roll(moved, 128 - shift, 1) if shift else moved
                value = value - jnp.where(start, moved, 0.0)
            if c == 0:
                value = value - third_pair[h]
            coef_ref[:, c * 256 + h * 128 : c * 256 + (h + 1) * 128] = value.astype(BF16)
            along = along + value * both[h]
        energy = energy + one[:, c : c + 1] * along
    energy_ref[...] = lax.dot_general(
        jnp.full((8, 128), 1.0, F32), energy, (((1,), (1,)), ((), ())), preferred_element_type=F32, precision=HIGHEST
    )[0:1]


def integral_kernel(parts_ref, integral_ref, out_ref):
    total = jnp.sum(parts_ref[...], axis=0, keepdims=True)
    shape = (out_ref.shape[0], 128)
    total = jnp.where((iota(shape, 1) >> 4) == iota(shape, 0), total, 0.0)
    out_ref[...] = dot_exact(total, integral_ref[...])


def call(kernel, outs, *args, name, apart=(), fetched=(), outs_apart=False, flops=0, scratch=()):
    moved = sum(int(np.prod(a.shape)) * a.dtype.itemsize for a in args) + sum(
        int(np.prod(o.shape)) * o.dtype.itemsize for o in outs
    )
    count = len(args) + len(outs) + len(scratch)

    def fetching(*refs):
        refs, held, sems = list(refs[:count]), refs[count:-1], refs[-1]
        copies = [
            pltpu.make_async_copy(refs[i], buffer, sems.at[k])
            for k, (i, buffer) in enumerate(zip(fetched, held, strict=True))
        ]
        for copy in copies:
            copy.start()
        for copy in copies:
            copy.wait()
        for i, buffer in zip(fetched, held, strict=True):
            refs[i] = buffer
        kernel(*refs)

    extra = []
    if fetched:
        extra = [pltpu.VMEM(args[i].shape, args[i].dtype) for i in fetched]
        extra.append(pltpu.SemaphoreType.DMA((len(fetched),)))
    outside = set(apart) | set(fetched)
    return pl.pallas_call(
        fetching if fetched else kernel,
        out_shape=outs,
        in_specs=[
            pl.BlockSpec(memory_space=pltpu.HBM if i in outside else pltpu.VMEM) for i in range(len(args))
        ],
        out_specs=[pl.BlockSpec(memory_space=pltpu.HBM if outs_apart else pltpu.VMEM)] * len(outs),
        scratch_shapes=list(scratch) + extra,
        compiler_params=pltpu.CompilerParams(vmem_limit_bytes=VMEM_LIMIT),
        cost_estimate=pl.CostEstimate(flops=flops, bytes_accessed=moved, transcendentals=0),
        name=name,
    )(*(far(a) if i in outside else a for i, a in enumerate(args)))


def far(a):
    return pltpu.with_memory_space_constraint(a, pltpu.HBM)


def shaped(shape, dtype=F32):
    return jax.ShapeDtypeStruct(shape, dtype)


def body(energies, triples, pair_surfaces, pair_slot, single_surfaces, modals, mode_slot):
    devices = lax.axis_size("dev")
    groups = lax.axis_size("grp")
    number = triples.shape[0]
    own = modals.shape[0]
    capacity = 3 * number // devices
    cos_wide = np.zeros((G * S, 128), np.float32)
    fit_wide = np.zeros((G, 128), np.float32)
    cos_block = np.zeros((128, own * G), np.float32)
    for m in range(own):
        cos_wide[::S, m * 32 : m * 32 + KEEP] = COSINES.T
        fit_wide[:, m * 32 + KEEP : m * 32 + 2 * KEEP] = FITTER.T
        cos_block[m * KEEP : (m + 1) * KEEP, m * G : (m + 1) * G] = COSINES
    kron = np.einsum("dh,el->hlde", FITTER, FITTER).reshape(G * G, KEEP * KEEP)
    hi, lo = (jnp.asarray(x) for x in halves_np(kron))
    fit_rows = np.zeros((G, 128), np.float32)
    fit_rows[:, :KEEP] = FITTER.T
    wide = np.zeros((2, 32, G, G))
    wide[0, :KEEP] = FITTER[:, :, None]
    wide[1, :KEEP] = FITTER[:, None, :]
    wide = jnp.asarray(np.stack([h[p] for p in range(2) for h in halves_np(wide.reshape(2, 32, G * G))]))
    send, meta = call(
        ask_kernel,
        [shaped((devices, 2, 128)), shaped((3 * number, 128))],
        triples.T,
        pair_slot,
        mode_slot.reshape(1, -1),
        modals,
        single_surfaces,
        jnp.asarray(cos_wide),
        jnp.asarray(fit_wide),
        fetched=tuple(range(7)),
        name="ask",
    )
    came = lax.all_to_all(send, "dev", 0, 0, tiled=True)
    table = shaped((pair_surfaces.shape[0], 512), BF16)
    table_hi, table_lo = call(
        table_kernel,
        [table, table],
        pair_surfaces,
        hi,
        lo,
        fetched=(0, 1, 2),
        name="table",
        flops=5 * 10**8,
    )
    each = 2 * capacity + 1
    answer, known = call(
        share_kernel,
        [shaped((devices * each, 128)), shaped((3 * number, 128))],
        came,
        table_hi,
        table_lo,
        energies,
        meta,
        jnp.asarray(fit_rows),
        wide,
        apart=(3, 5, 6),
        name="share",
        flops=10**9,
        scratch=[
            pltpu.VMEM((G, 128), F32),
            pltpu.VMEM((number, G * G), F32),
            pltpu.VMEM((number, G * G), F32),
            pltpu.VMEM((G, number, 128), F32),
            pltpu.VMEM(energies.shape, BF16),
            pltpu.VMEM(fit_rows.shape, F32),
            pltpu.VMEM(wide.shape, BF16),
            pltpu.SemaphoreType.DMA((number // 16,)),
            pltpu.SemaphoreType.DMA((2,)),
        ],
    )
    terms = lax.all_to_all(
        answer.reshape(devices, each, 1, 128), "dev", 0, 0, tiled=True
    ).reshape(devices * each, 128)
    first_hi, first_lo = (jnp.asarray(x) for x in halves_np(np.kron(FITTER, np.eye(8))))
    (fitted,) = call(
        fit_kernel,
        [pltpu.HBM((KEEP, number, KEEP**2), F32)],
        energies,
        hi,
        lo,
        first_hi,
        first_lo,
        apart=(0,),
        outs_apart=True,
        scratch=[
            pltpu.VMEM(energies.shape, BF16),
            pltpu.VMEM((KEEP, number, KEEP**2), F32),
            pltpu.SemaphoreType.DMA((number // 32,)),
            pltpu.SemaphoreType.DMA((number // 32,)),
        ],
        name="fit",
        flops=5 * 10**9,
    )
    (integral,) = call(
        unit_kernel, [shaped((128, S * S))], modals, jnp.asarray(cos_block), name="unit", flops=10**9
    )
    (mine,) = call(own_kernel, [shaped((groups, 128))], terms, name="own")
    parts = lax.all_to_all(mine.reshape(groups, 1, 128), "grp", 0, 0, tiled=True)
    coefficients, energy = call(
        face_kernel,
        [shaped((number, KEEP**3), BF16), shaped((1, number))],
        fitted,
        terms,
        known,
        meta,
        apart=(0,),
        scratch=[pltpu.VMEM(fitted.shape, F32), pltpu.SemaphoreType.DMA((4,))],
        name="faces",
        flops=10**9,
    )
    (mean_field,) = call(
        integral_kernel,
        [shaped((own, S * S))],
        parts.reshape(groups, 128),
        integral,
        name="integrals",
    )
    return coefficients, energy.reshape(number), mean_field


def solution(mesh):
    in_specs = (
        P(("grp", "dev"), None),
        P(("grp", "dev"), None),
        P("dev", None),
        P(),
        P("dev", None),
        P("dev", None),
        P(),
    )
    out_specs = (P(("grp", "dev"), None), P(("grp", "dev")), P("dev", None))
    return jax.shard_map(body, mesh=mesh, in_specs=in_specs, out_specs=out_specs, check_vma=False)
```

```python
import numpy as np
import jax
import jax.numpy as jnp
from jax import lax
from jax.experimental import pallas as pl
from jax.experimental.pallas import tpu as pltpu
from jax.sharding import PartitionSpec as P

G = 32
KEEP = 16
S = 16
F32 = jnp.float32
BF16 = jnp.bfloat16
HIGHEST = lax.Precision.HIGHEST
VMEM_LIMIT = 24 * 2**20


def tables():
    orders = np.arange(KEEP, dtype=np.float64)
    points = np.arange(G, dtype=np.float64) + 0.5
    cosines = np.cos(np.pi * orders[:, None] * points[None, :] / G)
    weights = np.where(orders == 0, 1.0, 2.0) / G
    return cosines, weights[:, None] * cosines


COSINES, FITTER = tables()


def halves(a):
    hi = a.astype(BF16)
    return hi, (a - hi.astype(F32)).astype(BF16)


def halves_np(a):
    a = a.astype(np.float32)
    hi = a.astype(jnp.bfloat16)
    return hi, (a - hi.astype(np.float32)).astype(jnp.bfloat16)


def dot(a, b):
    return jnp.dot(a, b, preferred_element_type=F32)


def dot_exact(a, b):
    return jnp.dot(a, b, preferred_element_type=F32, precision=HIGHEST)


def iota(shape, dim):
    return lax.broadcasted_iota(jnp.int32, shape, dim)


def lane_sum(a):
    return jnp.sum(a, axis=1, keepdims=True)


def column(row):
    n = row.shape[1]
    return lane_sum(jnp.where(iota((n, n), 0) == iota((n, n), 1), row, 0.0))


def one_hot(column_f, width):
    return (iota((column_f.shape[0], width), 1).astype(F32) == column_f).astype(F32).astype(BF16)


def dot_two(a, b):
    hi, lo = halves(a)
    return dot(hi, b) + dot(lo, b)


def pick_two(pick, hi, lo):
    return dot(pick, hi) + dot(pick, lo)


def ask_kernel(tri_ref, pair_ref, slot_ref, modal_ref, single_ref, cos_ref, fit_ref, out_ref, meta_ref):
    modes = slot_ref.shape[1]
    tri = tri_ref[...].astype(F32)
    first, second, third = (column(tri[p : p + 1]) for p in range(3))
    lower = jnp.concatenate([first, first, second], axis=0)
    upper = jnp.concatenate([second, third, third], axis=0)
    each = jnp.concatenate([first, second, third], axis=0)
    rows = lower.shape[0]
    number = rows // 3
    lane = iota((rows, modes), 1).astype(F32)
    pair = pair_ref[...]
    high = (pair >> 8).astype(F32).astype(BF16)
    low = (pair & 255).astype(F32).astype(BF16)
    pick = (lane == lower).astype(F32).astype(BF16)
    at = lane == upper
    owner = lane_sum(jnp.where(at, dot(pick, high), 0.0))
    local = lane_sum(jnp.where(at, dot(pick, low), 0.0))
    slots = slot_ref[...]
    slots = ((slots & 3) * 32 + (slots >> 2)).astype(F32)
    slot = lane_sum(jnp.where(lane == each, slots, 0.0))
    wide = iota((rows, 128), 1)
    wide_f = wide.astype(F32)
    hit = wide_f == owner
    hit_b = hit.astype(F32).astype(BF16)
    earlier = (iota((rows, rows), 1) < iota((rows, rows), 0)).astype(F32).astype(BF16)
    rank = lane_sum(jnp.where(hit, dot(earlier, hit_b), 0.0))
    ordered = lower < upper
    is_first = iota((rows, 1), 0) < number
    turned = jnp.where(is_first, ordered.astype(F32), 1.0 - ordered.astype(F32))
    s1, s2, s3 = (slot[p * number : (p + 1) * number] for p in range(3))
    left = jnp.concatenate([s1, s1, s2], axis=0)
    right = jnp.concatenate([s2, s3, s3], axis=0)
    other = jnp.concatenate([s3, s2, s1], axis=0)
    small = jnp.where(ordered, left, right)
    large = jnp.where(ordered, right, left)
    off = wide_f - rank
    said = jnp.where(off == 0.0, local, 0.0)
    for k, value in enumerate((turned, small, large, other)):
        said = said + jnp.where(off == 16.0 * (k + 1), value, 0.0)
    asked = lax.dot_general(hit_b, said.astype(BF16), (((0,), (0,)), ((), ())), preferred_element_type=F32)
    square = modal_ref[...] * modal_ref[...]
    mine = dot_exact(square, cos_ref[...]) + dot_exact(single_ref[...], fit_ref[...])
    four = mine.shape
    mine = jnp.sum(jnp.where((iota(four, 1) >> 5) == iota(four, 0), mine, 0.0), axis=0, keepdims=True)
    peers = out_ref.shape[0]
    out_ref[:, 0, :] = jnp.broadcast_to(mine, (peers, 128))
    out_ref[:, 1, :] = asked[:peers]
    meta_ref[...] = jnp.where(wide == 0, owner * 25.0 + rank, jnp.where(wide == 1, slot, 0.0))


def table_kernel(pair_ref, hi_ref, lo_ref, modal_ref, cosine_ref, table_hi_ref, table_lo_ref, integral_ref):
    a_hi, a_lo = halves(pair_ref[...])
    k_hi, k_lo = hi_ref[...], lo_ref[...]
    terms = dot(a_hi, k_hi) + dot(a_hi, k_lo) + dot(a_lo, k_hi)
    square = (256, 256)
    i, j = iota(square, 0), iota(square, 1)
    turn = (((i & 15) == (j >> 4)) & ((i >> 4) == (j & 15))).astype(F32).astype(BF16)
    t_hi, t_lo = halves(terms)
    table_hi_ref[:, :256] = t_hi
    table_lo_ref[:, :256] = t_lo
    table_hi_ref[:, 256:] = dot(t_hi, turn).astype(BF16)
    table_lo_ref[:, 256:] = dot(t_lo, turn).astype(BF16)
    modal = modal_ref[...]
    own = modal.shape[0]
    row = iota((own * G, G * S), 0)
    lane = iota((own * G, G * S), 1)
    spread = jnp.zeros((own * G, G * S), F32)
    for m in range(own):
        spread = jnp.where((row >> 5) == m, modal[m : m + 1, :], spread)
    spread = jnp.where((lane >> 4) == (row & 31), spread, 0.0)
    k, n = iota((G * S, 256), 0), iota((G * S, 256), 1)
    hi, lo = halves(spread)
    to_left = ((k & 15) == (n >> 4)).astype(F32).astype(BF16)
    to_right = ((k & 15) == (n & 15)).astype(F32).astype(BF16)
    left = dot(hi, to_left) + dot(lo, to_left)
    right = dot(hi, to_right) + dot(lo, to_right)
    integral_ref[...] = dot_exact(cosine_ref[...], left * right)


def fit_kernel(
    source_ref, hi_ref, lo_ref, first_hi_ref, first_lo_ref, far_ref, energy_ref, out_ref, sems, out_sems
):
    number = energy_ref.shape[0]
    cells = G * G
    tile, few = 32, 8
    tiles = number // tile

    def copy(r):
        rows = pl.ds(pl.multiple_of(r * tile, tile), tile)
        return pltpu.make_async_copy(source_ref.at[rows], energy_ref.at[rows], sems.at[r])

    def copy_out(r):
        rows = pl.ds(pl.multiple_of(r * tile, tile), tile)
        return pltpu.make_async_copy(out_ref.at[:, rows], far_ref.at[:, rows], out_sems.at[r])

    for r in range(2):
        copy(r).start()

    def over_rows(r, carry):
        copy(r).wait()

        @pl.when(r + 2 < tiles)
        def _():
            copy(r + 2).start()

        rows = pl.ds(pl.multiple_of(r * tile, tile), tile)
        stacked = jnp.concatenate([energy_ref[rows, g * cells : (g + 1) * cells] for g in range(G)], axis=0)
        two = dot(stacked, hi_ref[...]) + dot(stacked, lo_ref[...])
        for h in range(tile // few):
            part = jnp.concatenate(
                [two[g * tile + h * few : g * tile + (h + 1) * few] for g in range(G)], axis=0
            )
            p_hi, p_lo = halves(part)
            all_three = dot(first_hi_ref[...], p_hi) + dot(first_hi_ref[...], p_lo) + dot(first_lo_ref[...], p_hi)
            at = pl.ds(pl.multiple_of(r * tile + h * few, few), few)
            for c in range(KEEP):
                out_ref[c, at, :] = all_three[c * few : (c + 1) * few]
        copy_out(r).start()
        return carry

    lax.fori_loop(0, tiles, over_rows, 0)
    for r in range(tiles):
        copy_out(r).wait()


def share_kernel(
    came_ref,
    hi_ref,
    lo_ref,
    source_ref,
    meta_ref,
    fit_in,
    wide_in,
    out_ref,
    known_ref,
    w1_ref,
    w23_ref,
    lead_ref,
    along_ref,
    energy_ref,
    fit_ref,
    wide_ref,
    sems,
    more_sems,
):
    tile = 16
    tables_in = [
        pltpu.make_async_copy(fit_in, fit_ref, more_sems.at[0]),
        pltpu.make_async_copy(wide_in, wide_ref, more_sems.at[1]),
    ]
    for part in tables_in:
        part.start()

    def copy(r):
        rows_r = pl.ds(pl.multiple_of(r * tile, tile), tile)
        return pltpu.make_async_copy(source_ref.at[rows_r], energy_ref.at[rows_r], sems.at[r])

    tiles, ahead = energy_ref.shape[0] // tile, 4
    for r in range(ahead):
        copy(r).start()
    peers = came_ref.shape[0]
    number = energy_ref.shape[0]
    rows = 3 * number
    asked = came_ref[:, 1, :].astype(BF16)
    per = float(rows // peers)
    at = iota((rows, 1), 0).astype(F32)
    peer = jnp.floor((at + 0.5) * (1.0 / per))
    rank = at - per * peer
    seen = dot(one_hot(peer, peers), asked)
    off = iota((rows, 128), 1).astype(F32) - rank
    local, small, large, other = (
        lane_sum(jnp.where(off == 16.0 * k, seen, 0.0)) for k in (0, 2, 3, 4)
    )
    slot = jnp.concatenate([meta_ref[:, 1:2], small, large, other], axis=0)
    pick = one_hot(slot, 128)
    ground = came_ref[:, 0, :]
    spots = 128 // peers
    ground = jnp.concatenate([pltpu.roll(ground, 128 - 32 * j, 1) if j else ground for j in range(spots)], axis=0)
    ground = jnp.where(iota((128, 128), 1) < 32, ground, 0.0)
    ground = ground + pltpu.roll(ground, 32, 1)
    ground = ground + pltpu.roll(ground, 64, 1)
    known = pick_two(pick, *halves(ground))
    known_ref[...] = known[:rows]
    k, n = iota((128, 256), 0), iota((128, 256), 1)
    widen = (k == (n >> 4)).astype(F32).astype(BF16)
    k, n = iota((256, 128), 0), iota((256, 128), 1)
    to_high = ((k >> 4) == n).astype(F32).astype(BF16)
    to_low = ((k & 15) == n).astype(F32).astype(BF16)

    def repeated(a):
        part = jnp.where((iota(a.shape, 1) & 31) < 16, a, 0.0)
        return part + pltpu.roll(part, 16, 1)

    def twice(a):
        return jnp.concatenate([a, a], axis=1)

    terms = pick_two(one_hot(local, 256), hi_ref[:, :256], lo_ref[:, :256])
    g_small, g_large, g_other = (known[p * rows : (p + 1) * rows] for p in (1, 2, 3))
    of_small = dot_two(terms * twice(repeated(g_large)), to_high)
    of_large = dot_two(terms * dot_two(g_small, widen), to_low)
    norm = g_other[:, 0:1]
    of_other = lane_sum(of_small * g_small)
    lane = iota((rows, 128), 1)
    shares = [-norm * of_small, -norm * of_large, jnp.where(lane == 0, -of_other, 0.0)]
    one, two, three = (known[p * number : (p + 1) * number] for p in range(3))
    cells = G * G
    for part in tables_in:
        part.wait()
    w1_ref[...] = jnp.broadcast_to(lane_sum(fit_ref[...] * one[0:1]), w1_ref.shape)
    ways = [wide_ref[p] for p in range(4)]

    def weights(a, hi, lo):
        a_hi, a_lo = halves(a[:, :32])
        return dot(a_hi, hi) + dot(a_hi, lo) + dot(a_lo, hi)

    w2 = weights(two, ways[0], ways[1])
    w3 = weights(three, ways[2], ways[3])
    w23_ref[...] = w2 * w3
    lanes = cells // 128

    def over_rows(r, carry):
        copy(r).wait()

        @pl.when(r + ahead < tiles)
        def _():
            copy(r + ahead).start()

        rows_r = pl.ds(pl.multiple_of(r * tile, tile), tile)
        w23 = [w23_ref[rows_r, k * 128 : (k + 1) * 128] for k in range(lanes)]

        def over_points(g, lead):
            x = energy_ref[rows_r, pl.ds(pl.multiple_of(g * cells, cells), cells)].astype(F32)
            w1 = w1_ref[pl.ds(g, 1), :]
            fresh, along = [], None
            for k in range(lanes):
                part = x[:, k * 128 : (k + 1) * 128]
                fresh.append(lead[k] + w1 * part)
                term = part * w23[k]
                along = term if along is None else along + term
            along_ref[g, rows_r, :] = along
            return tuple(fresh)

        none = jnp.zeros((tile, 128), F32)
        lead = lax.fori_loop(0, G, over_points, (none,) * lanes, unroll=8)
        for k in range(lanes):
            lead_ref[rows_r, k * 128 : (k + 1) * 128] = lead[k]
        return carry

    lax.fori_loop(0, tiles, over_rows, 0)

    def back(a, hi, lo):
        a_hi, a_lo = halves(a)
        dims = (((1,), (1,)), ((), ()))
        total = lax.dot_general(a_hi, hi, dims, preferred_element_type=F32)
        total = total + lax.dot_general(a_hi, lo, dims, preferred_element_type=F32)
        total = total + lax.dot_general(a_lo, hi, dims, preferred_element_type=F32)
        return jnp.concatenate([total, jnp.zeros((number, 96), F32)], axis=1)

    thin = iota((number, 128), 1)
    v = jnp.zeros((number, 128), F32)
    for g in range(G):
        v = v + jnp.where(thin == g, lane_sum(along_ref[g]), 0.0)
    field_first = dot_exact(v[:, :G], fit_ref[...])
    field_second = back(lead_ref[...] * w3, ways[0], ways[1])
    field_third = back(lead_ref[...] * w2, ways[2], ways[3])
    own = known[:rows]
    lane = iota((rows, 128), 1)
    single = jnp.where(lane < 16, pltpu.roll(own, 112, 1), 0.0)
    along = lane_sum(single * own)
    norms = own[:, 0:1]
    n1, n2, n3 = (norms[p * number : (p + 1) * number] for p in range(3))
    q1, q2, q3 = (along[p * number : (p + 1) * number] for p in range(3))
    scale = jnp.concatenate([n2 * n3, n1 * n3, n1 * n2], axis=0)
    shift = jnp.concatenate([n3 * q2 + n2 * q3, n3 * q1 + n1 * q3, n2 * q1 + n1 * q2], axis=0)
    from_grid = jnp.concatenate([field_first, field_second, field_third], axis=0)
    from_grid = from_grid - scale * single - jnp.where(lane == 0, shift, 0.0)
    fields = jnp.concatenate([from_grid] + shares, axis=0)
    f_hi, f_lo = halves(fields)
    dims = (((0,), (0,)), ((), ()))
    part = lax.dot_general(pick, f_hi, dims, preferred_element_type=F32) + lax.dot_general(
        pick, f_lo, dims, preferred_element_type=F32
    )
    part = part[:peers] + sum(
        pltpu.roll(part[j * peers : (j + 1) * peers], 16 * j, 1) for j in range(1, spots)
    )
    slots = out_ref.shape[0]
    each = float(slots // peers)
    at = iota((slots, 1), 0).astype(F32)
    peer = jnp.floor((at + 0.5) * (1.0 / each))
    rest = at - each * peer
    late = rest >= per
    rank = rest - jnp.where(late, per, 0.0)
    from_peer = one_hot(peer, peers)
    seen = dot(from_peer, asked)
    off = iota((slots, 128), 1).astype(F32) - rank
    local = lane_sum(jnp.where(off == 0.0, seen, 0.0))
    turned = lane_sum(jnp.where(off == 16.0, seen, 0.0))
    terms = pick_two(one_hot(local, 256), hi_ref[...], lo_ref[...])
    terms = jnp.where(turned > 0.5, terms[:, 256:], terms[:, :256])
    terms = jnp.where(late, terms[:, 128:], terms[:, :128])
    p_hi, p_lo = halves(part)
    out_ref[...] = jnp.where(rest == 2.0 * per, pick_two(from_peer, p_hi, p_lo), terms)


def own_kernel(came_ref, out_ref):
    peers = came_ref.shape[0] // 25
    each = 25
    rows = came_ref[pl.ds(each - 1, peers, stride=each), :]
    total = jnp.sum(rows, axis=0, keepdims=True)
    out_ref[...] = jnp.broadcast_to(total, out_ref.shape)


def face_kernel(far_ref, came_ref, known_ref, meta_ref, coef_ref, energy_ref, fit_ref, sems):
    number = fit_ref.shape[1]
    some = 4
    copies = [
        pltpu.make_async_copy(far_ref.at[c : c + some], fit_ref.at[c : c + some], sems.at[c // some])
        for c in range(0, KEEP, some)
    ]
    for copy in copies:
        copy.start()
    place = meta_ref[:, 0:1]
    known = known_ref[...]
    one, two, three = (known[p * number : (p + 1) * number] for p in range(3))
    hi, lo = halves(came_ref[...])
    slots = came_ref.shape[0]
    got = [pick_two(one_hot(place + 12.0 * h, slots), hi, lo) for h in range(2)]
    lane = iota((number, 128), 1)
    k, n = iota((128, 256), 0), iota((128, 256), 1)
    two_wide = dot_two(two, (k == (n >> 4)).astype(F32).astype(BF16))
    two_single = dot_two(two, ((k == (n >> 4) + 16) & ((n & 15) == 0)).astype(F32).astype(BF16))
    three_low = jnp.where((lane & 31) < 16, three, 0.0)
    three_wide = three_low + pltpu.roll(three_low, 16, 1)
    start = lane < 16
    first_pair = [g[:number] for g in got]
    first_pair[0] = first_pair[0] + jnp.where(start, pltpu.roll(one, 112, 1), 0.0)
    second_pair = [g[number : 2 * number] for g in got]
    third_pair = [g[2 * number :] for g in got]
    third_pair[0] = third_pair[0] + jnp.where(start, pltpu.roll(three, 112, 1), 0.0)
    third_pair = [t + two_single[:, h * 128 : (h + 1) * 128] for h, t in enumerate(third_pair)]
    both = [two_wide[:, h * 128 : (h + 1) * 128] * three_wide for h in range(2)]
    spaced = (lane & 15) == 0
    energy = jnp.zeros((number, 128), F32)
    for c in range(KEEP):
        if c % some == 0:
            copies[c // some].wait()
        along = jnp.zeros((number, 128), F32)
        for h in range(2):
            moved = pltpu.roll(first_pair[h], 128 - c, 1) if c else first_pair[h]
            value = fit_ref[c, :, h * 128 : (h + 1) * 128] - jnp.where(spaced, moved, 0.0)
            if h == 0:
                shift = (c % 8) * 16
                moved = second_pair[c // 8]
                moved = pltpu.roll(moved, 128 - shift, 1) if shift else moved
                value = value - jnp.where(start, moved, 0.0)
            if c == 0:
                value = value - third_pair[h]
            coef_ref[:, c * 256 + h * 128 : c * 256 + (h + 1) * 128] = value.astype(BF16)
            along = along + value * both[h]
        energy = energy + one[:, c : c + 1] * along
    energy_ref[...] = lax.dot_general(
        jnp.full((8, 128), 1.0, F32), energy, (((1,), (1,)), ((), ())), preferred_element_type=F32, precision=HIGHEST
    )[0:1]


def integral_kernel(parts_ref, integral_ref, out_ref):
    total = jnp.sum(parts_ref[...], axis=0, keepdims=True)
    shape = (out_ref.shape[0], 128)
    total = jnp.where((iota(shape, 1) >> 4) == iota(shape, 0), total, 0.0)
    out_ref[...] = dot_exact(total, integral_ref[...])


def call(kernel, outs, *args, name, apart=(), fetched=(), outs_apart=False, flops=0, scratch=()):
    moved = sum(int(np.prod(a.shape)) * a.dtype.itemsize for a in args) + sum(
        int(np.prod(o.shape)) * o.dtype.itemsize for o in outs
    )
    count = len(args) + len(outs) + len(scratch)

    def fetching(*refs):
        refs, held, sems = list(refs[:count]), refs[count:-1], refs[-1]
        copies = [
            pltpu.make_async_copy(refs[i], buffer, sems.at[k])
            for k, (i, buffer) in enumerate(zip(fetched, held, strict=True))
        ]
        for copy in copies:
            copy.start()
        for copy in copies:
            copy.wait()
        for i, buffer in zip(fetched, held, strict=True):
            refs[i] = buffer
        kernel(*refs)

    extra = []
    if fetched:
        extra = [pltpu.VMEM(args[i].shape, args[i].dtype) for i in fetched]
        extra.append(pltpu.SemaphoreType.DMA((len(fetched),)))
    outside = set(apart) | set(fetched)
    return pl.pallas_call(
        fetching if fetched else kernel,
        out_shape=outs,
        in_specs=[
            pl.BlockSpec(memory_space=pltpu.HBM if i in outside else pltpu.VMEM) for i in range(len(args))
        ],
        out_specs=[pl.BlockSpec(memory_space=pltpu.HBM if outs_apart else pltpu.VMEM)] * len(outs),
        scratch_shapes=list(scratch) + extra,
        compiler_params=pltpu.CompilerParams(vmem_limit_bytes=VMEM_LIMIT),
        cost_estimate=pl.CostEstimate(flops=flops, bytes_accessed=moved, transcendentals=0),
        name=name,
    )(*(far(a) if i in outside else a for i, a in enumerate(args)))


def far(a):
    return pltpu.with_memory_space_constraint(a, pltpu.HBM)


def shaped(shape, dtype=F32):
    return jax.ShapeDtypeStruct(shape, dtype)


def body(energies, triples, pair_surfaces, pair_slot, single_surfaces, modals, mode_slot):
    devices = lax.axis_size("dev")
    groups = lax.axis_size("grp")
    number = triples.shape[0]
    own = modals.shape[0]
    capacity = 3 * number // devices
    cos_wide = np.zeros((G * S, 128), np.float32)
    fit_wide = np.zeros((G, 128), np.float32)
    cos_block = np.zeros((128, own * G), np.float32)
    for m in range(own):
        cos_wide[::S, m * 32 : m * 32 + KEEP] = COSINES.T
        fit_wide[:, m * 32 + KEEP : m * 32 + 2 * KEEP] = FITTER.T
        cos_block[m * KEEP : (m + 1) * KEEP, m * G : (m + 1) * G] = COSINES
    kron = np.einsum("dh,el->hlde", FITTER, FITTER).reshape(G * G, KEEP * KEEP)
    hi, lo = (jnp.asarray(x) for x in halves_np(kron))
    fit_rows = np.zeros((G, 128), np.float32)
    fit_rows[:, :KEEP] = FITTER.T
    wide = np.zeros((2, 32, G, G))
    wide[0, :KEEP] = FITTER[:, :, None]
    wide[1, :KEEP] = FITTER[:, None, :]
    wide = jnp.asarray(np.stack([h[p] for p in range(2) for h in halves_np(wide.reshape(2, 32, G * G))]))
    send, meta = call(
        ask_kernel,
        [shaped((devices, 2, 128)), shaped((3 * number, 128))],
        triples.T,
        pair_slot,
        mode_slot.reshape(1, -1),
        modals,
        single_surfaces,
        jnp.asarray(cos_wide),
        jnp.asarray(fit_wide),
        fetched=tuple(range(7)),
        name="ask",
    )
    came = lax.all_to_all(send, "dev", 0, 0, tiled=True)
    table = shaped((pair_surfaces.shape[0], 512), BF16)
    table_hi, table_lo, integral = call(
        table_kernel,
        [table, table, shaped((128, S * S))],
        pair_surfaces,
        hi,
        lo,
        modals,
        jnp.asarray(cos_block),
        fetched=(0, 1, 2, 3, 4),
        name="table",
        flops=5 * 10**8,
    )
    each = 2 * capacity + 1
    answer, known = call(
        share_kernel,
        [shaped((devices * each, 128)), shaped((3 * number, 128))],
        came,
        table_hi,
        table_lo,
        energies,
        meta,
        jnp.asarray(fit_rows),
        wide,
        apart=(3, 5, 6),
        name="share",
        flops=10**9,
        scratch=[
            pltpu.VMEM((G, 128), F32),
            pltpu.VMEM((number, G * G), F32),
            pltpu.VMEM((number, G * G), F32),
            pltpu.VMEM((G, number, 128), F32),
            pltpu.VMEM(energies.shape, BF16),
            pltpu.VMEM(fit_rows.shape, F32),
            pltpu.VMEM(wide.shape, BF16),
            pltpu.SemaphoreType.DMA((number // 16,)),
            pltpu.SemaphoreType.DMA((2,)),
        ],
    )
    terms = lax.all_to_all(
        answer.reshape(devices, each, 1, 128), "dev", 0, 0, tiled=True
    ).reshape(devices * each, 128)
    first_hi, first_lo = (jnp.asarray(x) for x in halves_np(np.kron(FITTER, np.eye(8))))
    (fitted,) = call(
        fit_kernel,
        [pltpu.HBM((KEEP, number, KEEP**2), F32)],
        energies,
        hi,
        lo,
        first_hi,
        first_lo,
        apart=(0,),
        outs_apart=True,
        scratch=[
            pltpu.VMEM(energies.shape, BF16),
            pltpu.VMEM((KEEP, number, KEEP**2), F32),
            pltpu.SemaphoreType.DMA((number // 32,)),
            pltpu.SemaphoreType.DMA((number // 32,)),
        ],
        name="fit",
        flops=5 * 10**9,
    )
    (mine,) = call(own_kernel, [shaped((groups, 128))], terms, name="own")
    parts = lax.all_to_all(mine.reshape(groups, 1, 128), "grp", 0, 0, tiled=True)
    coefficients, energy = call(
        face_kernel,
        [shaped((number, KEEP**3), BF16), shaped((1, number))],
        fitted,
        terms,
        known,
        meta,
        apart=(0,),
        scratch=[pltpu.VMEM(fitted.shape, F32), pltpu.SemaphoreType.DMA((4,))],
        name="faces",
        flops=10**9,
    )
    (mean_field,) = call(
        integral_kernel,
        [shaped((own, S * S))],
        parts.reshape(groups, 128),
        integral,
        name="integrals",
    )
    return coefficients, energy.reshape(number), mean_field


def solution(mesh):
    in_specs = (
        P(("grp", "dev"), None),
        P(("grp", "dev"), None),
        P("dev", None),
        P(),
        P("dev", None),
        P("dev", None),
        P(),
    )
    out_specs = (P(("grp", "dev"), None), P(("grp", "dev")), P("dev", None))
    return jax.shard_map(body, mesh=mesh, in_specs=in_specs, out_specs=out_specs, check_vma=False)
```

```python
import numpy as np
import jax
import jax.numpy as jnp
from jax import lax
from jax.experimental import pallas as pl
from jax.experimental.pallas import tpu as pltpu
from jax.sharding import PartitionSpec as P

G = 32
KEEP = 16
S = 16
F32 = jnp.float32
BF16 = jnp.bfloat16
HIGHEST = lax.Precision.HIGHEST
VMEM_LIMIT = 24 * 2**20


def tables():
    orders = np.arange(KEEP, dtype=np.float64)
    points = np.arange(G, dtype=np.float64) + 0.5
    cosines = np.cos(np.pi * orders[:, None] * points[None, :] / G)
    weights = np.where(orders == 0, 1.0, 2.0) / G
    return cosines, weights[:, None] * cosines


COSINES, FITTER = tables()


def halves(a):
    hi = a.astype(BF16)
    return hi, (a - hi.astype(F32)).astype(BF16)


def halves_np(a):
    a = a.astype(np.float32)
    hi = a.astype(jnp.bfloat16)
    return hi, (a - hi.astype(np.float32)).astype(jnp.bfloat16)


def dot(a, b):
    return jnp.dot(a, b, preferred_element_type=F32)


def dot_exact(a, b):
    return jnp.dot(a, b, preferred_element_type=F32, precision=HIGHEST)


def iota(shape, dim):
    return lax.broadcasted_iota(jnp.int32, shape, dim)


def lane_sum(a):
    return jnp.sum(a, axis=1, keepdims=True)


def column(row):
    n = row.shape[1]
    return lane_sum(jnp.where(iota((n, n), 0) == iota((n, n), 1), row, 0.0))


def one_hot(column_f, width):
    return (iota((column_f.shape[0], width), 1).astype(F32) == column_f).astype(F32).astype(BF16)


def dot_two(a, b):
    hi, lo = halves(a)
    return dot(hi, b) + dot(lo, b)


def pick_two(pick, hi, lo):
    return dot(pick, hi) + dot(pick, lo)


def ask_kernel(tri_ref, pair_ref, slot_ref, modal_ref, single_ref, cos_ref, fit_ref, out_ref, meta_ref):
    modes = slot_ref.shape[1]
    tri = tri_ref[...].astype(F32)
    first, second, third = (column(tri[p : p + 1]) for p in range(3))
    lower = jnp.concatenate([first, first, second], axis=0)
    upper = jnp.concatenate([second, third, third], axis=0)
    each = jnp.concatenate([first, second, third], axis=0)
    rows = lower.shape[0]
    number = rows // 3
    lane = iota((rows, modes), 1).astype(F32)
    pair = pair_ref[...]
    high = (pair >> 8).astype(F32).astype(BF16)
    low = (pair & 255).astype(F32).astype(BF16)
    pick = (lane == lower).astype(F32).astype(BF16)
    at = lane == upper
    owner = lane_sum(jnp.where(at, dot(pick, high), 0.0))
    local = lane_sum(jnp.where(at, dot(pick, low), 0.0))
    slots = slot_ref[...]
    slots = ((slots & 3) * 32 + (slots >> 2)).astype(F32)
    slot = lane_sum(jnp.where(lane == each, slots, 0.0))
    wide = iota((rows, 128), 1)
    wide_f = wide.astype(F32)
    hit = wide_f == owner
    hit_b = hit.astype(F32).astype(BF16)
    earlier = (iota((rows, rows), 1) < iota((rows, rows), 0)).astype(F32).astype(BF16)
    rank = lane_sum(jnp.where(hit, dot(earlier, hit_b), 0.0))
    ordered = lower < upper
    is_first = iota((rows, 1), 0) < number
    turned = jnp.where(is_first, ordered.astype(F32), 1.0 - ordered.astype(F32))
    s1, s2, s3 = (slot[p * number : (p + 1) * number] for p in range(3))
    left = jnp.concatenate([s1, s1, s2], axis=0)
    right = jnp.concatenate([s2, s3, s3], axis=0)
    other = jnp.concatenate([s3, s2, s1], axis=0)
    small = jnp.where(ordered, left, right)
    large = jnp.where(ordered, right, left)
    off = wide_f - rank
    said = jnp.where(off == 0.0, local, 0.0)
    for k, value in enumerate((turned, small, large, other)):
        said = said + jnp.where(off == 16.0 * (k + 1), value, 0.0)
    asked = lax.dot_general(hit_b, said.astype(BF16), (((0,), (0,)), ((), ())), preferred_element_type=F32)
    square = modal_ref[...] * modal_ref[...]
    mine = dot_exact(square, cos_ref[...]) + dot_exact(single_ref[...], fit_ref[...])
    four = mine.shape
    mine = jnp.sum(jnp.where((iota(four, 1) >> 5) == iota(four, 0), mine, 0.0), axis=0, keepdims=True)
    peers = out_ref.shape[0]
    out_ref[:, 0, :] = jnp.broadcast_to(mine, (peers, 128))
    out_ref[:, 1, :] = asked[:peers]
    meta_ref[...] = jnp.where(wide == 0, owner * 25.0 + rank, jnp.where(wide == 1, slot, 0.0))


FIT_TILE = 32


def fit_some(energy_ref, hi_ref, lo_ref, first_ref, out_ref, start):
    cells = G * G
    few = 8
    rows = pl.ds(pl.multiple_of(start, FIT_TILE), FIT_TILE)
    stacked = jnp.concatenate([energy_ref[rows, g * cells : (g + 1) * cells] for g in range(G)], axis=0)
    two = dot(stacked, hi_ref[...]) + dot(stacked, lo_ref[...])
    half = first_ref.shape[0] // 2
    for h in range(FIT_TILE // few):
        at = h * few
        part = jnp.concatenate(
            [two[g * FIT_TILE + at : g * FIT_TILE + at + few] for g in range(G)], axis=0
        )
        p_hi, p_lo = halves(part)
        large = dot(first_ref[...], p_hi)
        all_three = large[:half] + large[half:] + dot(first_ref[:half], p_lo)
        some = pl.ds(pl.multiple_of(start + at, few), few)
        for c in range(KEEP):
            out_ref[c, some, :] = all_three[c * few : (c + 1) * few]


def table_kernel(
    pair_ref,
    hi_ref,
    lo_ref,
    modal_ref,
    cosine_ref,
    first_ref,
    source_ref,
    table_hi_ref,
    table_lo_ref,
    integral_ref,
    far_ref,
    energy_ref,
    fit_ref,
    sem,
):
    copy_in = pltpu.make_async_copy(source_ref.at[:FIT_TILE], energy_ref, sem)
    copy_in.start()
    a_hi, a_lo = halves(pair_ref[...])
    k_hi, k_lo = hi_ref[...], lo_ref[...]
    terms = dot(a_hi, k_hi) + dot(a_hi, k_lo) + dot(a_lo, k_hi)
    square = (256, 256)
    i, j = iota(square, 0), iota(square, 1)
    turn = (((i & 15) == (j >> 4)) & ((i >> 4) == (j & 15))).astype(F32).astype(BF16)
    t_hi, t_lo = halves(terms)
    table_hi_ref[:, :256] = t_hi
    table_lo_ref[:, :256] = t_lo
    table_hi_ref[:, 256:] = dot(t_hi, turn).astype(BF16)
    table_lo_ref[:, 256:] = dot(t_lo, turn).astype(BF16)
    copy_in.wait()
    fit_some(energy_ref, hi_ref, lo_ref, first_ref, fit_ref, 0)
    copy_out = pltpu.make_async_copy(fit_ref, far_ref, sem)
    copy_out.start()
    modal = modal_ref[...]
    own = modal.shape[0]
    row = iota((own * G, G * S), 0)
    lane = iota((own * G, G * S), 1)
    spread = jnp.zeros((own * G, G * S), F32)
    for m in range(own):
        spread = jnp.where((row >> 5) == m, modal[m : m + 1, :], spread)
    spread = jnp.where((lane >> 4) == (row & 31), spread, 0.0)
    k, n = iota((G * S, 256), 0), iota((G * S, 256), 1)
    hi, lo = halves(spread)
    to_left = ((k & 15) == (n >> 4)).astype(F32).astype(BF16)
    to_right = ((k & 15) == (n & 15)).astype(F32).astype(BF16)
    left = dot(hi, to_left) + dot(lo, to_left)
    right = dot(hi, to_right) + dot(lo, to_right)
    integral_ref[...] = dot_exact(cosine_ref[...], left * right)
    copy_out.wait()


def fit_kernel(source_ref, hi_ref, lo_ref, first_ref, far_ref, energy_ref, out_ref, sems, out_sems):
    skipped = source_ref.shape[0] - energy_ref.shape[0]
    tiles = energy_ref.shape[0] // FIT_TILE

    def copy(r):
        rows = pl.ds(pl.multiple_of(r * FIT_TILE, FIT_TILE), FIT_TILE)
        there = pl.ds(pl.multiple_of(skipped + r * FIT_TILE, FIT_TILE), FIT_TILE)
        return pltpu.make_async_copy(source_ref.at[there], energy_ref.at[rows], sems.at[r])

    def copy_out(r):
        rows = pl.ds(pl.multiple_of(r * FIT_TILE, FIT_TILE), FIT_TILE)
        return pltpu.make_async_copy(out_ref.at[:, rows], far_ref.at[:, rows], out_sems.at[r])

    for r in range(2):
        copy(r).start()

    def over_rows(r, carry):
        copy(r).wait()

        @pl.when(r + 2 < tiles)
        def _():
            copy(r + 2).start()

        fit_some(energy_ref, hi_ref, lo_ref, first_ref, out_ref, r * FIT_TILE)
        copy_out(r).start()
        return carry

    lax.fori_loop(0, tiles, over_rows, 0)
    for r in range(tiles):
        copy_out(r).wait()


def share_kernel(
    came_ref,
    hi_ref,
    lo_ref,
    source_ref,
    meta_ref,
    fit_in,
    wide_in,
    out_ref,
    known_ref,
    w1_ref,
    w23_ref,
    lead_ref,
    along_ref,
    energy_ref,
    fit_ref,
    wide_ref,
    sems,
    more_sems,
):
    tile = 16
    tables_in = [
        pltpu.make_async_copy(fit_in, fit_ref, more_sems.at[0]),
        pltpu.make_async_copy(wide_in, wide_ref, more_sems.at[1]),
    ]
    for part in tables_in:
        part.start()

    def copy(r):
        rows_r = pl.ds(pl.multiple_of(r * tile, tile), tile)
        return pltpu.make_async_copy(source_ref.at[rows_r], energy_ref.at[rows_r], sems.at[r])

    tiles, ahead = energy_ref.shape[0] // tile, 4
    for r in range(ahead):
        copy(r).start()
    peers = came_ref.shape[0]
    number = energy_ref.shape[0]
    rows = 3 * number
    asked = came_ref[:, 1, :].astype(BF16)
    per = float(rows // peers)
    at = iota((rows, 1), 0).astype(F32)
    peer = jnp.floor((at + 0.5) * (1.0 / per))
    rank = at - per * peer
    seen = dot(one_hot(peer, peers), asked)
    off = iota((rows, 128), 1).astype(F32) - rank
    local, small, large, other = (
        lane_sum(jnp.where(off == 16.0 * k, seen, 0.0)) for k in (0, 2, 3, 4)
    )
    slot = jnp.concatenate([meta_ref[:, 1:2], small, large, other], axis=0)
    pick = one_hot(slot, 128)
    ground = came_ref[:, 0, :]
    spots = 128 // peers
    ground = jnp.concatenate([pltpu.roll(ground, 128 - 32 * j, 1) if j else ground for j in range(spots)], axis=0)
    ground = jnp.where(iota((128, 128), 1) < 32, ground, 0.0)
    ground = ground + pltpu.roll(ground, 32, 1)
    ground = ground + pltpu.roll(ground, 64, 1)
    known = pick_two(pick, *halves(ground))
    known_ref[...] = known[:rows]
    k, n = iota((128, 256), 0), iota((128, 256), 1)
    widen = (k == (n >> 4)).astype(F32).astype(BF16)
    k, n = iota((256, 128), 0), iota((256, 128), 1)
    to_high = ((k >> 4) == n).astype(F32).astype(BF16)
    to_low = ((k & 15) == n).astype(F32).astype(BF16)

    def repeated(a):
        part = jnp.where((iota(a.shape, 1) & 31) < 16, a, 0.0)
        return part + pltpu.roll(part, 16, 1)

    def twice(a):
        return jnp.concatenate([a, a], axis=1)

    terms = pick_two(one_hot(local, 256), hi_ref[:, :256], lo_ref[:, :256])
    g_small, g_large, g_other = (known[p * rows : (p + 1) * rows] for p in (1, 2, 3))
    of_small = dot_two(terms * twice(repeated(g_large)), to_high)
    of_large = dot_two(terms * dot_two(g_small, widen), to_low)
    norm = g_other[:, 0:1]
    of_other = lane_sum(of_small * g_small)
    lane = iota((rows, 128), 1)
    shares = [-norm * of_small, -norm * of_large, jnp.where(lane == 0, -of_other, 0.0)]
    one, two, three = (known[p * number : (p + 1) * number] for p in range(3))
    cells = G * G
    for part in tables_in:
        part.wait()
    w1_ref[...] = jnp.broadcast_to(lane_sum(fit_ref[...] * one[0:1]), w1_ref.shape)
    ways = [wide_ref[p] for p in range(4)]

    def weights(a, hi, lo):
        a_hi, a_lo = halves(a[:, :32])
        return dot(a_hi, hi) + dot(a_hi, lo) + dot(a_lo, hi)

    w2 = weights(two, ways[0], ways[1])
    w3 = weights(three, ways[2], ways[3])
    w23_ref[...] = w2 * w3
    lanes = cells // 128

    def over_rows(r, carry):
        copy(r).wait()

        @pl.when(r + ahead < tiles)
        def _():
            copy(r + ahead).start()

        rows_r = pl.ds(pl.multiple_of(r * tile, tile), tile)
        w23 = [w23_ref[rows_r, k * 128 : (k + 1) * 128] for k in range(lanes)]

        def over_points(g, lead):
            x = energy_ref[rows_r, pl.ds(pl.multiple_of(g * cells, cells), cells)].astype(F32)
            w1 = w1_ref[pl.ds(g, 1), :]
            fresh, along = [], None
            for k in range(lanes):
                part = x[:, k * 128 : (k + 1) * 128]
                fresh.append(lead[k] + w1 * part)
                term = part * w23[k]
                along = term if along is None else along + term
            along_ref[g] += along
            return tuple(fresh)

        none = jnp.zeros((tile, 128), F32)
        lead = lax.fori_loop(0, G, over_points, (none,) * lanes, unroll=8)
        for k in range(lanes):
            lead_ref[rows_r, k * 128 : (k + 1) * 128] = lead[k]
        return carry

    along_ref[...] = jnp.zeros_like(along_ref)
    lax.fori_loop(0, tiles, over_rows, 0)

    def back(a, hi, lo):
        a_hi, a_lo = halves(a)
        dims = (((1,), (1,)), ((), ()))
        total = lax.dot_general(a_hi, hi, dims, preferred_element_type=F32)
        total = total + lax.dot_general(a_hi, lo, dims, preferred_element_type=F32)
        total = total + lax.dot_general(a_lo, hi, dims, preferred_element_type=F32)
        return jnp.concatenate([total, jnp.zeros((number, 96), F32)], axis=1)

    sums = lane_sum(jnp.sum(along_ref[...], axis=1))
    field_first = jnp.sum(sums * fit_ref[...], axis=0, keepdims=True)
    field_first = jnp.where(iota((number, 128), 0) == 0, field_first, 0.0)
    field_second = back(lead_ref[...] * w3, ways[0], ways[1])
    field_third = back(lead_ref[...] * w2, ways[2], ways[3])
    own = known[:rows]
    lane = iota((rows, 128), 1)
    single = jnp.where(lane < 16, pltpu.roll(own, 112, 1), 0.0)
    along = lane_sum(single * own)
    norms = own[:, 0:1]
    n1, n2, n3 = (norms[p * number : (p + 1) * number] for p in range(3))
    q1, q2, q3 = (along[p * number : (p + 1) * number] for p in range(3))
    scale = jnp.concatenate([n2 * n3, n1 * n3, n1 * n2], axis=0)
    shift = jnp.concatenate([n3 * q2 + n2 * q3, n3 * q1 + n1 * q3, n2 * q1 + n1 * q2], axis=0)
    from_grid = jnp.concatenate([field_first, field_second, field_third], axis=0)
    from_grid = from_grid - scale * single - jnp.where(lane == 0, shift, 0.0)
    fields = jnp.concatenate([from_grid] + shares, axis=0)
    f_hi, f_lo = halves(fields)
    dims = (((0,), (0,)), ((), ()))
    part = lax.dot_general(pick, f_hi, dims, preferred_element_type=F32) + lax.dot_general(
        pick, f_lo, dims, preferred_element_type=F32
    )
    part = part[:peers] + sum(
        pltpu.roll(part[j * peers : (j + 1) * peers], 16 * j, 1) for j in range(1, spots)
    )
    slots = out_ref.shape[0]
    each = float(slots // peers)
    at = iota((slots, 1), 0).astype(F32)
    peer = jnp.floor((at + 0.5) * (1.0 / each))
    rest = at - each * peer
    late = rest >= per
    rank = rest - jnp.where(late, per, 0.0)
    from_peer = one_hot(peer, peers)
    seen = dot(from_peer, asked)
    off = iota((slots, 128), 1).astype(F32) - rank
    local = lane_sum(jnp.where(off == 0.0, seen, 0.0))
    turned = lane_sum(jnp.where(off == 16.0, seen, 0.0))
    terms = pick_two(one_hot(local, 256), hi_ref[...], lo_ref[...])
    terms = jnp.where(turned > 0.5, terms[:, 256:], terms[:, :256])
    terms = jnp.where(late, terms[:, 128:], terms[:, :128])
    p_hi, p_lo = halves(part)
    out_ref[...] = jnp.where(rest == 2.0 * per, pick_two(from_peer, p_hi, p_lo), terms)


def own_kernel(came_ref, out_ref):
    peers = came_ref.shape[0] // 25
    each = 25
    rows = came_ref[pl.ds(each - 1, peers, stride=each), :]
    total = jnp.sum(rows, axis=0, keepdims=True)
    out_ref[...] = jnp.broadcast_to(total, out_ref.shape)


def face_kernel(near_in, far_in, came_ref, known_ref, meta_ref, coef_ref, energy_ref, fit_ref, sems):
    number = fit_ref.shape[1]
    some = 4
    split = near_in.shape[1]
    copies = []
    for k in range(KEEP // some):
        these = slice(k * some, (k + 1) * some)
        copies.append(
            (
                pltpu.make_async_copy(near_in.at[these], fit_ref.at[these, :split], sems.at[k, 0]),
                pltpu.make_async_copy(far_in.at[these], fit_ref.at[these, split:], sems.at[k, 1]),
            )
        )
    for pair in copies:
        for copy in pair:
            copy.start()
    place = meta_ref[:, 0:1]
    known = known_ref[...]
    one, two, three = (known[p * number : (p + 1) * number] for p in range(3))
    hi, lo = halves(came_ref[...])
    slots = came_ref.shape[0]
    got = [pick_two(one_hot(place + 12.0 * h, slots), hi, lo) for h in range(2)]
    lane = iota((number, 128), 1)
    k, n = iota((128, 256), 0), iota((128, 256), 1)
    two_wide = dot_two(two, (k == (n >> 4)).astype(F32).astype(BF16))
    two_single = dot_two(two, ((k == (n >> 4) + 16) & ((n & 15) == 0)).astype(F32).astype(BF16))
    three_low = jnp.where((lane & 31) < 16, three, 0.0)
    three_wide = three_low + pltpu.roll(three_low, 16, 1)
    start = lane < 16
    first_pair = [g[:number] for g in got]
    first_pair[0] = first_pair[0] + jnp.where(start, pltpu.roll(one, 112, 1), 0.0)
    second_pair = [g[number : 2 * number] for g in got]
    third_pair = [g[2 * number :] for g in got]
    third_pair[0] = third_pair[0] + jnp.where(start, pltpu.roll(three, 112, 1), 0.0)
    third_pair = [t + two_single[:, h * 128 : (h + 1) * 128] for h, t in enumerate(third_pair)]
    both = [two_wide[:, h * 128 : (h + 1) * 128] * three_wide for h in range(2)]
    spaced = (lane & 15) == 0
    energy = jnp.zeros((number, 128), F32)
    for c in range(KEEP):
        if c % some == 0:
            for copy in copies[c // some]:
                copy.wait()
        along = jnp.zeros((number, 128), F32)
        for h in range(2):
            moved = pltpu.roll(first_pair[h], 128 - c, 1) if c else first_pair[h]
            value = fit_ref[c, :, h * 128 : (h + 1) * 128] - jnp.where(spaced, moved, 0.0)
            if h == 0:
                shift = (c % 8) * 16
                moved = second_pair[c // 8]
                moved = pltpu.roll(moved, 128 - shift, 1) if shift else moved
                value = value - jnp.where(start, moved, 0.0)
            if c == 0:
                value = value - third_pair[h]
            coef_ref[:, c * 256 + h * 128 : c * 256 + (h + 1) * 128] = value.astype(BF16)
            along = along + value * both[h]
        energy = energy + one[:, c : c + 1] * along
    energy_ref[...] = lax.dot_general(
        jnp.full((8, 128), 1.0, F32), energy, (((1,), (1,)), ((), ())), preferred_element_type=F32, precision=HIGHEST
    )[0:1]


def integral_kernel(parts_ref, integral_ref, out_ref):
    total = jnp.sum(parts_ref[...], axis=0, keepdims=True)
    shape = (out_ref.shape[0], 128)
    total = jnp.where((iota(shape, 1) >> 4) == iota(shape, 0), total, 0.0)
    out_ref[...] = dot_exact(total, integral_ref[...])


def call(kernel, outs, *args, name, apart=(), fetched=(), outs_apart=(), flops=0, scratch=()):
    moved = sum(int(np.prod(a.shape)) * a.dtype.itemsize for a in args) + sum(
        int(np.prod(o.shape)) * o.dtype.itemsize for o in outs
    )
    count = len(args) + len(outs) + len(scratch)

    def fetching(*refs):
        refs, held, sems = list(refs[:count]), refs[count:-1], refs[-1]
        copies = [
            pltpu.make_async_copy(refs[i], buffer, sems.at[k])
            for k, (i, buffer) in enumerate(zip(fetched, held, strict=True))
        ]
        for copy in copies:
            copy.start()
        for copy in copies:
            copy.wait()
        for i, buffer in zip(fetched, held, strict=True):
            refs[i] = buffer
        kernel(*refs)

    extra = []
    if fetched:
        extra = [pltpu.VMEM(args[i].shape, args[i].dtype) for i in fetched]
        extra.append(pltpu.SemaphoreType.DMA((len(fetched),)))
    outside = set(apart) | set(fetched)
    return pl.pallas_call(
        fetching if fetched else kernel,
        out_shape=outs,
        in_specs=[
            pl.BlockSpec(memory_space=pltpu.HBM if i in outside else pltpu.VMEM) for i in range(len(args))
        ],
        out_specs=[
            pl.BlockSpec(memory_space=pltpu.HBM if i in outs_apart else pltpu.VMEM) for i in range(len(outs))
        ],
        scratch_shapes=list(scratch) + extra,
        compiler_params=pltpu.CompilerParams(vmem_limit_bytes=VMEM_LIMIT),
        cost_estimate=pl.CostEstimate(flops=flops, bytes_accessed=moved, transcendentals=0),
        name=name,
    )(*(far(a) if i in outside else a for i, a in enumerate(args)))


def far(a):
    return pltpu.with_memory_space_constraint(a, pltpu.HBM)


def shaped(shape, dtype=F32):
    return jax.ShapeDtypeStruct(shape, dtype)


def body(energies, triples, pair_surfaces, pair_slot, single_surfaces, modals, mode_slot):
    devices = lax.axis_size("dev")
    groups = lax.axis_size("grp")
    number = triples.shape[0]
    own = modals.shape[0]
    capacity = 3 * number // devices
    cos_wide = np.zeros((G * S, 128), np.float32)
    fit_wide = np.zeros((G, 128), np.float32)
    cos_block = np.zeros((128, own * G), np.float32)
    for m in range(own):
        cos_wide[::S, m * 32 : m * 32 + KEEP] = COSINES.T
        fit_wide[:, m * 32 + KEEP : m * 32 + 2 * KEEP] = FITTER.T
        cos_block[m * KEEP : (m + 1) * KEEP, m * G : (m + 1) * G] = COSINES
    kron = np.einsum("dh,el->hlde", FITTER, FITTER).reshape(G * G, KEEP * KEEP)
    hi, lo = (jnp.asarray(x) for x in halves_np(kron))
    fit_rows = np.zeros((G, 128), np.float32)
    fit_rows[:, :KEEP] = FITTER.T
    wide = np.zeros((2, 32, G, G))
    wide[0, :KEEP] = FITTER[:, :, None]
    wide[1, :KEEP] = FITTER[:, None, :]
    wide = jnp.asarray(np.stack([h[p] for p in range(2) for h in halves_np(wide.reshape(2, 32, G * G))]))
    send, meta = call(
        ask_kernel,
        [shaped((devices, 2, 128)), shaped((3 * number, 128))],
        triples.T,
        pair_slot,
        mode_slot.reshape(1, -1),
        modals,
        single_surfaces,
        jnp.asarray(cos_wide),
        jnp.asarray(fit_wide),
        fetched=tuple(range(7)),
        name="ask",
    )
    came = lax.all_to_all(send, "dev", 0, 0, tiled=True)
    table = shaped((pair_surfaces.shape[0], 512), BF16)
    first_hi, first_lo = halves_np(np.kron(FITTER, np.eye(8)))
    first = jnp.asarray(np.concatenate([first_hi, first_lo], axis=0))
    table_hi, table_lo, integral, fitted_first = call(
        table_kernel,
        [table, table, shaped((128, S * S)), pltpu.HBM((KEEP, FIT_TILE, KEEP**2), F32)],
        pair_surfaces,
        hi,
        lo,
        modals,
        jnp.asarray(cos_block),
        first,
        energies,
        fetched=(0, 1, 2, 3, 4, 5),
        apart=(6,),
        outs_apart=(3,),
        scratch=[
            pltpu.VMEM((FIT_TILE, G**3), BF16),
            pltpu.VMEM((KEEP, FIT_TILE, KEEP**2), F32),
            pltpu.SemaphoreType.DMA,
        ],
        name="table",
        flops=5 * 10**8,
    )
    each = 2 * capacity + 1
    answer, known = call(
        share_kernel,
        [shaped((devices * each, 128)), shaped((3 * number, 128))],
        came,
        table_hi,
        table_lo,
        energies,
        meta,
        jnp.asarray(fit_rows),
        wide,
        apart=(3, 5, 6),
        name="share",
        flops=10**9,
        scratch=[
            pltpu.VMEM((G, 128), F32),
            pltpu.VMEM((number, G * G), F32),
            pltpu.VMEM((number, G * G), F32),
            pltpu.VMEM((G, 16, 128), F32),
            pltpu.VMEM(energies.shape, BF16),
            pltpu.VMEM(fit_rows.shape, F32),
            pltpu.VMEM(wide.shape, BF16),
            pltpu.SemaphoreType.DMA((number // 16,)),
            pltpu.SemaphoreType.DMA((2,)),
        ],
    )
    terms = lax.all_to_all(
        answer.reshape(devices, each, 1, 128), "dev", 0, 0, tiled=True
    ).reshape(devices * each, 128)
    others = number - FIT_TILE
    (fitted_others,) = call(
        fit_kernel,
        [pltpu.HBM((KEEP, others, KEEP**2), F32)],
        energies,
        hi,
        lo,
        first,
        apart=(0,),
        outs_apart=(0,),
        scratch=[
            pltpu.VMEM((others, G**3), BF16),
            pltpu.VMEM((KEEP, others, KEEP**2), F32),
            pltpu.SemaphoreType.DMA((others // FIT_TILE,)),
            pltpu.SemaphoreType.DMA((others // FIT_TILE,)),
        ],
        name="fit",
        flops=5 * 10**9,
    )
    (mine,) = call(own_kernel, [shaped((groups, 128))], terms, name="own")
    parts = lax.all_to_all(mine.reshape(groups, 1, 128), "grp", 0, 0, tiled=True)
    coefficients, energy = call(
        face_kernel,
        [shaped((number, KEEP**3), BF16), shaped((1, number))],
        fitted_first,
        fitted_others,
        terms,
        known,
        meta,
        apart=(0, 1),
        scratch=[pltpu.VMEM((KEEP, number, KEEP**2), F32), pltpu.SemaphoreType.DMA((4, 2))],
        name="faces",
        flops=10**9,
    )
    (mean_field,) = call(
        integral_kernel,
        [shaped((own, S * S))],
        parts.reshape(groups, 128),
        integral,
        name="integrals",
    )
    return coefficients, energy.reshape(number), mean_field


def solution(mesh):
    in_specs = (
        P(("grp", "dev"), None),
        P(("grp", "dev"), None),
        P("dev", None),
        P(),
        P("dev", None),
        P("dev", None),
        P(),
    )
    out_specs = (P(("grp", "dev"), None), P(("grp", "dev")), P("dev", None))
    return jax.shard_map(body, mesh=mesh, in_specs=in_specs, out_specs=out_specs, check_vma=False)
```

```python
import numpy as np
import jax
import jax.numpy as jnp
from jax import lax
from jax.experimental import pallas as pl
from jax.experimental.pallas import tpu as pltpu
from jax.sharding import PartitionSpec as P

G = 32
KEEP = 16
S = 16
F32 = jnp.float32
BF16 = jnp.bfloat16
HIGHEST = lax.Precision.HIGHEST
VMEM_LIMIT = 24 * 2**20


def tables():
    orders = np.arange(KEEP, dtype=np.float64)
    points = np.arange(G, dtype=np.float64) + 0.5
    cosines = np.cos(np.pi * orders[:, None] * points[None, :] / G)
    weights = np.where(orders == 0, 1.0, 2.0) / G
    return cosines, weights[:, None] * cosines


COSINES, FITTER = tables()


def halves(a):
    hi = a.astype(BF16)
    return hi, (a - hi.astype(F32)).astype(BF16)


def halves_np(a):
    a = a.astype(np.float32)
    hi = a.astype(jnp.bfloat16)
    return hi, (a - hi.astype(np.float32)).astype(jnp.bfloat16)


def dot(a, b):
    return jnp.dot(a, b, preferred_element_type=F32)


def dot_exact(a, b):
    return jnp.dot(a, b, preferred_element_type=F32, precision=HIGHEST)


def iota(shape, dim):
    return lax.broadcasted_iota(jnp.int32, shape, dim)


def lane_sum(a):
    return jnp.sum(a, axis=1, keepdims=True)


def column(row):
    n = row.shape[1]
    return lane_sum(jnp.where(iota((n, n), 0) == iota((n, n), 1), row, 0.0))


def one_hot(column_f, width):
    return (iota((column_f.shape[0], width), 1).astype(F32) == column_f).astype(F32).astype(BF16)


def dot_two(a, b):
    hi, lo = halves(a)
    return dot(hi, b) + dot(lo, b)


def pick_two(pick, hi, lo):
    return dot(pick, hi) + dot(pick, lo)


def ask_kernel(tri_ref, pair_ref, slot_ref, modal_ref, single_ref, cos_ref, fit_ref, out_ref, meta_ref):
    modes = slot_ref.shape[1]
    tri = tri_ref[...].astype(F32)
    first, second, third = (column(tri[p : p + 1]) for p in range(3))
    lower = jnp.concatenate([first, first, second], axis=0)
    upper = jnp.concatenate([second, third, third], axis=0)
    each = jnp.concatenate([first, second, third], axis=0)
    rows = lower.shape[0]
    number = rows // 3
    lane = iota((rows, modes), 1).astype(F32)
    pair = pair_ref[...]
    high = (pair >> 8).astype(F32).astype(BF16)
    low = (pair & 255).astype(F32).astype(BF16)
    pick = (lane == lower).astype(F32).astype(BF16)
    at = lane == upper
    owner = lane_sum(jnp.where(at, dot(pick, high), 0.0))
    local = lane_sum(jnp.where(at, dot(pick, low), 0.0))
    slots = slot_ref[...]
    slots = ((slots & 3) * 32 + (slots >> 2)).astype(F32)
    slot = lane_sum(jnp.where(lane == each, slots, 0.0))
    wide = iota((rows, 128), 1)
    wide_f = wide.astype(F32)
    hit = wide_f == owner
    hit_b = hit.astype(F32).astype(BF16)
    earlier = (iota((rows, rows), 1) < iota((rows, rows), 0)).astype(F32).astype(BF16)
    rank = lane_sum(jnp.where(hit, dot(earlier, hit_b), 0.0))
    ordered = lower < upper
    is_first = iota((rows, 1), 0) < number
    turned = jnp.where(is_first, ordered.astype(F32), 1.0 - ordered.astype(F32))
    s1, s2, s3 = (slot[p * number : (p + 1) * number] for p in range(3))
    left = jnp.concatenate([s1, s1, s2], axis=0)
    right = jnp.concatenate([s2, s3, s3], axis=0)
    other = jnp.concatenate([s3, s2, s1], axis=0)
    small = jnp.where(ordered, left, right)
    large = jnp.where(ordered, right, left)
    off = wide_f - rank
    said = jnp.where(off == 0.0, local, 0.0)
    for k, value in enumerate((turned, small, large, other)):
        said = said + jnp.where(off == 16.0 * (k + 1), value, 0.0)
    asked = lax.dot_general(hit_b, said.astype(BF16), (((0,), (0,)), ((), ())), preferred_element_type=F32)
    square = modal_ref[...] * modal_ref[...]
    mine = dot_exact(square, cos_ref[...]) + dot_exact(single_ref[...], fit_ref[...])
    four = mine.shape
    mine = jnp.sum(jnp.where((iota(four, 1) >> 5) == iota(four, 0), mine, 0.0), axis=0, keepdims=True)
    peers = out_ref.shape[0]
    out_ref[:, 0, :] = jnp.broadcast_to(mine, (peers, 128))
    out_ref[:, 1, :] = asked[:peers]
    meta_ref[...] = jnp.where(wide == 0, owner * 25.0 + rank, jnp.where(wide == 1, slot, 0.0))


FIT_TILE = 32


def fit_some(energy_ref, hi_ref, lo_ref, first_ref, out_ref, start):
    cells = G * G
    few = 8
    rows = pl.ds(pl.multiple_of(start, FIT_TILE), FIT_TILE)
    stacked = jnp.concatenate([energy_ref[rows, g * cells : (g + 1) * cells] for g in range(G)], axis=0)
    two = dot(stacked, hi_ref[...]) + dot(stacked, lo_ref[...])
    half = first_ref.shape[0] // 2
    for h in range(FIT_TILE // few):
        at = h * few
        part = jnp.concatenate(
            [two[g * FIT_TILE + at : g * FIT_TILE + at + few] for g in range(G)], axis=0
        )
        p_hi, p_lo = halves(part)
        large = dot(first_ref[...], p_hi)
        all_three = large[:half] + large[half:] + dot(first_ref[:half], p_lo)
        some = pl.ds(pl.multiple_of(start + at, few), few)
        for c in range(KEEP):
            out_ref[c, some, :] = all_three[c * few : (c + 1) * few]


def table_kernel(
    pair_ref,
    hi_ref,
    lo_ref,
    modal_ref,
    cosine_ref,
    table_hi_ref,
    table_lo_ref,
    integral_ref,
):
    a_hi, a_lo = halves(pair_ref[...])
    k_hi, k_lo = hi_ref[...], lo_ref[...]
    terms = dot(a_hi, k_hi) + dot(a_hi, k_lo) + dot(a_lo, k_hi)
    square = (256, 256)
    i, j = iota(square, 0), iota(square, 1)
    turn = (((i & 15) == (j >> 4)) & ((i >> 4) == (j & 15))).astype(F32).astype(BF16)
    t_hi, t_lo = halves(terms)
    table_hi_ref[:, :256] = t_hi
    table_lo_ref[:, :256] = t_lo
    table_hi_ref[:, 256:] = dot(t_hi, turn).astype(BF16)
    table_lo_ref[:, 256:] = dot(t_lo, turn).astype(BF16)
    modal = modal_ref[...]
    own = modal.shape[0]
    row = iota((own * G, G * S), 0)
    lane = iota((own * G, G * S), 1)
    spread = jnp.zeros((own * G, G * S), F32)
    for m in range(own):
        spread = jnp.where((row >> 5) == m, modal[m : m + 1, :], spread)
    spread = jnp.where((lane >> 4) == (row & 31), spread, 0.0)
    k, n = iota((G * S, 256), 0), iota((G * S, 256), 1)
    hi, lo = halves(spread)
    to_left = ((k & 15) == (n >> 4)).astype(F32).astype(BF16)
    to_right = ((k & 15) == (n & 15)).astype(F32).astype(BF16)
    left = dot(hi, to_left) + dot(lo, to_left)
    right = dot(hi, to_right) + dot(lo, to_right)
    integral_ref[...] = dot_exact(cosine_ref[...], left * right)


def fit_kernel(source_ref, hi_ref, lo_ref, first_ref, far_ref, energy_ref, out_ref, sems, out_sems):
    tiles = energy_ref.shape[0] // FIT_TILE

    def copy(r):
        rows = pl.ds(pl.multiple_of(r * FIT_TILE, FIT_TILE), FIT_TILE)
        return pltpu.make_async_copy(source_ref.at[rows], energy_ref.at[rows], sems.at[r])

    def copy_out(r):
        rows = pl.ds(pl.multiple_of(r * FIT_TILE, FIT_TILE), FIT_TILE)
        return pltpu.make_async_copy(out_ref.at[:, rows], far_ref.at[:, rows], out_sems.at[r])

    for r in range(2):
        copy(r).start()

    def over_rows(r, carry):
        copy(r).wait()

        @pl.when(r + 2 < tiles)
        def _():
            copy(r + 2).start()

        fit_some(energy_ref, hi_ref, lo_ref, first_ref, out_ref, r * FIT_TILE)
        copy_out(r).start()
        return carry

    lax.fori_loop(0, tiles, over_rows, 0)
    for r in range(tiles):
        copy_out(r).wait()


def share_kernel(
    came_ref,
    hi_ref,
    lo_ref,
    source_ref,
    meta_ref,
    fit_in,
    wide_in,
    out_ref,
    known_ref,
    w1_ref,
    w23_ref,
    lead_ref,
    along_ref,
    energy_ref,
    fit_ref,
    wide_ref,
    sems,
    more_sems,
):
    tile = 16
    tables_in = [
        pltpu.make_async_copy(fit_in, fit_ref, more_sems.at[0]),
        pltpu.make_async_copy(wide_in, wide_ref, more_sems.at[1]),
    ]
    for part in tables_in:
        part.start()

    def copy(r):
        rows_r = pl.ds(pl.multiple_of(r * tile, tile), tile)
        return pltpu.make_async_copy(source_ref.at[rows_r], energy_ref.at[rows_r], sems.at[r])

    tiles, ahead = energy_ref.shape[0] // tile, 4
    for r in range(ahead):
        copy(r).start()
    peers = came_ref.shape[0]
    number = energy_ref.shape[0]
    rows = 3 * number
    asked = came_ref[:, 1, :].astype(BF16)
    per = float(rows // peers)
    at = iota((rows, 1), 0).astype(F32)
    peer = jnp.floor((at + 0.5) * (1.0 / per))
    rank = at - per * peer
    seen = dot(one_hot(peer, peers), asked)
    off = iota((rows, 128), 1).astype(F32) - rank
    local, small, large, other = (
        lane_sum(jnp.where(off == 16.0 * k, seen, 0.0)) for k in (0, 2, 3, 4)
    )
    slot = jnp.concatenate([meta_ref[:, 1:2], small, large, other], axis=0)
    pick = one_hot(slot, 128)
    ground = came_ref[:, 0, :]
    spots = 128 // peers
    ground = jnp.concatenate([pltpu.roll(ground, 128 - 32 * j, 1) if j else ground for j in range(spots)], axis=0)
    ground = jnp.where(iota((128, 128), 1) < 32, ground, 0.0)
    ground = ground + pltpu.roll(ground, 32, 1)
    ground = ground + pltpu.roll(ground, 64, 1)
    known = pick_two(pick, *halves(ground))
    known_ref[...] = known[:rows]
    k, n = iota((128, 256), 0), iota((128, 256), 1)
    widen = (k == (n >> 4)).astype(F32).astype(BF16)
    k, n = iota((256, 128), 0), iota((256, 128), 1)
    to_high = ((k >> 4) == n).astype(F32).astype(BF16)
    to_low = ((k & 15) == n).astype(F32).astype(BF16)

    def repeated(a):
        part = jnp.where((iota(a.shape, 1) & 31) < 16, a, 0.0)
        return part + pltpu.roll(part, 16, 1)

    def twice(a):
        return jnp.concatenate([a, a], axis=1)

    terms = pick_two(one_hot(local, 256), hi_ref[:, :256], lo_ref[:, :256])
    g_small, g_large, g_other = (known[p * rows : (p + 1) * rows] for p in (1, 2, 3))
    of_small = dot_two(terms * twice(repeated(g_large)), to_high)
    of_large = dot_two(terms * dot_two(g_small, widen), to_low)
    norm = g_other[:, 0:1]
    of_other = lane_sum(of_small * g_small)
    lane = iota((rows, 128), 1)
    shares = [-norm * of_small, -norm * of_large, jnp.where(lane == 0, -of_other, 0.0)]
    one, two, three = (known[p * number : (p + 1) * number] for p in range(3))
    cells = G * G
    for part in tables_in:
        part.wait()
    w1_ref[...] = jnp.broadcast_to(lane_sum(fit_ref[...] * one[0:1]), w1_ref.shape)
    ways = [wide_ref[p] for p in range(4)]

    def weights(a, hi, lo):
        a_hi, a_lo = halves(a[:, :32])
        return dot(a_hi, hi) + dot(a_hi, lo) + dot(a_lo, hi)

    w2 = weights(two, ways[0], ways[1])
    w3 = weights(three, ways[2], ways[3])
    w23_ref[...] = w2 * w3
    lanes = cells // 128

    def over_rows(r, carry):
        copy(r).wait()

        @pl.when(r + ahead < tiles)
        def _():
            copy(r + ahead).start()

        rows_r = pl.ds(pl.multiple_of(r * tile, tile), tile)
        w23 = [w23_ref[rows_r, k * 128 : (k + 1) * 128] for k in range(lanes)]

        def over_points(g, lead):
            x = energy_ref[rows_r, pl.ds(pl.multiple_of(g * cells, cells), cells)].astype(F32)
            w1 = w1_ref[pl.ds(g, 1), :]
            fresh, along = [], None
            for k in range(lanes):
                part = x[:, k * 128 : (k + 1) * 128]
                fresh.append(lead[k] + w1 * part)
                term = part * w23[k]
                along = term if along is None else along + term
            along_ref[g] += along
            return tuple(fresh)

        none = jnp.zeros((tile, 128), F32)
        lead = lax.fori_loop(0, G, over_points, (none,) * lanes, unroll=8)
        for k in range(lanes):
            lead_ref[rows_r, k * 128 : (k + 1) * 128] = lead[k]
        return carry

    along_ref[...] = jnp.zeros_like(along_ref)
    lax.fori_loop(0, tiles, over_rows, 0)

    def back(a, hi, lo):
        a_hi, a_lo = halves(a)
        dims = (((1,), (1,)), ((), ()))
        total = lax.dot_general(a_hi, hi, dims, preferred_element_type=F32)
        total = total + lax.dot_general(a_hi, lo, dims, preferred_element_type=F32)
        total = total + lax.dot_general(a_lo, hi, dims, preferred_element_type=F32)
        return jnp.concatenate([total, jnp.zeros((number, 96), F32)], axis=1)

    sums = lane_sum(jnp.sum(along_ref[...], axis=1))
    field_first = jnp.sum(sums * fit_ref[...], axis=0, keepdims=True)
    field_first = jnp.where(iota((number, 128), 0) == 0, field_first, 0.0)
    field_second = back(lead_ref[...] * w3, ways[0], ways[1])
    field_third = back(lead_ref[...] * w2, ways[2], ways[3])
    own = known[:rows]
    lane = iota((rows, 128), 1)
    single = jnp.where(lane < 16, pltpu.roll(own, 112, 1), 0.0)
    along = lane_sum(single * own)
    norms = own[:, 0:1]
    n1, n2, n3 = (norms[p * number : (p + 1) * number] for p in range(3))
    q1, q2, q3 = (along[p * number : (p + 1) * number] for p in range(3))
    scale = jnp.concatenate([n2 * n3, n1 * n3, n1 * n2], axis=0)
    shift = jnp.concatenate([n3 * q2 + n2 * q3, n3 * q1 + n1 * q3, n2 * q1 + n1 * q2], axis=0)
    from_grid = jnp.concatenate([field_first, field_second, field_third], axis=0)
    from_grid = from_grid - scale * single - jnp.where(lane == 0, shift, 0.0)
    fields = jnp.concatenate([from_grid] + shares, axis=0)
    f_hi, f_lo = halves(fields)
    dims = (((0,), (0,)), ((), ()))
    part = lax.dot_general(pick, f_hi, dims, preferred_element_type=F32) + lax.dot_general(
        pick, f_lo, dims, preferred_element_type=F32
    )
    part = part[:peers] + sum(
        pltpu.roll(part[j * peers : (j + 1) * peers], 16 * j, 1) for j in range(1, spots)
    )
    slots = out_ref.shape[0]
    each = float(slots // peers)
    at = iota((slots, 1), 0).astype(F32)
    peer = jnp.floor((at + 0.5) * (1.0 / each))
    rest = at - each * peer
    late = rest >= per
    rank = rest - jnp.where(late, per, 0.0)
    from_peer = one_hot(peer, peers)
    seen = dot(from_peer, asked)
    off = iota((slots, 128), 1).astype(F32) - rank
    local = lane_sum(jnp.where(off == 0.0, seen, 0.0))
    turned = lane_sum(jnp.where(off == 16.0, seen, 0.0))
    terms = pick_two(one_hot(local, 256), hi_ref[...], lo_ref[...])
    terms = jnp.where(turned > 0.5, terms[:, 256:], terms[:, :256])
    terms = jnp.where(late, terms[:, 128:], terms[:, :128])
    p_hi, p_lo = halves(part)
    out_ref[...] = jnp.where(rest == 2.0 * per, pick_two(from_peer, p_hi, p_lo), terms)


def own_kernel(came_ref, out_ref):
    peers = came_ref.shape[0] // 25
    each = 25
    rows = came_ref[pl.ds(each - 1, peers, stride=each), :]
    out_ref[...] = jnp.sum(rows, axis=0, keepdims=True)


def face_kernel(far_ref, came_ref, known_ref, meta_ref, far_out, energy_ref, fit_ref, coef_ref, sems, out_sems):
    number = fit_ref.shape[1]
    some = 4
    copies, leaving = [], []
    for k in range(KEEP // some):
        these = slice(k * some, (k + 1) * some)
        copies.append(pltpu.make_async_copy(far_ref.at[these], fit_ref.at[these], sems.at[k]))
        cols = slice(k * some * 256, (k + 1) * some * 256)
        leaving.append(pltpu.make_async_copy(coef_ref.at[:, cols], far_out.at[:, cols], out_sems.at[k]))
    for copy in copies:
        copy.start()
    place = meta_ref[:, 0:1]
    known = known_ref[...]
    one, two, three = (known[p * number : (p + 1) * number] for p in range(3))
    hi, lo = halves(came_ref[...])
    slots = came_ref.shape[0]
    got = [pick_two(one_hot(place + 12.0 * h, slots), hi, lo) for h in range(2)]
    lane = iota((number, 128), 1)
    k, n = iota((128, 256), 0), iota((128, 256), 1)
    two_wide = dot_two(two, (k == (n >> 4)).astype(F32).astype(BF16))
    two_single = dot_two(two, ((k == (n >> 4) + 16) & ((n & 15) == 0)).astype(F32).astype(BF16))
    three_low = jnp.where((lane & 31) < 16, three, 0.0)
    three_wide = three_low + pltpu.roll(three_low, 16, 1)
    start = lane < 16
    first_pair = [g[:number] for g in got]
    first_pair[0] = first_pair[0] + jnp.where(start, pltpu.roll(one, 112, 1), 0.0)
    second_pair = [g[number : 2 * number] for g in got]
    third_pair = [g[2 * number :] for g in got]
    third_pair[0] = third_pair[0] + jnp.where(start, pltpu.roll(three, 112, 1), 0.0)
    third_pair = [t + two_single[:, h * 128 : (h + 1) * 128] for h, t in enumerate(third_pair)]
    both = [two_wide[:, h * 128 : (h + 1) * 128] * three_wide for h in range(2)]
    spaced = (lane & 15) == 0
    energy = jnp.zeros((number, 128), F32)
    for c in range(KEEP):
        if c % some == 0:
            copies[c // some].wait()
        along = jnp.zeros((number, 128), F32)
        for h in range(2):
            moved = pltpu.roll(first_pair[h], 128 - c, 1) if c else first_pair[h]
            value = fit_ref[c, :, h * 128 : (h + 1) * 128] - jnp.where(spaced, moved, 0.0)
            if h == 0:
                shift = (c % 8) * 16
                moved = second_pair[c // 8]
                moved = pltpu.roll(moved, 128 - shift, 1) if shift else moved
                value = value - jnp.where(start, moved, 0.0)
            if c == 0:
                value = value - third_pair[h]
            coef_ref[:, c * 256 + h * 128 : c * 256 + (h + 1) * 128] = value.astype(BF16)
            along = along + value * both[h]
        energy = energy + one[:, c : c + 1] * along
        if c % some == some - 1:
            leaving[c // some].start()
    energy_ref[...] = lax.dot_general(
        jnp.full((8, 128), 1.0, F32), energy, (((1,), (1,)), ((), ())), preferred_element_type=F32, precision=HIGHEST
    )[0:1]
    for copy in leaving:
        copy.wait()


def integral_kernel(*refs):
    *parts, integral_ref, out_ref = refs
    parts = [p[...] for p in parts]
    while len(parts) > 1:
        parts = [parts[i] + parts[i + 1] for i in range(0, len(parts), 2)]
    shape = (out_ref.shape[0], 128)
    total = jnp.where((iota(shape, 1) >> 4) == iota(shape, 0), parts[0], 0.0)
    out_ref[...] = dot_exact(total, integral_ref[...])


def call(kernel, outs, *args, name, apart=(), fetched=(), outs_apart=(), flops=0, scratch=()):
    moved = sum(int(np.prod(a.shape)) * a.dtype.itemsize for a in args) + sum(
        int(np.prod(o.shape)) * o.dtype.itemsize for o in outs
    )
    count = len(args) + len(outs) + len(scratch)

    def fetching(*refs):
        refs, held, sems = list(refs[:count]), refs[count:-1], refs[-1]
        copies = [
            pltpu.make_async_copy(refs[i], buffer, sems.at[k])
            for k, (i, buffer) in enumerate(zip(fetched, held, strict=True))
        ]
        for copy in copies:
            copy.start()
        for copy in copies:
            copy.wait()
        for i, buffer in zip(fetched, held, strict=True):
            refs[i] = buffer
        kernel(*refs)

    extra = []
    if fetched:
        extra = [pltpu.VMEM(args[i].shape, args[i].dtype) for i in fetched]
        extra.append(pltpu.SemaphoreType.DMA((len(fetched),)))
    outside = set(apart) | set(fetched)
    return pl.pallas_call(
        fetching if fetched else kernel,
        out_shape=outs,
        in_specs=[
            pl.BlockSpec(memory_space=pltpu.HBM if i in outside else pltpu.VMEM) for i in range(len(args))
        ],
        out_specs=[
            pl.BlockSpec(memory_space=pltpu.HBM if i in outs_apart else pltpu.VMEM) for i in range(len(outs))
        ],
        scratch_shapes=list(scratch) + extra,
        compiler_params=pltpu.CompilerParams(vmem_limit_bytes=VMEM_LIMIT),
        cost_estimate=pl.CostEstimate(flops=flops, bytes_accessed=moved, transcendentals=0),
        name=name,
    )(*(far(a) if i in outside else a for i, a in enumerate(args)))


def across(a, k):
    return lax.ppermute(a, "grp", [(i, i ^ k) for i in range(lax.axis_size("grp"))])


def far(a):
    return pltpu.with_memory_space_constraint(a, pltpu.HBM)


def shaped(shape, dtype=F32):
    return jax.ShapeDtypeStruct(shape, dtype)


def body(energies, triples, pair_surfaces, pair_slot, single_surfaces, modals, mode_slot):
    devices = lax.axis_size("dev")
    groups = lax.axis_size("grp")
    number = triples.shape[0]
    own = modals.shape[0]
    capacity = 3 * number // devices
    cos_wide = np.zeros((G * S, 128), np.float32)
    fit_wide = np.zeros((G, 128), np.float32)
    cos_block = np.zeros((128, own * G), np.float32)
    for m in range(own):
        cos_wide[::S, m * 32 : m * 32 + KEEP] = COSINES.T
        fit_wide[:, m * 32 + KEEP : m * 32 + 2 * KEEP] = FITTER.T
        cos_block[m * KEEP : (m + 1) * KEEP, m * G : (m + 1) * G] = COSINES
    kron = np.einsum("dh,el->hlde", FITTER, FITTER).reshape(G * G, KEEP * KEEP)
    hi, lo = (jnp.asarray(x) for x in halves_np(kron))
    fit_rows = np.zeros((G, 128), np.float32)
    fit_rows[:, :KEEP] = FITTER.T
    wide = np.zeros((2, 32, G, G))
    wide[0, :KEEP] = FITTER[:, :, None]
    wide[1, :KEEP] = FITTER[:, None, :]
    wide = jnp.asarray(np.stack([h[p] for p in range(2) for h in halves_np(wide.reshape(2, 32, G * G))]))
    send, meta = call(
        ask_kernel,
        [shaped((devices, 2, 128)), shaped((3 * number, 128))],
        triples.T,
        pair_slot,
        mode_slot.reshape(1, -1),
        modals,
        single_surfaces,
        jnp.asarray(cos_wide),
        jnp.asarray(fit_wide),
        fetched=tuple(range(7)),
        name="ask",
    )
    came = lax.all_to_all(send, "dev", 0, 0, tiled=True)
    table = shaped((pair_surfaces.shape[0], 512), BF16)
    first_hi, first_lo = halves_np(np.kron(FITTER, np.eye(8)))
    first = jnp.asarray(np.concatenate([first_hi, first_lo], axis=0))
    table_hi, table_lo, integral = call(
        table_kernel,
        [table, table, shaped((128, S * S))],
        pair_surfaces,
        hi,
        lo,
        modals,
        jnp.asarray(cos_block),
        fetched=(0, 1, 2, 3, 4),
        name="table",
        flops=5 * 10**8,
    )
    each = 2 * capacity + 1
    answer, known = call(
        share_kernel,
        [shaped((devices * each, 128)), shaped((3 * number, 128))],
        came,
        table_hi,
        table_lo,
        energies,
        meta,
        jnp.asarray(fit_rows),
        wide,
        apart=(3, 5, 6),
        name="share",
        flops=10**9,
        scratch=[
            pltpu.VMEM((G, 128), F32),
            pltpu.VMEM((number, G * G), F32),
            pltpu.VMEM((number, G * G), F32),
            pltpu.VMEM((G, 16, 128), F32),
            pltpu.VMEM(energies.shape, BF16),
            pltpu.VMEM(fit_rows.shape, F32),
            pltpu.VMEM(wide.shape, BF16),
            pltpu.SemaphoreType.DMA((number // 16,)),
            pltpu.SemaphoreType.DMA((2,)),
        ],
    )
    terms = lax.all_to_all(
        answer.reshape(devices, each, 1, 128), "dev", 0, 0, tiled=True
    ).reshape(devices * each, 128)
    (fitted,) = call(
        fit_kernel,
        [pltpu.HBM((KEEP, number, KEEP**2), F32)],
        energies,
        hi,
        lo,
        first,
        apart=(0,),
        outs_apart=(0,),
        scratch=[
            pltpu.VMEM(energies.shape, BF16),
            pltpu.VMEM((KEEP, number, KEEP**2), F32),
            pltpu.SemaphoreType.DMA((number // FIT_TILE,)),
            pltpu.SemaphoreType.DMA((number // FIT_TILE,)),
        ],
        name="fit",
        flops=5 * 10**9,
    )
    terms, fitted = lax.optimization_barrier((terms, fitted))
    (mine,) = call(own_kernel, [shaped((1, 128))], terms, name="own")
    mine = mine + across(mine, 1)
    parts = [mine] + [across(mine, k) for k in range(2, groups, 2)]
    mine, known = lax.optimization_barrier((mine, known))
    coefficients, energy = call(
        face_kernel,
        [pltpu.HBM((number, KEEP**3), BF16), shaped((1, number))],
        fitted,
        terms,
        known,
        meta,
        apart=(0,),
        outs_apart=(0,),
        scratch=[
            pltpu.VMEM((KEEP, number, KEEP**2), F32),
            pltpu.VMEM((number, KEEP**3), BF16),
            pltpu.SemaphoreType.DMA((4,)),
            pltpu.SemaphoreType.DMA((4,)),
        ],
        name="faces",
        flops=10**9,
    )
    (mean_field,) = call(
        integral_kernel,
        [shaped((own, S * S))],
        *parts,
        integral,
        name="integrals",
    )
    return coefficients, energy.reshape(number), mean_field


def solution(mesh):
    in_specs = (
        P(("grp", "dev"), None),
        P(("grp", "dev"), None),
        P("dev", None),
        P(),
        P("dev", None),
        P("dev", None),
        P(),
    )
    out_specs = (P(("grp", "dev"), None), P(("grp", "dev")), P("dev", None))
    return jax.shard_map(body, mesh=mesh, in_specs=in_specs, out_specs=out_specs, check_vma=False)
```

```python
import numpy as np
import jax
import jax.numpy as jnp
from jax import lax
from jax.experimental import pallas as pl
from jax.experimental.pallas import tpu as pltpu
from jax.sharding import PartitionSpec as P

G = 32
KEEP = 16
S = 16
F32 = jnp.float32
BF16 = jnp.bfloat16
HIGHEST = lax.Precision.HIGHEST
VMEM_LIMIT = 24 * 2**20


def tables():
    orders = np.arange(KEEP, dtype=np.float64)
    points = np.arange(G, dtype=np.float64) + 0.5
    cosines = np.cos(np.pi * orders[:, None] * points[None, :] / G)
    weights = np.where(orders == 0, 1.0, 2.0) / G
    return cosines, weights[:, None] * cosines


COSINES, FITTER = tables()


def halves(a):
    hi = a.astype(BF16)
    return hi, (a - hi.astype(F32)).astype(BF16)


def halves_np(a):
    a = a.astype(np.float32)
    hi = a.astype(jnp.bfloat16)
    return hi, (a - hi.astype(np.float32)).astype(jnp.bfloat16)


def dot(a, b):
    return jnp.dot(a, b, preferred_element_type=F32)


def dot_exact(a, b):
    return jnp.dot(a, b, preferred_element_type=F32, precision=HIGHEST)


def iota(shape, dim):
    return lax.broadcasted_iota(jnp.int32, shape, dim)


def lane_sum(a):
    return jnp.sum(a, axis=1, keepdims=True)


def column(row):
    n = row.shape[1]
    return lane_sum(jnp.where(iota((n, n), 0) == iota((n, n), 1), row, 0.0))


def one_hot(column_f, width):
    return (iota((column_f.shape[0], width), 1).astype(F32) == column_f).astype(F32).astype(BF16)


def dot_two(a, b):
    hi, lo = halves(a)
    return dot(hi, b) + dot(lo, b)


def pick_two(pick, hi, lo):
    return dot(pick, hi) + dot(pick, lo)


def ask_kernel(tri_ref, pair_ref, slot_ref, modal_ref, single_ref, cos_ref, fit_ref, out_ref, meta_ref):
    modes = slot_ref.shape[1]
    tri = tri_ref[...].astype(F32)
    first, second, third = (column(tri[p : p + 1]) for p in range(3))
    lower = jnp.concatenate([first, first, second], axis=0)
    upper = jnp.concatenate([second, third, third], axis=0)
    each = jnp.concatenate([first, second, third], axis=0)
    rows = lower.shape[0]
    number = rows // 3
    lane = iota((rows, modes), 1).astype(F32)
    pair = pair_ref[...]
    high = (pair >> 8).astype(F32).astype(BF16)
    low = (pair & 255).astype(F32).astype(BF16)
    pick = (lane == lower).astype(F32).astype(BF16)
    at = lane == upper
    owner = lane_sum(jnp.where(at, dot(pick, high), 0.0))
    local = lane_sum(jnp.where(at, dot(pick, low), 0.0))
    slots = slot_ref[...]
    slots = ((slots & 3) * 32 + (slots >> 2)).astype(F32)
    slot = lane_sum(jnp.where(lane == each, slots, 0.0))
    wide = iota((rows, 128), 1)
    wide_f = wide.astype(F32)
    hit = wide_f == owner
    hit_b = hit.astype(F32).astype(BF16)
    earlier = (iota((rows, rows), 1) < iota((rows, rows), 0)).astype(F32).astype(BF16)
    rank = lane_sum(jnp.where(hit, dot(earlier, hit_b), 0.0))
    ordered = lower < upper
    is_first = iota((rows, 1), 0) < number
    turned = jnp.where(is_first, ordered.astype(F32), 1.0 - ordered.astype(F32))
    s1, s2, s3 = (slot[p * number : (p + 1) * number] for p in range(3))
    left = jnp.concatenate([s1, s1, s2], axis=0)
    right = jnp.concatenate([s2, s3, s3], axis=0)
    other = jnp.concatenate([s3, s2, s1], axis=0)
    small = jnp.where(ordered, left, right)
    large = jnp.where(ordered, right, left)
    off = wide_f - rank
    said = jnp.where(off == 0.0, local, 0.0)
    for k, value in enumerate((turned, small, large, other)):
        said = said + jnp.where(off == 16.0 * (k + 1), value, 0.0)
    asked = lax.dot_general(hit_b, said.astype(BF16), (((0,), (0,)), ((), ())), preferred_element_type=F32)
    square = modal_ref[...] * modal_ref[...]
    mine = dot_exact(square, cos_ref[...]) + dot_exact(single_ref[...], fit_ref[...])
    four = mine.shape
    mine = jnp.sum(jnp.where((iota(four, 1) >> 5) == iota(four, 0), mine, 0.0), axis=0, keepdims=True)
    peers = out_ref.shape[0]
    out_ref[:, 0, :] = jnp.broadcast_to(mine, (peers, 128))
    out_ref[:, 1, :] = asked[:peers]
    meta_ref[...] = jnp.where(wide == 0, owner * 25.0 + rank, jnp.where(wide == 1, slot, 0.0))


FIT_TILE = 32
NEAR = 10


def fit_some(energy_ref, hi_ref, lo_ref, first_ref, out_refs, start):
    cells = G * G
    few = 8
    rows = pl.ds(pl.multiple_of(start, FIT_TILE), FIT_TILE)
    stacked = jnp.concatenate([energy_ref[rows, g * cells : (g + 1) * cells] for g in range(G)], axis=0)
    two = dot(stacked, hi_ref[...]) + dot(stacked, lo_ref[...])
    half = first_ref.shape[0] // 2
    for h in range(FIT_TILE // few):
        at = h * few
        part = jnp.concatenate(
            [two[g * FIT_TILE + at : g * FIT_TILE + at + few] for g in range(G)], axis=0
        )
        p_hi, p_lo = halves(part)
        large = dot(first_ref[...], p_hi)
        all_three = large[:half] + large[half:] + dot(first_ref[:half], p_lo)
        some = pl.ds(pl.multiple_of(start + at, few), few)
        for c in range(KEEP):
            out_refs[c][some, :] = all_three[c * few : (c + 1) * few]


def table_kernel(
    pair_ref,
    hi_ref,
    lo_ref,
    modal_ref,
    cosine_ref,
    table_hi_ref,
    table_lo_ref,
    integral_ref,
):
    a_hi, a_lo = halves(pair_ref[...])
    k_hi, k_lo = hi_ref[...], lo_ref[...]
    terms = dot(a_hi, k_hi) + dot(a_hi, k_lo) + dot(a_lo, k_hi)
    square = (256, 256)
    i, j = iota(square, 0), iota(square, 1)
    turn = (((i & 15) == (j >> 4)) & ((i >> 4) == (j & 15))).astype(F32).astype(BF16)
    t_hi, t_lo = halves(terms)
    table_hi_ref[:, :256] = t_hi
    table_lo_ref[:, :256] = t_lo
    table_hi_ref[:, 256:] = dot(t_hi, turn).astype(BF16)
    table_lo_ref[:, 256:] = dot(t_lo, turn).astype(BF16)
    modal = modal_ref[...]
    own = modal.shape[0]
    row = iota((own * G, G * S), 0)
    lane = iota((own * G, G * S), 1)
    spread = jnp.zeros((own * G, G * S), F32)
    for m in range(own):
        spread = jnp.where((row >> 5) == m, modal[m : m + 1, :], spread)
    spread = jnp.where((lane >> 4) == (row & 31), spread, 0.0)
    k, n = iota((G * S, 256), 0), iota((G * S, 256), 1)
    hi, lo = halves(spread)
    to_left = ((k & 15) == (n >> 4)).astype(F32).astype(BF16)
    to_right = ((k & 15) == (n & 15)).astype(F32).astype(BF16)
    left = dot(hi, to_left) + dot(lo, to_left)
    right = dot(hi, to_right) + dot(lo, to_right)
    integral_ref[...] = dot_exact(cosine_ref[...], left * right)


def fit_kernel(source_ref, hi_ref, lo_ref, first_ref, *refs):
    near_refs = list(refs[:NEAR])
    far_ref, energy_ref, rest_ref, sems, out_sems = refs[NEAR:]
    tiles = energy_ref.shape[0] // FIT_TILE
    out_refs = near_refs + [rest_ref.at[c] for c in range(KEEP - NEAR)]

    def copy(r):
        rows = pl.ds(pl.multiple_of(r * FIT_TILE, FIT_TILE), FIT_TILE)
        return pltpu.make_async_copy(source_ref.at[rows], energy_ref.at[rows], sems.at[r])

    def copy_out(r):
        rows = pl.ds(pl.multiple_of(r * FIT_TILE, FIT_TILE), FIT_TILE)
        return pltpu.make_async_copy(rest_ref.at[:, rows], far_ref.at[:, rows], out_sems.at[r])

    for r in range(2):
        copy(r).start()

    def over_rows(r, carry):
        copy(r).wait()

        @pl.when(r + 2 < tiles)
        def _():
            copy(r + 2).start()

        fit_some(energy_ref, hi_ref, lo_ref, first_ref, out_refs, r * FIT_TILE)
        copy_out(r).start()
        return carry

    lax.fori_loop(0, tiles, over_rows, 0)
    for r in range(tiles):
        copy_out(r).wait()


def share_kernel(
    came_ref,
    hi_ref,
    lo_ref,
    source_ref,
    meta_ref,
    fit_in,
    wide_in,
    out_ref,
    known_ref,
    w1_ref,
    w23_ref,
    lead_ref,
    along_ref,
    energy_ref,
    fit_ref,
    wide_ref,
    sems,
    more_sems,
):
    tile = 16
    tables_in = [
        pltpu.make_async_copy(fit_in, fit_ref, more_sems.at[0]),
        pltpu.make_async_copy(wide_in, wide_ref, more_sems.at[1]),
    ]
    for part in tables_in:
        part.start()

    def copy(r):
        rows_r = pl.ds(pl.multiple_of(r * tile, tile), tile)
        return pltpu.make_async_copy(source_ref.at[rows_r], energy_ref.at[rows_r], sems.at[r])

    tiles, ahead = energy_ref.shape[0] // tile, 4
    for r in range(ahead):
        copy(r).start()
    peers = came_ref.shape[0]
    number = energy_ref.shape[0]
    rows = 3 * number
    asked = came_ref[:, 1, :].astype(BF16)
    per = float(rows // peers)
    at = iota((rows, 1), 0).astype(F32)
    peer = jnp.floor((at + 0.5) * (1.0 / per))
    rank = at - per * peer
    seen = dot(one_hot(peer, peers), asked)
    off = iota((rows, 128), 1).astype(F32) - rank
    local, small, large, other = (
        lane_sum(jnp.where(off == 16.0 * k, seen, 0.0)) for k in (0, 2, 3, 4)
    )
    slot = jnp.concatenate([meta_ref[:, 1:2], small, large, other], axis=0)
    pick = one_hot(slot, 128)
    ground = came_ref[:, 0, :]
    spots = 128 // peers
    ground = jnp.concatenate([pltpu.roll(ground, 128 - 32 * j, 1) if j else ground for j in range(spots)], axis=0)
    ground = jnp.where(iota((128, 128), 1) < 32, ground, 0.0)
    ground = ground + pltpu.roll(ground, 32, 1)
    ground = ground + pltpu.roll(ground, 64, 1)
    known = pick_two(pick, *halves(ground))
    known_ref[...] = known[:rows]
    k, n = iota((128, 256), 0), iota((128, 256), 1)
    widen = (k == (n >> 4)).astype(F32).astype(BF16)
    k, n = iota((256, 128), 0), iota((256, 128), 1)
    to_high = ((k >> 4) == n).astype(F32).astype(BF16)
    to_low = ((k & 15) == n).astype(F32).astype(BF16)

    def repeated(a):
        part = jnp.where((iota(a.shape, 1) & 31) < 16, a, 0.0)
        return part + pltpu.roll(part, 16, 1)

    def twice(a):
        return jnp.concatenate([a, a], axis=1)

    terms = pick_two(one_hot(local, 256), hi_ref[:, :256], lo_ref[:, :256])
    g_small, g_large, g_other = (known[p * rows : (p + 1) * rows] for p in (1, 2, 3))
    of_small = dot_two(terms * twice(repeated(g_large)), to_high)
    of_large = dot_two(terms * dot_two(g_small, widen), to_low)
    norm = g_other[:, 0:1]
    of_other = lane_sum(of_small * g_small)
    lane = iota((rows, 128), 1)
    shares = [-norm * of_small, -norm * of_large, jnp.where(lane == 0, -of_other, 0.0)]
    one, two, three = (known[p * number : (p + 1) * number] for p in range(3))
    cells = G * G
    for part in tables_in:
        part.wait()
    w1_ref[...] = jnp.broadcast_to(lane_sum(fit_ref[...] * one[0:1]), w1_ref.shape)
    ways = [wide_ref[p] for p in range(4)]

    def weights(a, hi, lo):
        a_hi, a_lo = halves(a[:, :32])
        return dot(a_hi, hi) + dot(a_hi, lo) + dot(a_lo, hi)

    w2 = weights(two, ways[0], ways[1])
    w3 = weights(three, ways[2], ways[3])
    w23_ref[...] = w2 * w3
    lanes = cells // 128

    def over_rows(r, carry):
        copy(r).wait()

        @pl.when(r + ahead < tiles)
        def _():
            copy(r + ahead).start()

        rows_r = pl.ds(pl.multiple_of(r * tile, tile), tile)
        w23 = [w23_ref[rows_r, k * 128 : (k + 1) * 128] for k in range(lanes)]

        def over_points(g, lead):
            x = energy_ref[rows_r, pl.ds(pl.multiple_of(g * cells, cells), cells)].astype(F32)
            w1 = w1_ref[pl.ds(g, 1), :]
            fresh, along = [], None
            for k in range(lanes):
                part = x[:, k * 128 : (k + 1) * 128]
                fresh.append(lead[k] + w1 * part)
                term = part * w23[k]
                along = term if along is None else along + term
            along_ref[g] += along
            return tuple(fresh)

        none = jnp.zeros((tile, 128), F32)
        lead = lax.fori_loop(0, G, over_points, (none,) * lanes, unroll=8)
        for k in range(lanes):
            lead_ref[rows_r, k * 128 : (k + 1) * 128] = lead[k]
        return carry

    along_ref[...] = jnp.zeros_like(along_ref)
    lax.fori_loop(0, tiles, over_rows, 0)

    def back(a, hi, lo):
        a_hi, a_lo = halves(a)
        dims = (((1,), (1,)), ((), ()))
        total = lax.dot_general(a_hi, hi, dims, preferred_element_type=F32)
        total = total + lax.dot_general(a_hi, lo, dims, preferred_element_type=F32)
        total = total + lax.dot_general(a_lo, hi, dims, preferred_element_type=F32)
        return jnp.concatenate([total, jnp.zeros((number, 96), F32)], axis=1)

    sums = lane_sum(jnp.sum(along_ref[...], axis=1))
    field_first = jnp.sum(sums * fit_ref[...], axis=0, keepdims=True)
    field_first = jnp.where(iota((number, 128), 0) == 0, field_first, 0.0)
    field_second = back(lead_ref[...] * w3, ways[0], ways[1])
    field_third = back(lead_ref[...] * w2, ways[2], ways[3])
    own = known[:rows]
    lane = iota((rows, 128), 1)
    single = jnp.where(lane < 16, pltpu.roll(own, 112, 1), 0.0)
    along = lane_sum(single * own)
    norms = own[:, 0:1]
    n1, n2, n3 = (norms[p * number : (p + 1) * number] for p in range(3))
    q1, q2, q3 = (along[p * number : (p + 1) * number] for p in range(3))
    scale = jnp.concatenate([n2 * n3, n1 * n3, n1 * n2], axis=0)
    shift = jnp.concatenate([n3 * q2 + n2 * q3, n3 * q1 + n1 * q3, n2 * q1 + n1 * q2], axis=0)
    from_grid = jnp.concatenate([field_first, field_second, field_third], axis=0)
    from_grid = from_grid - scale * single - jnp.where(lane == 0, shift, 0.0)
    fields = jnp.concatenate([from_grid] + shares, axis=0)
    f_hi, f_lo = halves(fields)
    dims = (((0,), (0,)), ((), ()))
    part = lax.dot_general(pick, f_hi, dims, preferred_element_type=F32) + lax.dot_general(
        pick, f_lo, dims, preferred_element_type=F32
    )
    part = part[:peers] + sum(
        pltpu.roll(part[j * peers : (j + 1) * peers], 16 * j, 1) for j in range(1, spots)
    )
    slots = out_ref.shape[0]
    each = float(slots // peers)
    at = iota((slots, 1), 0).astype(F32)
    peer = jnp.floor((at + 0.5) * (1.0 / each))
    rest = at - each * peer
    late = rest >= per
    rank = rest - jnp.where(late, per, 0.0)
    from_peer = one_hot(peer, peers)
    seen = dot(from_peer, asked)
    off = iota((slots, 128), 1).astype(F32) - rank
    local = lane_sum(jnp.where(off == 0.0, seen, 0.0))
    turned = lane_sum(jnp.where(off == 16.0, seen, 0.0))
    terms = pick_two(one_hot(local, 256), hi_ref[...], lo_ref[...])
    terms = jnp.where(turned > 0.5, terms[:, 256:], terms[:, :256])
    terms = jnp.where(late, terms[:, 128:], terms[:, :128])
    p_hi, p_lo = halves(part)
    out_ref[...] = jnp.where(rest == 2.0 * per, pick_two(from_peer, p_hi, p_lo), terms)


def own_kernel(came_ref, out_ref):
    peers = came_ref.shape[0] // 25
    each = 25
    rows = came_ref[pl.ds(each - 1, peers, stride=each), :]
    out_ref[...] = jnp.sum(rows, axis=0, keepdims=True)


def face_kernel(*refs):
    far_ref, came_ref, known_ref, meta_ref, far_out, energy_ref, coef_ref, rest_ref, out_sems, sem = refs[NEAR:]
    fit_refs = list(refs[:NEAR]) + [rest_ref.at[c] for c in range(KEEP - NEAR)]
    coming = pltpu.make_async_copy(far_ref, rest_ref, sem)
    coming.start()
    number = coef_ref.shape[0]
    some = 4
    leaving = []
    for k in range(KEEP // some):
        cols = slice(k * some * 256, (k + 1) * some * 256)
        leaving.append(pltpu.make_async_copy(coef_ref.at[:, cols], far_out.at[:, cols], out_sems.at[k]))
    place = meta_ref[:, 0:1]
    known = known_ref[...]
    one, two, three = (known[p * number : (p + 1) * number] for p in range(3))
    hi, lo = halves(came_ref[...])
    slots = came_ref.shape[0]
    got = [pick_two(one_hot(place + 12.0 * h, slots), hi, lo) for h in range(2)]
    lane = iota((number, 128), 1)
    k, n = iota((128, 256), 0), iota((128, 256), 1)
    two_wide = dot_two(two, (k == (n >> 4)).astype(F32).astype(BF16))
    two_single = dot_two(two, ((k == (n >> 4) + 16) & ((n & 15) == 0)).astype(F32).astype(BF16))
    three_low = jnp.where((lane & 31) < 16, three, 0.0)
    three_wide = three_low + pltpu.roll(three_low, 16, 1)
    start = lane < 16
    first_pair = [g[:number] for g in got]
    first_pair[0] = first_pair[0] + jnp.where(start, pltpu.roll(one, 112, 1), 0.0)
    second_pair = [g[number : 2 * number] for g in got]
    third_pair = [g[2 * number :] for g in got]
    third_pair[0] = third_pair[0] + jnp.where(start, pltpu.roll(three, 112, 1), 0.0)
    third_pair = [t + two_single[:, h * 128 : (h + 1) * 128] for h, t in enumerate(third_pair)]
    both = [two_wide[:, h * 128 : (h + 1) * 128] * three_wide for h in range(2)]
    spaced = (lane & 15) == 0
    energy = jnp.zeros((number, 128), F32)
    for c in range(KEEP):
        if c == NEAR:
            coming.wait()
        along = jnp.zeros((number, 128), F32)
        for h in range(2):
            moved = pltpu.roll(first_pair[h], 128 - c, 1) if c else first_pair[h]
            value = fit_refs[c][:, h * 128 : (h + 1) * 128] - jnp.where(spaced, moved, 0.0)
            if h == 0:
                shift = (c % 8) * 16
                moved = second_pair[c // 8]
                moved = pltpu.roll(moved, 128 - shift, 1) if shift else moved
                value = value - jnp.where(start, moved, 0.0)
            if c == 0:
                value = value - third_pair[h]
            coef_ref[:, c * 256 + h * 128 : c * 256 + (h + 1) * 128] = value.astype(BF16)
            along = along + value * both[h]
        energy = energy + one[:, c : c + 1] * along
        if c % some == some - 1:
            leaving[c // some].start()
    energy_ref[...] = lax.dot_general(
        jnp.full((8, 128), 1.0, F32), energy, (((1,), (1,)), ((), ())), preferred_element_type=F32, precision=HIGHEST
    )[0:1]
    for copy in leaving:
        copy.wait()


def integral_kernel(*refs):
    *parts, integral_ref, out_ref = refs
    parts = [p[...] for p in parts]
    while len(parts) > 1:
        parts = [parts[i] + parts[i + 1] for i in range(0, len(parts), 2)]
    shape = (out_ref.shape[0], 128)
    total = jnp.where((iota(shape, 1) >> 4) == iota(shape, 0), parts[0], 0.0)
    out_ref[...] = dot_exact(total, integral_ref[...])


def call(kernel, outs, *args, name, apart=(), fetched=(), outs_apart=(), flops=0, scratch=()):
    moved = sum(int(np.prod(a.shape)) * a.dtype.itemsize for a in args) + sum(
        int(np.prod(o.shape)) * o.dtype.itemsize for o in outs
    )
    count = len(args) + len(outs) + len(scratch)

    def fetching(*refs):
        refs, held, sems = list(refs[:count]), refs[count:-1], refs[-1]
        copies = [
            pltpu.make_async_copy(refs[i], buffer, sems.at[k])
            for k, (i, buffer) in enumerate(zip(fetched, held, strict=True))
        ]
        for copy in copies:
            copy.start()
        for copy in copies:
            copy.wait()
        for i, buffer in zip(fetched, held, strict=True):
            refs[i] = buffer
        kernel(*refs)

    extra = []
    if fetched:
        extra = [pltpu.VMEM(args[i].shape, args[i].dtype) for i in fetched]
        extra.append(pltpu.SemaphoreType.DMA((len(fetched),)))
    outside = set(apart) | set(fetched)
    return pl.pallas_call(
        fetching if fetched else kernel,
        out_shape=outs,
        in_specs=[
            pl.BlockSpec(memory_space=pltpu.HBM if i in outside else pltpu.VMEM) for i in range(len(args))
        ],
        out_specs=[
            pl.BlockSpec(memory_space=pltpu.HBM if i in outs_apart else pltpu.VMEM) for i in range(len(outs))
        ],
        scratch_shapes=list(scratch) + extra,
        compiler_params=pltpu.CompilerParams(vmem_limit_bytes=VMEM_LIMIT),
        cost_estimate=pl.CostEstimate(flops=flops, bytes_accessed=moved, transcendentals=0),
        name=name,
    )(*(far(a) if i in outside else a for i, a in enumerate(args)))


def across(a, k):
    return lax.ppermute(a, "grp", [(i, i ^ k) for i in range(lax.axis_size("grp"))])


def far(a):
    return pltpu.with_memory_space_constraint(a, pltpu.HBM)


def shaped(shape, dtype=F32):
    return jax.ShapeDtypeStruct(shape, dtype)


def body(energies, triples, pair_surfaces, pair_slot, single_surfaces, modals, mode_slot):
    devices = lax.axis_size("dev")
    groups = lax.axis_size("grp")
    number = triples.shape[0]
    own = modals.shape[0]
    capacity = 3 * number // devices
    cos_wide = np.zeros((G * S, 128), np.float32)
    fit_wide = np.zeros((G, 128), np.float32)
    cos_block = np.zeros((128, own * G), np.float32)
    for m in range(own):
        cos_wide[::S, m * 32 : m * 32 + KEEP] = COSINES.T
        fit_wide[:, m * 32 + KEEP : m * 32 + 2 * KEEP] = FITTER.T
        cos_block[m * KEEP : (m + 1) * KEEP, m * G : (m + 1) * G] = COSINES
    kron = np.einsum("dh,el->hlde", FITTER, FITTER).reshape(G * G, KEEP * KEEP)
    hi, lo = (jnp.asarray(x) for x in halves_np(kron))
    fit_rows = np.zeros((G, 128), np.float32)
    fit_rows[:, :KEEP] = FITTER.T
    wide = np.zeros((2, 32, G, G))
    wide[0, :KEEP] = FITTER[:, :, None]
    wide[1, :KEEP] = FITTER[:, None, :]
    wide = jnp.asarray(np.stack([h[p] for p in range(2) for h in halves_np(wide.reshape(2, 32, G * G))]))
    send, meta = call(
        ask_kernel,
        [shaped((devices, 2, 128)), shaped((3 * number, 128))],
        triples.T,
        pair_slot,
        mode_slot.reshape(1, -1),
        modals,
        single_surfaces,
        jnp.asarray(cos_wide),
        jnp.asarray(fit_wide),
        fetched=tuple(range(7)),
        name="ask",
    )
    came = lax.all_to_all(send, "dev", 0, 0, tiled=True)
    table = shaped((pair_surfaces.shape[0], 512), BF16)
    first_hi, first_lo = halves_np(np.kron(FITTER, np.eye(8)))
    first = jnp.asarray(np.concatenate([first_hi, first_lo], axis=0))
    table_hi, table_lo, integral = call(
        table_kernel,
        [table, table, shaped((128, S * S))],
        pair_surfaces,
        hi,
        lo,
        modals,
        jnp.asarray(cos_block),
        fetched=(0, 1, 2, 3, 4),
        name="table",
        flops=5 * 10**8,
    )
    each = 2 * capacity + 1
    answer, known = call(
        share_kernel,
        [shaped((devices * each, 128)), shaped((3 * number, 128))],
        came,
        table_hi,
        table_lo,
        energies,
        meta,
        jnp.asarray(fit_rows),
        wide,
        apart=(3, 5, 6),
        name="share",
        flops=10**9,
        scratch=[
            pltpu.VMEM((G, 128), F32),
            pltpu.VMEM((number, G * G), F32),
            pltpu.VMEM((number, G * G), F32),
            pltpu.VMEM((G, 16, 128), F32),
            pltpu.VMEM(energies.shape, BF16),
            pltpu.VMEM(fit_rows.shape, F32),
            pltpu.VMEM(wide.shape, BF16),
            pltpu.SemaphoreType.DMA((number // 16,)),
            pltpu.SemaphoreType.DMA((2,)),
        ],
    )
    terms = lax.all_to_all(
        answer.reshape(devices, each, 1, 128), "dev", 0, 0, tiled=True
    ).reshape(devices * each, 128)
    far_part = (KEEP - NEAR, number, KEEP**2)
    fitted = call(
        fit_kernel,
        [shaped((number, KEEP**2))] * NEAR + [pltpu.HBM(far_part, F32)],
        energies,
        hi,
        lo,
        first,
        apart=(0,),
        outs_apart=(NEAR,),
        scratch=[
            pltpu.VMEM(energies.shape, BF16),
            pltpu.VMEM(far_part, F32),
            pltpu.SemaphoreType.DMA((number // FIT_TILE,)),
            pltpu.SemaphoreType.DMA((number // FIT_TILE,)),
        ],
        name="fit",
        flops=5 * 10**9,
    )
    terms, fitted = lax.optimization_barrier((terms, fitted))
    (mine,) = call(own_kernel, [shaped((1, 128))], terms, name="own")
    mine = mine + across(mine, 1)
    parts = [mine] + [across(mine, k) for k in range(2, groups, 2)]
    mine, known = lax.optimization_barrier((mine, known))
    coefficients, energy = call(
        face_kernel,
        [pltpu.HBM((number, KEEP**3), BF16), shaped((1, number))],
        *fitted,
        terms,
        known,
        meta,
        apart=(NEAR,),
        outs_apart=(0,),
        scratch=[
            pltpu.VMEM((number, KEEP**3), BF16),
            pltpu.VMEM(far_part, F32),
            pltpu.SemaphoreType.DMA((4,)),
            pltpu.SemaphoreType.DMA,
        ],
        name="faces",
        flops=10**9,
    )
    (mean_field,) = call(
        integral_kernel,
        [shaped((own, S * S))],
        *parts,
        integral,
        name="integrals",
    )
    return coefficients, energy.reshape(number), mean_field


def solution(mesh):
    in_specs = (
        P(("grp", "dev"), None),
        P(("grp", "dev"), None),
        P("dev", None),
        P(),
        P("dev", None),
        P("dev", None),
        P(),
    )
    out_specs = (P(("grp", "dev"), None), P(("grp", "dev")), P("dev", None))
    return jax.shard_map(body, mesh=mesh, in_specs=in_specs, out_specs=out_specs, check_vma=False)
```

```python
import numpy as np
import jax
import jax.numpy as jnp
from jax import lax
from jax.experimental import pallas as pl
from jax.experimental.pallas import tpu as pltpu
from jax.sharding import PartitionSpec as P

G = 32
KEEP = 16
S = 16
F32 = jnp.float32
BF16 = jnp.bfloat16
HIGHEST = lax.Precision.HIGHEST
VMEM_LIMIT = 24 * 2**20


def tables():
    orders = np.arange(KEEP, dtype=np.float64)
    points = np.arange(G, dtype=np.float64) + 0.5
    cosines = np.cos(np.pi * orders[:, None] * points[None, :] / G)
    weights = np.where(orders == 0, 1.0, 2.0) / G
    return cosines, weights[:, None] * cosines


COSINES, FITTER = tables()


def halves(a):
    hi = a.astype(BF16)
    return hi, (a - hi.astype(F32)).astype(BF16)


def halves_np(a):
    a = a.astype(np.float32)
    hi = a.astype(jnp.bfloat16)
    return hi, (a - hi.astype(np.float32)).astype(jnp.bfloat16)


def dot(a, b):
    return jnp.dot(a, b, preferred_element_type=F32)


def dot_exact(a, b):
    return jnp.dot(a, b, preferred_element_type=F32, precision=HIGHEST)


def iota(shape, dim):
    return lax.broadcasted_iota(jnp.int32, shape, dim)


def lane_sum(a):
    return jnp.sum(a, axis=1, keepdims=True)


def column(row):
    n = row.shape[1]
    return lane_sum(jnp.where(iota((n, n), 0) == iota((n, n), 1), row, 0.0))


def one_hot(column_f, width):
    return (iota((column_f.shape[0], width), 1).astype(F32) == column_f).astype(F32).astype(BF16)


def dot_two(a, b):
    hi, lo = halves(a)
    return dot(hi, b) + dot(lo, b)


def pick_two(pick, hi, lo):
    return dot(pick, hi) + dot(pick, lo)


def ask_kernel(tri_ref, pair_ref, slot_ref, modal_ref, single_ref, cos_ref, fit_ref, out_ref, meta_ref):
    modes = slot_ref.shape[1]
    tri = tri_ref[...].astype(F32)
    first, second, third = (column(tri[p : p + 1]) for p in range(3))
    lower = jnp.concatenate([first, first, second], axis=0)
    upper = jnp.concatenate([second, third, third], axis=0)
    each = jnp.concatenate([first, second, third], axis=0)
    rows = lower.shape[0]
    number = rows // 3
    lane = iota((rows, modes), 1).astype(F32)
    pair = pair_ref[...]
    high = (pair >> 8).astype(F32).astype(BF16)
    low = (pair & 255).astype(F32).astype(BF16)
    pick = (lane == lower).astype(F32).astype(BF16)
    at = lane == upper
    owner = lane_sum(jnp.where(at, dot(pick, high), 0.0))
    local = lane_sum(jnp.where(at, dot(pick, low), 0.0))
    slots = slot_ref[...]
    slots = ((slots & 3) * 32 + (slots >> 2)).astype(F32)
    slot = lane_sum(jnp.where(lane == each, slots, 0.0))
    wide = iota((rows, 128), 1)
    wide_f = wide.astype(F32)
    hit = wide_f == owner
    hit_b = hit.astype(F32).astype(BF16)
    earlier = (iota((rows, rows), 1) < iota((rows, rows), 0)).astype(F32).astype(BF16)
    rank = lane_sum(jnp.where(hit, dot(earlier, hit_b), 0.0))
    ordered = lower < upper
    is_first = iota((rows, 1), 0) < number
    turned = jnp.where(is_first, ordered.astype(F32), 1.0 - ordered.astype(F32))
    s1, s2, s3 = (slot[p * number : (p + 1) * number] for p in range(3))
    left = jnp.concatenate([s1, s1, s2], axis=0)
    right = jnp.concatenate([s2, s3, s3], axis=0)
    other = jnp.concatenate([s3, s2, s1], axis=0)
    small = jnp.where(ordered, left, right)
    large = jnp.where(ordered, right, left)
    off = wide_f - rank
    said = jnp.where(off == 0.0, local, 0.0)
    for k, value in enumerate((turned, small, large, other)):
        said = said + jnp.where(off == 16.0 * (k + 1), value, 0.0)
    asked = lax.dot_general(hit_b, said.astype(BF16), (((0,), (0,)), ((), ())), preferred_element_type=F32)
    square = modal_ref[...] * modal_ref[...]
    spread = jnp.broadcast_to(cos_ref[...][:, None, :], (G, S, 128)).reshape(G * S, 128)
    spread = jnp.where((iota((G * S, 128), 0) & 15) == 0, spread, 0.0)
    mine = dot_exact(square, spread) + dot_exact(single_ref[...], fit_ref[...])
    four = mine.shape
    mine = jnp.sum(jnp.where((iota(four, 1) >> 5) == iota(four, 0), mine, 0.0), axis=0, keepdims=True)
    peers = out_ref.shape[0]
    out_ref[:, 0, :] = jnp.broadcast_to(mine, (peers, 128))
    out_ref[:, 1, :] = asked[:peers]
    meta_ref[...] = jnp.where(wide == 0, owner * 25.0 + rank, jnp.where(wide == 1, slot, 0.0))


FIT_TILE = 32
NEAR = 10


def fit_some(energy_ref, hi_ref, lo_ref, first_ref, out_refs, start):
    cells = G * G
    few = 8
    rows = pl.ds(pl.multiple_of(start, FIT_TILE), FIT_TILE)
    stacked = jnp.concatenate([energy_ref[rows, g * cells : (g + 1) * cells] for g in range(G)], axis=0)
    two = dot(stacked, hi_ref[...]) + dot(stacked, lo_ref[...])
    half = first_ref.shape[0] // 2
    for h in range(FIT_TILE // few):
        at = h * few
        part = jnp.concatenate(
            [two[g * FIT_TILE + at : g * FIT_TILE + at + few] for g in range(G)], axis=0
        )
        p_hi, p_lo = halves(part)
        large = dot(first_ref[...], p_hi)
        all_three = large[:half] + large[half:] + dot(first_ref[:half], p_lo)
        some = pl.ds(pl.multiple_of(start + at, few), few)
        for c in range(KEEP):
            out_refs[c][some, :] = all_three[c * few : (c + 1) * few]


def table_kernel(
    pair_ref,
    hi_ref,
    lo_ref,
    modal_ref,
    cosine_ref,
    table_hi_ref,
    table_lo_ref,
    integral_ref,
):
    a_hi, a_lo = halves(pair_ref[...])
    k_hi, k_lo = hi_ref[...], lo_ref[...]
    terms = dot(a_hi, k_hi) + dot(a_hi, k_lo) + dot(a_lo, k_hi)
    square = (256, 256)
    i, j = iota(square, 0), iota(square, 1)
    turn = (((i & 15) == (j >> 4)) & ((i >> 4) == (j & 15))).astype(F32).astype(BF16)
    t_hi, t_lo = halves(terms)
    table_hi_ref[:, :256] = t_hi
    table_lo_ref[:, :256] = t_lo
    table_hi_ref[:, 256:] = dot(t_hi, turn).astype(BF16)
    table_lo_ref[:, 256:] = dot(t_lo, turn).astype(BF16)
    modal = modal_ref[...]
    own = modal.shape[0]
    row = iota((own * G, G * S), 0)
    lane = iota((own * G, G * S), 1)
    spread = jnp.zeros((own * G, G * S), F32)
    for m in range(own):
        spread = jnp.where((row >> 5) == m, modal[m : m + 1, :], spread)
    spread = jnp.where((lane >> 4) == (row & 31), spread, 0.0)
    k, n = iota((G * S, 256), 0), iota((G * S, 256), 1)
    hi, lo = halves(spread)
    to_left = ((k & 15) == (n >> 4)).astype(F32).astype(BF16)
    to_right = ((k & 15) == (n & 15)).astype(F32).astype(BF16)
    left = dot(hi, to_left) + dot(lo, to_left)
    right = dot(hi, to_right) + dot(lo, to_right)
    integral_ref[...] = dot_exact(cosine_ref[...], left * right)


def fit_kernel(source_ref, hi_ref, lo_ref, first_ref, *refs):
    near_refs = list(refs[:NEAR])
    far_ref, energy_ref, rest_ref, sems, out_sems = refs[NEAR:]
    tiles = energy_ref.shape[0] // FIT_TILE
    out_refs = near_refs + [rest_ref.at[c] for c in range(KEEP - NEAR)]

    def copies(r):
        few = FIT_TILE // 4
        for k in range(4):
            rows = pl.ds(pl.multiple_of(r * FIT_TILE + k * few, few), few)
            yield pltpu.make_async_copy(source_ref.at[rows], energy_ref.at[rows], sems.at[r, k])

    def copy_out(r):
        rows = pl.ds(pl.multiple_of(r * FIT_TILE, FIT_TILE), FIT_TILE)
        return pltpu.make_async_copy(rest_ref.at[:, rows], far_ref.at[:, rows], out_sems.at[r])

    for r in range(2):
        for copy in copies(r):
            copy.start()

    def over_rows(r, carry):
        for copy in copies(r):
            copy.wait()

        @pl.when(r + 2 < tiles)
        def _():
            for copy in copies(r + 2):
                copy.start()

        fit_some(energy_ref, hi_ref, lo_ref, first_ref, out_refs, r * FIT_TILE)
        copy_out(r).start()
        return carry

    lax.fori_loop(0, tiles, over_rows, 0)
    for r in range(tiles):
        copy_out(r).wait()


def share_kernel(
    came_ref,
    hi_ref,
    lo_ref,
    source_ref,
    meta_ref,
    fit_in,
    wide_in,
    out_ref,
    known_ref,
    w1_ref,
    w23_ref,
    lead_ref,
    along_ref,
    energy_ref,
    fit_ref,
    wide_ref,
    sems,
    more_sems,
):
    tile = 16
    tables_in = [
        pltpu.make_async_copy(fit_in, fit_ref, more_sems.at[0]),
        pltpu.make_async_copy(wide_in, wide_ref, more_sems.at[1]),
    ]
    for part in tables_in:
        part.start()

    def copy(r):
        rows_r = pl.ds(pl.multiple_of(r * tile, tile), tile)
        return pltpu.make_async_copy(source_ref.at[rows_r], energy_ref.at[rows_r], sems.at[r])

    tiles, ahead = energy_ref.shape[0] // tile, 4
    for r in range(ahead):
        copy(r).start()
    peers = came_ref.shape[0]
    number = energy_ref.shape[0]
    rows = 3 * number
    asked = came_ref[:, 1, :].astype(BF16)
    per = float(rows // peers)
    at = iota((rows, 1), 0).astype(F32)
    peer = jnp.floor((at + 0.5) * (1.0 / per))
    rank = at - per * peer
    seen = dot(one_hot(peer, peers), asked)
    off = iota((rows, 128), 1).astype(F32) - rank
    local, small, large, other = (
        lane_sum(jnp.where(off == 16.0 * k, seen, 0.0)) for k in (0, 2, 3, 4)
    )
    slot = jnp.concatenate([meta_ref[:, 1:2], small, large, other], axis=0)
    pick = one_hot(slot, 128)
    ground = came_ref[:, 0, :]
    spots = 128 // peers
    ground = jnp.concatenate([pltpu.roll(ground, 128 - 32 * j, 1) if j else ground for j in range(spots)], axis=0)
    ground = jnp.where(iota((128, 128), 1) < 32, ground, 0.0)
    ground = ground + pltpu.roll(ground, 32, 1)
    ground = ground + pltpu.roll(ground, 64, 1)
    known = pick_two(pick, *halves(ground))
    known_ref[...] = known[:rows]
    k, n = iota((128, 256), 0), iota((128, 256), 1)
    widen = (k == (n >> 4)).astype(F32).astype(BF16)
    k, n = iota((256, 128), 0), iota((256, 128), 1)
    to_high = ((k >> 4) == n).astype(F32).astype(BF16)
    to_low = ((k & 15) == n).astype(F32).astype(BF16)

    def repeated(a):
        part = jnp.where((iota(a.shape, 1) & 31) < 16, a, 0.0)
        return part + pltpu.roll(part, 16, 1)

    def twice(a):
        return jnp.concatenate([a, a], axis=1)

    terms = pick_two(one_hot(local, 256), hi_ref[:, :256], lo_ref[:, :256])
    g_small, g_large, g_other = (known[p * rows : (p + 1) * rows] for p in (1, 2, 3))
    of_small = dot_two(terms * twice(repeated(g_large)), to_high)
    of_large = dot_two(terms * dot_two(g_small, widen), to_low)
    norm = g_other[:, 0:1]
    of_other = lane_sum(of_small * g_small)
    lane = iota((rows, 128), 1)
    shares = [-norm * of_small, -norm * of_large, jnp.where(lane == 0, -of_other, 0.0)]
    one, two, three = (known[p * number : (p + 1) * number] for p in range(3))
    cells = G * G
    for part in tables_in:
        part.wait()
    w1_ref[...] = jnp.broadcast_to(lane_sum(fit_ref[...] * one[0:1]), w1_ref.shape)
    ways = [wide_ref[p] for p in range(4)]

    def weights(a, hi, lo):
        a_hi, a_lo = halves(a[:, :32])
        return dot(a_hi, hi) + dot(a_hi, lo) + dot(a_lo, hi)

    w2 = weights(two, ways[0], ways[1])
    w3 = weights(three, ways[2], ways[3])
    w23_ref[...] = w2 * w3
    lanes = cells // 128

    def over_rows(r, carry):
        copy(r).wait()

        @pl.when(r + ahead < tiles)
        def _():
            copy(r + ahead).start()

        rows_r = pl.ds(pl.multiple_of(r * tile, tile), tile)
        w23 = [w23_ref[rows_r, k * 128 : (k + 1) * 128] for k in range(lanes)]

        def over_points(g, lead):
            x = energy_ref[rows_r, pl.ds(pl.multiple_of(g * cells, cells), cells)].astype(F32)
            w1 = w1_ref[pl.ds(g, 1), :]
            fresh, along = [], None
            for k in range(lanes):
                part = x[:, k * 128 : (k + 1) * 128]
                fresh.append(lead[k] + w1 * part)
                term = part * w23[k]
                along = term if along is None else along + term
            along_ref[g] += along
            return tuple(fresh)

        none = jnp.zeros((tile, 128), F32)
        lead = lax.fori_loop(0, G, over_points, (none,) * lanes, unroll=8)
        for k in range(lanes):
            lead_ref[rows_r, k * 128 : (k + 1) * 128] = lead[k]
        return carry

    along_ref[...] = jnp.zeros_like(along_ref)
    lax.fori_loop(0, tiles, over_rows, 0)

    def back(a, hi, lo):
        a_hi, a_lo = halves(a)
        dims = (((1,), (1,)), ((), ()))
        total = lax.dot_general(a_hi, hi, dims, preferred_element_type=F32)
        total = total + lax.dot_general(a_hi, lo, dims, preferred_element_type=F32)
        total = total + lax.dot_general(a_lo, hi, dims, preferred_element_type=F32)
        return jnp.concatenate([total, jnp.zeros((number, 96), F32)], axis=1)

    sums = lane_sum(jnp.sum(along_ref[...], axis=1))
    field_first = jnp.sum(sums * fit_ref[...], axis=0, keepdims=True)
    field_first = jnp.where(iota((number, 128), 0) == 0, field_first, 0.0)
    field_second = back(lead_ref[...] * w3, ways[0], ways[1])
    field_third = back(lead_ref[...] * w2, ways[2], ways[3])
    own = known[:rows]
    lane = iota((rows, 128), 1)
    single = jnp.where(lane < 16, pltpu.roll(own, 112, 1), 0.0)
    along = lane_sum(single * own)
    norms = own[:, 0:1]
    n1, n2, n3 = (norms[p * number : (p + 1) * number] for p in range(3))
    q1, q2, q3 = (along[p * number : (p + 1) * number] for p in range(3))
    scale = jnp.concatenate([n2 * n3, n1 * n3, n1 * n2], axis=0)
    shift = jnp.concatenate([n3 * q2 + n2 * q3, n3 * q1 + n1 * q3, n2 * q1 + n1 * q2], axis=0)
    from_grid = jnp.concatenate([field_first, field_second, field_third], axis=0)
    from_grid = from_grid - scale * single - jnp.where(lane == 0, shift, 0.0)
    fields = jnp.concatenate([from_grid] + shares, axis=0)
    f_hi, f_lo = halves(fields)
    dims = (((0,), (0,)), ((), ()))
    part = lax.dot_general(pick, f_hi, dims, preferred_element_type=F32) + lax.dot_general(
        pick, f_lo, dims, preferred_element_type=F32
    )
    part = part[:peers] + sum(
        pltpu.roll(part[j * peers : (j + 1) * peers], 16 * j, 1) for j in range(1, spots)
    )
    slots = out_ref.shape[0]
    each = float(slots // peers)
    at = iota((slots, 1), 0).astype(F32)
    peer = jnp.floor((at + 0.5) * (1.0 / each))
    rest = at - each * peer
    late = rest >= per
    rank = rest - jnp.where(late, per, 0.0)
    from_peer = one_hot(peer, peers)
    seen = dot(from_peer, asked)
    off = iota((slots, 128), 1).astype(F32) - rank
    local = lane_sum(jnp.where(off == 0.0, seen, 0.0))
    turned = lane_sum(jnp.where(off == 16.0, seen, 0.0))
    terms = pick_two(one_hot(local, 256), hi_ref[...], lo_ref[...])
    terms = jnp.where(turned > 0.5, terms[:, 256:], terms[:, :256])
    terms = jnp.where(late, terms[:, 128:], terms[:, :128])
    p_hi, p_lo = halves(part)
    out_ref[...] = jnp.where(rest == 2.0 * per, pick_two(from_peer, p_hi, p_lo), terms)


def own_kernel(came_ref, out_ref):
    peers = came_ref.shape[0] // 25
    each = 25
    rows = came_ref[pl.ds(each - 1, peers, stride=each), :]
    out_ref[...] = jnp.sum(rows, axis=0, keepdims=True)


def face_kernel(*refs):
    far_ref, came_ref, known_ref, meta_ref, far_out, energy_ref, coef_ref, rest_ref, out_sems, sem = refs[NEAR:]
    fit_refs = list(refs[:NEAR]) + [rest_ref.at[c] for c in range(KEEP - NEAR)]
    coming = pltpu.make_async_copy(far_ref, rest_ref, sem)
    coming.start()
    number = coef_ref.shape[0]
    some = 4
    leaving = []
    for k in range(KEEP // some):
        cols = slice(k * some * 256, (k + 1) * some * 256)
        leaving.append(pltpu.make_async_copy(coef_ref.at[:, cols], far_out.at[:, cols], out_sems.at[k]))
    place = meta_ref[:, 0:1]
    known = known_ref[...]
    one, two, three = (known[p * number : (p + 1) * number] for p in range(3))
    hi, lo = halves(came_ref[...])
    slots = came_ref.shape[0]
    got = [pick_two(one_hot(place + 12.0 * h, slots), hi, lo) for h in range(2)]
    lane = iota((number, 128), 1)
    k, n = iota((128, 256), 0), iota((128, 256), 1)
    two_wide = dot_two(two, (k == (n >> 4)).astype(F32).astype(BF16))
    two_single = dot_two(two, ((k == (n >> 4) + 16) & ((n & 15) == 0)).astype(F32).astype(BF16))
    three_low = jnp.where((lane & 31) < 16, three, 0.0)
    three_wide = three_low + pltpu.roll(three_low, 16, 1)
    start = lane < 16
    first_pair = [g[:number] for g in got]
    first_pair[0] = first_pair[0] + jnp.where(start, pltpu.roll(one, 112, 1), 0.0)
    second_pair = [g[number : 2 * number] for g in got]
    third_pair = [g[2 * number :] for g in got]
    third_pair[0] = third_pair[0] + jnp.where(start, pltpu.roll(three, 112, 1), 0.0)
    third_pair = [t + two_single[:, h * 128 : (h + 1) * 128] for h, t in enumerate(third_pair)]
    both = [two_wide[:, h * 128 : (h + 1) * 128] * three_wide for h in range(2)]
    spaced = (lane & 15) == 0
    energy = jnp.zeros((number, 128), F32)
    for c in range(KEEP):
        if c == NEAR:
            coming.wait()
        along = jnp.zeros((number, 128), F32)
        for h in range(2):
            moved = pltpu.roll(first_pair[h], 128 - c, 1) if c else first_pair[h]
            value = fit_refs[c][:, h * 128 : (h + 1) * 128] - jnp.where(spaced, moved, 0.0)
            if h == 0:
                shift = (c % 8) * 16
                moved = second_pair[c // 8]
                moved = pltpu.roll(moved, 128 - shift, 1) if shift else moved
                value = value - jnp.where(start, moved, 0.0)
            if c == 0:
                value = value - third_pair[h]
            coef_ref[:, c * 256 + h * 128 : c * 256 + (h + 1) * 128] = value.astype(BF16)
            along = along + value * both[h]
        energy = energy + one[:, c : c + 1] * along
        if c % some == some - 1:
            leaving[c // some].start()
    energy_ref[...] = lax.dot_general(
        jnp.full((8, 128), 1.0, F32), energy, (((1,), (1,)), ((), ())), preferred_element_type=F32, precision=HIGHEST
    )[0:1]
    for copy in leaving:
        copy.wait()


def integral_kernel(*refs):
    *parts, integral_ref, out_ref = refs
    parts = [p[...] for p in parts]
    while len(parts) > 1:
        parts = [parts[i] + parts[i + 1] for i in range(0, len(parts), 2)]
    shape = (out_ref.shape[0], 128)
    total = jnp.where((iota(shape, 1) >> 4) == iota(shape, 0), parts[0], 0.0)
    out_ref[...] = dot_exact(total, integral_ref[...])


def call(kernel, outs, *args, name, apart=(), fetched=(), outs_apart=(), flops=0, scratch=()):
    moved = sum(int(np.prod(a.shape)) * a.dtype.itemsize for a in args) + sum(
        int(np.prod(o.shape)) * o.dtype.itemsize for o in outs
    )
    count = len(args) + len(outs) + len(scratch)
    pieces = {i: 4 if args[i].size * args[i].dtype.itemsize >= 2**18 else 1 for i in fetched}

    def fetching(*refs):
        refs, held, sems = list(refs[:count]), refs[count:-1], refs[-1]
        copies = []
        for i, buffer in zip(fetched, held, strict=True):
            rows = args[i].shape[0] // pieces[i]
            for k in range(pieces[i]):
                some = slice(k * rows, (k + 1) * rows)
                ends = (refs[i].at[some], buffer.at[some]) if pieces[i] > 1 else (refs[i], buffer)
                copies.append(pltpu.make_async_copy(*ends, sems.at[len(copies)]))
        for copy in copies:
            copy.start()
        for copy in copies:
            copy.wait()
        for i, buffer in zip(fetched, held, strict=True):
            refs[i] = buffer
        kernel(*refs)

    extra = []
    if fetched:
        extra = [pltpu.VMEM(args[i].shape, args[i].dtype) for i in fetched]
        extra.append(pltpu.SemaphoreType.DMA((sum(pieces.values()),)))
    outside = set(apart) | set(fetched)
    return pl.pallas_call(
        fetching if fetched else kernel,
        out_shape=outs,
        in_specs=[
            pl.BlockSpec(memory_space=pltpu.HBM if i in outside else pltpu.VMEM) for i in range(len(args))
        ],
        out_specs=[
            pl.BlockSpec(memory_space=pltpu.HBM if i in outs_apart else pltpu.VMEM) for i in range(len(outs))
        ],
        scratch_shapes=list(scratch) + extra,
        compiler_params=pltpu.CompilerParams(vmem_limit_bytes=VMEM_LIMIT),
        cost_estimate=pl.CostEstimate(flops=flops, bytes_accessed=moved, transcendentals=0),
        name=name,
    )(*(far(a) if i in outside else a for i, a in enumerate(args)))


def across(a, k):
    return lax.ppermute(a, "grp", [(i, i ^ k) for i in range(lax.axis_size("grp"))])


def far(a):
    return pltpu.with_memory_space_constraint(a, pltpu.HBM)


def shaped(shape, dtype=F32):
    return jax.ShapeDtypeStruct(shape, dtype)


def body(energies, triples, pair_surfaces, pair_slot, single_surfaces, modals, mode_slot):
    devices = lax.axis_size("dev")
    groups = lax.axis_size("grp")
    number = triples.shape[0]
    own = modals.shape[0]
    capacity = 3 * number // devices
    cos_wide = np.zeros((G, 128), np.float32)
    fit_wide = np.zeros((G, 128), np.float32)
    cos_block = np.zeros((128, own * G), np.float32)
    for m in range(own):
        cos_wide[:, m * 32 : m * 32 + KEEP] = COSINES.T
        fit_wide[:, m * 32 + KEEP : m * 32 + 2 * KEEP] = FITTER.T
        cos_block[m * KEEP : (m + 1) * KEEP, m * G : (m + 1) * G] = COSINES
    kron = np.einsum("dh,el->hlde", FITTER, FITTER).reshape(G * G, KEEP * KEEP)
    hi, lo = (jnp.asarray(x) for x in halves_np(kron))
    fit_rows = np.zeros((G, 128), np.float32)
    fit_rows[:, :KEEP] = FITTER.T
    wide = np.zeros((2, 32, G, G))
    wide[0, :KEEP] = FITTER[:, :, None]
    wide[1, :KEEP] = FITTER[:, None, :]
    wide = jnp.asarray(np.stack([h[p] for p in range(2) for h in halves_np(wide.reshape(2, 32, G * G))]))
    send, meta = call(
        ask_kernel,
        [shaped((devices, 2, 128)), shaped((3 * number, 128))],
        triples.T,
        pair_slot,
        mode_slot.reshape(1, -1),
        modals,
        single_surfaces,
        jnp.asarray(cos_wide),
        jnp.asarray(fit_wide),
        fetched=tuple(range(7)),
        name="ask",
    )
    came = lax.all_to_all(send, "dev", 0, 0, tiled=True)
    table = shaped((pair_surfaces.shape[0], 512), BF16)
    first_hi, first_lo = halves_np(np.kron(FITTER, np.eye(8)))
    first = jnp.asarray(np.concatenate([first_hi, first_lo], axis=0))
    table_hi, table_lo, integral = call(
        table_kernel,
        [table, table, shaped((128, S * S))],
        pair_surfaces,
        hi,
        lo,
        modals,
        jnp.asarray(cos_block),
        fetched=(0, 1, 2, 3, 4),
        name="table",
        flops=5 * 10**8,
    )
    each = 2 * capacity + 1
    answer, known = call(
        share_kernel,
        [shaped((devices * each, 128)), shaped((3 * number, 128))],
        came,
        table_hi,
        table_lo,
        energies,
        meta,
        jnp.asarray(fit_rows),
        wide,
        apart=(3, 5, 6),
        name="share",
        flops=10**9,
        scratch=[
            pltpu.VMEM((G, 128), F32),
            pltpu.VMEM((number, G * G), F32),
            pltpu.VMEM((number, G * G), F32),
            pltpu.VMEM((G, 16, 128), F32),
            pltpu.VMEM(energies.shape, BF16),
            pltpu.VMEM(fit_rows.shape, F32),
            pltpu.VMEM(wide.shape, BF16),
            pltpu.SemaphoreType.DMA((number // 16,)),
            pltpu.SemaphoreType.DMA((2,)),
        ],
    )
    terms = lax.all_to_all(
        answer.reshape(devices, each, 1, 128), "dev", 0, 0, tiled=True
    ).reshape(devices * each, 128)
    far_part = (KEEP - NEAR, number, KEEP**2)
    fitted = call(
        fit_kernel,
        [shaped((number, KEEP**2))] * NEAR + [pltpu.HBM(far_part, F32)],
        energies,
        hi,
        lo,
        first,
        apart=(0,),
        outs_apart=(NEAR,),
        scratch=[
            pltpu.VMEM(energies.shape, BF16),
            pltpu.VMEM(far_part, F32),
            pltpu.SemaphoreType.DMA((number // FIT_TILE, 4)),
            pltpu.SemaphoreType.DMA((number // FIT_TILE,)),
        ],
        name="fit",
        flops=5 * 10**9,
    )
    terms, fitted = lax.optimization_barrier((terms, fitted))
    (mine,) = call(own_kernel, [shaped((1, 128))], terms, name="own")
    mine = mine + across(mine, 1)
    parts = [mine] + [across(mine, k) for k in range(2, groups, 2)]
    mine, known = lax.optimization_barrier((mine, known))
    coefficients, energy = call(
        face_kernel,
        [pltpu.HBM((number, KEEP**3), BF16), shaped((1, number))],
        *fitted,
        terms,
        known,
        meta,
        apart=(NEAR,),
        outs_apart=(0,),
        scratch=[
            pltpu.VMEM((number, KEEP**3), BF16),
            pltpu.VMEM(far_part, F32),
            pltpu.SemaphoreType.DMA((4,)),
            pltpu.SemaphoreType.DMA,
        ],
        name="faces",
        flops=10**9,
    )
    (mean_field,) = call(
        integral_kernel,
        [shaped((own, S * S))],
        *parts,
        integral,
        name="integrals",
    )
    return coefficients, energy.reshape(number), mean_field


def solution(mesh):
    in_specs = (
        P(("grp", "dev"), None),
        P(("grp", "dev"), None),
        P("dev", None),
        P(),
        P("dev", None),
        P("dev", None),
        P(),
    )
    out_specs = (P(("grp", "dev"), None), P(("grp", "dev")), P("dev", None))
    return jax.shard_map(body, mesh=mesh, in_specs=in_specs, out_specs=out_specs, check_vma=False)
```

```python
import numpy as np
import jax
import jax.numpy as jnp
from jax import lax
from jax.experimental import pallas as pl
from jax.experimental.pallas import tpu as pltpu
from jax.sharding import PartitionSpec as P

G = 32
KEEP = 16
S = 16
F32 = jnp.float32
BF16 = jnp.bfloat16
HIGHEST = lax.Precision.HIGHEST
VMEM_LIMIT = 24 * 2**20


def tables():
    orders = np.arange(KEEP, dtype=np.float64)
    points = np.arange(G, dtype=np.float64) + 0.5
    cosines = np.cos(np.pi * orders[:, None] * points[None, :] / G)
    weights = np.where(orders == 0, 1.0, 2.0) / G
    return cosines, weights[:, None] * cosines


COSINES, FITTER = tables()


def halves(a):
    hi = a.astype(BF16)
    return hi, (a - hi.astype(F32)).astype(BF16)


def halves_np(a):
    a = a.astype(np.float32)
    hi = a.astype(jnp.bfloat16)
    return hi, (a - hi.astype(np.float32)).astype(jnp.bfloat16)


def dot(a, b):
    return jnp.dot(a, b, preferred_element_type=F32)


def dot_exact(a, b):
    return jnp.dot(a, b, preferred_element_type=F32, precision=HIGHEST)


def iota(shape, dim):
    return lax.broadcasted_iota(jnp.int32, shape, dim)


def lane_sum(a):
    return jnp.sum(a, axis=1, keepdims=True)


def column(row):
    n = row.shape[1]
    return lane_sum(jnp.where(iota((n, n), 0) == iota((n, n), 1), row, 0.0))


def one_hot(column_f, width):
    return (iota((column_f.shape[0], width), 1).astype(F32) == column_f).astype(F32).astype(BF16)


def dot_two(a, b):
    hi, lo = halves(a)
    return dot(hi, b) + dot(lo, b)


def pick_two(pick, hi, lo):
    return dot(pick, hi) + dot(pick, lo)


def ask_kernel(tri_ref, pair_ref, slot_ref, modal_ref, single_ref, cos_ref, fit_ref, out_ref, meta_ref):
    modes = slot_ref.shape[1]
    tri = tri_ref[...].astype(F32)
    first, second, third = (column(tri[p : p + 1]) for p in range(3))
    lower = jnp.concatenate([first, first, second], axis=0)
    upper = jnp.concatenate([second, third, third], axis=0)
    each = jnp.concatenate([first, second, third], axis=0)
    rows = lower.shape[0]
    number = rows // 3
    lane = iota((rows, modes), 1).astype(F32)
    pair = pair_ref[...]
    high = (pair >> 8).astype(F32).astype(BF16)
    low = (pair & 255).astype(F32).astype(BF16)
    pick = (lane == lower).astype(F32).astype(BF16)
    at = lane == upper
    owner = lane_sum(jnp.where(at, dot(pick, high), 0.0))
    local = lane_sum(jnp.where(at, dot(pick, low), 0.0))
    slots = slot_ref[...]
    slots = ((slots & 3) * 32 + (slots >> 2)).astype(F32)
    slot = lane_sum(jnp.where(lane == each, slots, 0.0))
    wide = iota((rows, 128), 1)
    wide_f = wide.astype(F32)
    hit = wide_f == owner
    hit_b = hit.astype(F32).astype(BF16)
    earlier = (iota((rows, rows), 1) < iota((rows, rows), 0)).astype(F32).astype(BF16)
    rank = lane_sum(jnp.where(hit, dot(earlier, hit_b), 0.0))
    ordered = lower < upper
    is_first = iota((rows, 1), 0) < number
    turned = jnp.where(is_first, ordered.astype(F32), 1.0 - ordered.astype(F32))
    s1, s2, s3 = (slot[p * number : (p + 1) * number] for p in range(3))
    left = jnp.concatenate([s1, s1, s2], axis=0)
    right = jnp.concatenate([s2, s3, s3], axis=0)
    other = jnp.concatenate([s3, s2, s1], axis=0)
    small = jnp.where(ordered, left, right)
    large = jnp.where(ordered, right, left)
    off = wide_f - rank
    said = jnp.where(off == 0.0, local, 0.0)
    for k, value in enumerate((turned, small, large, other)):
        said = said + jnp.where(off == 16.0 * (k + 1), value, 0.0)
    asked = lax.dot_general(hit_b, said.astype(BF16), (((0,), (0,)), ((), ())), preferred_element_type=F32)
    square = modal_ref[...] * modal_ref[...]
    spread = jnp.broadcast_to(cos_ref[...][:, None, :], (G, S, 128)).reshape(G * S, 128)
    spread = jnp.where((iota((G * S, 128), 0) & 15) == 0, spread, 0.0)
    mine = dot_exact(square, spread) + dot_exact(single_ref[...], fit_ref[...])
    four = mine.shape
    mine = jnp.sum(jnp.where((iota(four, 1) >> 5) == iota(four, 0), mine, 0.0), axis=0, keepdims=True)
    peers = out_ref.shape[0]
    out_ref[:, 0, :] = jnp.broadcast_to(mine, (peers, 128))
    out_ref[:, 1, :] = asked[:peers]
    meta_ref[...] = jnp.where(wide == 0, owner * 25.0 + rank, jnp.where(wide == 1, slot, 0.0))


FIT_TILE = 32
NEAR = 10


def fit_some(energy_ref, hi_ref, lo_ref, first_ref, out_refs, start):
    cells = G * G
    few = 8
    rows = pl.ds(pl.multiple_of(start, FIT_TILE), FIT_TILE)
    stacked = jnp.concatenate([energy_ref[rows, g * cells : (g + 1) * cells] for g in range(G)], axis=0)
    two = dot(stacked, hi_ref[...]) + dot(stacked, lo_ref[...])
    half = first_ref.shape[0] // 2
    for h in range(FIT_TILE // few):
        at = h * few
        part = jnp.concatenate(
            [two[g * FIT_TILE + at : g * FIT_TILE + at + few] for g in range(G)], axis=0
        )
        p_hi, p_lo = halves(part)
        large = dot(first_ref[...], p_hi)
        all_three = large[:half] + large[half:] + dot(first_ref[:half], p_lo)
        some = pl.ds(pl.multiple_of(start + at, few), few)
        for c in range(KEEP):
            out_refs[c][some, :] = all_three[c * few : (c + 1) * few]


def table_kernel(
    pair_ref,
    hi_ref,
    lo_ref,
    modal_ref,
    cosine_ref,
    table_hi_ref,
    table_lo_ref,
    integral_ref,
):
    a_hi, a_lo = halves(pair_ref[...])
    k_hi, k_lo = hi_ref[...], lo_ref[...]
    terms = dot(a_hi, k_hi) + dot(a_hi, k_lo) + dot(a_lo, k_hi)
    square = (256, 256)
    i, j = iota(square, 0), iota(square, 1)
    turn = (((i & 15) == (j >> 4)) & ((i >> 4) == (j & 15))).astype(F32).astype(BF16)
    t_hi, t_lo = halves(terms)
    table_hi_ref[:, :256] = t_hi
    table_lo_ref[:, :256] = t_lo
    table_hi_ref[:, 256:] = dot(t_hi, turn).astype(BF16)
    table_lo_ref[:, 256:] = dot(t_lo, turn).astype(BF16)
    modal = modal_ref[...]
    own = modal.shape[0]
    row = iota((own * G, G * S), 0)
    lane = iota((own * G, G * S), 1)
    spread = jnp.zeros((own * G, G * S), F32)
    for m in range(own):
        spread = jnp.where((row >> 5) == m, modal[m : m + 1, :], spread)
    spread = jnp.where((lane >> 4) == (row & 31), spread, 0.0)
    k, n = iota((G * S, 256), 0), iota((G * S, 256), 1)
    hi, lo = halves(spread)
    to_left = ((k & 15) == (n >> 4)).astype(F32).astype(BF16)
    to_right = ((k & 15) == (n & 15)).astype(F32).astype(BF16)
    left = dot(hi, to_left) + dot(lo, to_left)
    right = dot(hi, to_right) + dot(lo, to_right)
    integral_ref[...] = dot_exact(cosine_ref[...], left * right)


def fit_kernel(source_ref, hi_ref, lo_ref, first_ref, *refs):
    near_refs = list(refs[:NEAR])
    far_ref, energy_ref, rest_ref, sems, out_sems = refs[NEAR:]
    tiles = energy_ref.shape[0] // FIT_TILE
    out_refs = near_refs + [rest_ref.at[c] for c in range(KEEP - NEAR)]

    def copies(r):
        few = FIT_TILE // 4
        for k in range(4):
            rows = pl.ds(pl.multiple_of(r * FIT_TILE + k * few, few), few)
            yield pltpu.make_async_copy(source_ref.at[rows], energy_ref.at[rows], sems.at[r, k])

    def copy_out(r):
        rows = pl.ds(pl.multiple_of(r * FIT_TILE, FIT_TILE), FIT_TILE)
        return pltpu.make_async_copy(rest_ref.at[:, rows], far_ref.at[:, rows], out_sems.at[r])

    for r in range(2):
        for copy in copies(r):
            copy.start()

    def over_rows(r, carry):
        for copy in copies(r):
            copy.wait()

        @pl.when(r + 2 < tiles)
        def _():
            for copy in copies(r + 2):
                copy.start()

        fit_some(energy_ref, hi_ref, lo_ref, first_ref, out_refs, r * FIT_TILE)
        copy_out(r).start()
        return carry

    lax.fori_loop(0, tiles, over_rows, 0)
    for r in range(tiles):
        copy_out(r).wait()


def share_kernel(
    came_ref,
    hi_ref,
    lo_ref,
    source_ref,
    meta_ref,
    fit_in,
    wide_in,
    out_ref,
    known_ref,
    w1_ref,
    w23_ref,
    lead_ref,
    along_ref,
    energy_ref,
    fit_ref,
    wide_ref,
    sems,
    more_sems,
):
    tile = 16
    tables_in = [
        pltpu.make_async_copy(fit_in, fit_ref, more_sems.at[0]),
        pltpu.make_async_copy(wide_in, wide_ref, more_sems.at[1]),
    ]
    for part in tables_in:
        part.start()

    def copy(r):
        rows_r = pl.ds(pl.multiple_of(r * tile, tile), tile)
        return pltpu.make_async_copy(source_ref.at[rows_r], energy_ref.at[rows_r], sems.at[r])

    tiles, ahead = energy_ref.shape[0] // tile, 4
    for r in range(ahead):
        copy(r).start()
    peers = came_ref.shape[0]
    number = energy_ref.shape[0]
    rows = 3 * number
    asked = came_ref[:, 1, :].astype(BF16)
    per = float(rows // peers)
    at = iota((rows, 1), 0).astype(F32)
    peer = jnp.floor((at + 0.5) * (1.0 / per))
    rank = at - per * peer
    seen = dot(one_hot(peer, peers), asked)
    off = iota((rows, 128), 1).astype(F32) - rank
    local, small, large, other = (
        lane_sum(jnp.where(off == 16.0 * k, seen, 0.0)) for k in (0, 2, 3, 4)
    )
    slot = jnp.concatenate([meta_ref[:, 1:2], small, large, other], axis=0)
    pick = one_hot(slot, 128)
    ground = came_ref[:, 0, :]
    spots = 128 // peers
    ground = jnp.concatenate([pltpu.roll(ground, 128 - 32 * j, 1) if j else ground for j in range(spots)], axis=0)
    ground = jnp.where(iota((128, 128), 1) < 32, ground, 0.0)
    ground = ground + pltpu.roll(ground, 32, 1)
    ground = ground + pltpu.roll(ground, 64, 1)
    known = pick_two(pick, *halves(ground))
    known_ref[...] = known[:rows]
    k, n = iota((128, 256), 0), iota((128, 256), 1)
    widen = (k == (n >> 4)).astype(F32).astype(BF16)
    k, n = iota((256, 128), 0), iota((256, 128), 1)
    to_high = ((k >> 4) == n).astype(F32).astype(BF16)
    to_low = ((k & 15) == n).astype(F32).astype(BF16)

    def repeated(a):
        part = jnp.where((iota(a.shape, 1) & 31) < 16, a, 0.0)
        return part + pltpu.roll(part, 16, 1)

    def twice(a):
        return jnp.concatenate([a, a], axis=1)

    terms = pick_two(one_hot(local, 256), hi_ref[:, :256], lo_ref[:, :256])
    g_small, g_large, g_other = (known[p * rows : (p + 1) * rows] for p in (1, 2, 3))
    of_small = dot_two(terms * twice(repeated(g_large)), to_high)
    of_large = dot_two(terms * dot_two(g_small, widen), to_low)
    norm = g_other[:, 0:1]
    of_other = lane_sum(of_small * g_small)
    lane = iota((rows, 128), 1)
    shares = [-norm * of_small, -norm * of_large, jnp.where(lane == 0, -of_other, 0.0)]
    one, two, three = (known[p * number : (p + 1) * number] for p in range(3))
    cells = G * G
    for part in tables_in:
        part.wait()
    w1_ref[...] = jnp.broadcast_to(lane_sum(fit_ref[...] * one[0:1]), w1_ref.shape)
    ways = [wide_ref[p] for p in range(4)]

    def weights(a, hi, lo):
        a_hi, a_lo = halves(a[:, :32])
        return dot(a_hi, hi) + dot(a_hi, lo) + dot(a_lo, hi)

    w2 = weights(two, ways[0], ways[1])
    w3 = weights(three, ways[2], ways[3])
    w23_ref[...] = w2 * w3
    lanes = cells // 128

    def over_rows(r, carry):
        copy(r).wait()

        @pl.when(r + ahead < tiles)
        def _():
            copy(r + ahead).start()

        rows_r = pl.ds(pl.multiple_of(r * tile, tile), tile)
        w23 = [w23_ref[rows_r, k * 128 : (k + 1) * 128] for k in range(lanes)]

        def over_points(g, lead):
            x = energy_ref[rows_r, pl.ds(pl.multiple_of(g * cells, cells), cells)].astype(F32)
            w1 = w1_ref[pl.ds(g, 1), :]
            fresh, along = [], None
            for k in range(lanes):
                part = x[:, k * 128 : (k + 1) * 128]
                fresh.append(lead[k] + w1 * part)
                term = part * w23[k]
                along = term if along is None else along + term
            along_ref[g] += along
            return tuple(fresh)

        none = jnp.zeros((tile, 128), F32)
        lead = lax.fori_loop(0, G, over_points, (none,) * lanes, unroll=16)
        for k in range(lanes):
            lead_ref[rows_r, k * 128 : (k + 1) * 128] = lead[k]
        return carry

    along_ref[...] = jnp.zeros_like(along_ref)
    lax.fori_loop(0, tiles, over_rows, 0)

    def back(a, hi, lo):
        a_hi, a_lo = halves(a)
        dims = (((1,), (1,)), ((), ()))
        total = lax.dot_general(a_hi, hi, dims, preferred_element_type=F32)
        total = total + lax.dot_general(a_hi, lo, dims, preferred_element_type=F32)
        total = total + lax.dot_general(a_lo, hi, dims, preferred_element_type=F32)
        return jnp.concatenate([total, jnp.zeros((number, 96), F32)], axis=1)

    sums = lane_sum(jnp.sum(along_ref[...], axis=1))
    field_first = jnp.sum(sums * fit_ref[...], axis=0, keepdims=True)
    field_first = jnp.where(iota((number, 128), 0) == 0, field_first, 0.0)
    field_second = back(lead_ref[...] * w3, ways[0], ways[1])
    field_third = back(lead_ref[...] * w2, ways[2], ways[3])
    own = known[:rows]
    lane = iota((rows, 128), 1)
    single = jnp.where(lane < 16, pltpu.roll(own, 112, 1), 0.0)
    along = lane_sum(single * own)
    norms = own[:, 0:1]
    n1, n2, n3 = (norms[p * number : (p + 1) * number] for p in range(3))
    q1, q2, q3 = (along[p * number : (p + 1) * number] for p in range(3))
    scale = jnp.concatenate([n2 * n3, n1 * n3, n1 * n2], axis=0)
    shift = jnp.concatenate([n3 * q2 + n2 * q3, n3 * q1 + n1 * q3, n2 * q1 + n1 * q2], axis=0)
    from_grid = jnp.concatenate([field_first, field_second, field_third], axis=0)
    from_grid = from_grid - scale * single - jnp.where(lane == 0, shift, 0.0)
    fields = jnp.concatenate([from_grid] + shares, axis=0)
    f_hi, f_lo = halves(fields)
    dims = (((0,), (0,)), ((), ()))
    part = lax.dot_general(pick, f_hi, dims, preferred_element_type=F32) + lax.dot_general(
        pick, f_lo, dims, preferred_element_type=F32
    )
    part = part[:peers] + sum(
        pltpu.roll(part[j * peers : (j + 1) * peers], 16 * j, 1) for j in range(1, spots)
    )
    slots = out_ref.shape[0]
    each = float(slots // peers)
    at = iota((slots, 1), 0).astype(F32)
    peer = jnp.floor((at + 0.5) * (1.0 / each))
    rest = at - each * peer
    late = rest >= per
    rank = rest - jnp.where(late, per, 0.0)
    from_peer = one_hot(peer, peers)
    seen = dot(from_peer, asked)
    off = iota((slots, 128), 1).astype(F32) - rank
    local = lane_sum(jnp.where(off == 0.0, seen, 0.0))
    turned = lane_sum(jnp.where(off == 16.0, seen, 0.0))
    terms = pick_two(one_hot(local, 256), hi_ref[...], lo_ref[...])
    terms = jnp.where(turned > 0.5, terms[:, 256:], terms[:, :256])
    terms = jnp.where(late, terms[:, 128:], terms[:, :128])
    p_hi, p_lo = halves(part)
    out_ref[...] = jnp.where(rest == 2.0 * per, pick_two(from_peer, p_hi, p_lo), terms)


def own_kernel(came_ref, out_ref):
    peers = came_ref.shape[0] // 25
    each = 25
    rows = came_ref[pl.ds(each - 1, peers, stride=each), :]
    out_ref[...] = jnp.sum(rows, axis=0, keepdims=True)


def gather_kernel(came_ref, meta_ref, out_ref):
    place = meta_ref[:, 0:1]
    hi, lo = halves(came_ref[...])
    slots = came_ref.shape[0]
    for h in range(2):
        out_ref[:, h * 128 : (h + 1) * 128] = pick_two(one_hot(place + 12.0 * h, slots), hi, lo)


def face_kernel(*refs):
    far_ref, got_ref, known_ref, far_out, energy_ref, coef_ref, rest_ref, out_sems, sem = refs[NEAR:]
    fit_refs = list(refs[:NEAR]) + [rest_ref.at[c] for c in range(KEEP - NEAR)]
    coming = pltpu.make_async_copy(far_ref, rest_ref, sem)
    coming.start()
    number = coef_ref.shape[0]
    some = 4
    leaving = []
    for k in range(KEEP // some):
        cols = slice(k * some * 256, (k + 1) * some * 256)
        leaving.append(pltpu.make_async_copy(coef_ref.at[:, cols], far_out.at[:, cols], out_sems.at[k]))
    known = known_ref[...]
    one, two, three = (known[p * number : (p + 1) * number] for p in range(3))
    got = [got_ref[:, h * 128 : (h + 1) * 128] for h in range(2)]
    lane = iota((number, 128), 1)
    k, n = iota((128, 256), 0), iota((128, 256), 1)
    two_wide = dot_two(two, (k == (n >> 4)).astype(F32).astype(BF16))
    two_single = dot_two(two, ((k == (n >> 4) + 16) & ((n & 15) == 0)).astype(F32).astype(BF16))
    three_low = jnp.where((lane & 31) < 16, three, 0.0)
    three_wide = three_low + pltpu.roll(three_low, 16, 1)
    start = lane < 16
    first_pair = [g[:number] for g in got]
    first_pair[0] = first_pair[0] + jnp.where(start, pltpu.roll(one, 112, 1), 0.0)
    second_pair = [g[number : 2 * number] for g in got]
    third_pair = [g[2 * number :] for g in got]
    third_pair[0] = third_pair[0] + jnp.where(start, pltpu.roll(three, 112, 1), 0.0)
    third_pair = [t + two_single[:, h * 128 : (h + 1) * 128] for h, t in enumerate(third_pair)]
    both = [two_wide[:, h * 128 : (h + 1) * 128] * three_wide for h in range(2)]
    spaced = (lane & 15) == 0
    energy = jnp.zeros((number, 128), F32)
    for c in range(KEEP):
        if c == NEAR:
            coming.wait()
        along = jnp.zeros((number, 128), F32)
        for h in range(2):
            moved = pltpu.roll(first_pair[h], 128 - c, 1) if c else first_pair[h]
            value = fit_refs[c][:, h * 128 : (h + 1) * 128] - jnp.where(spaced, moved, 0.0)
            if h == 0:
                shift = (c % 8) * 16
                moved = second_pair[c // 8]
                moved = pltpu.roll(moved, 128 - shift, 1) if shift else moved
                value = value - jnp.where(start, moved, 0.0)
            if c == 0:
                value = value - third_pair[h]
            coef_ref[:, c * 256 + h * 128 : c * 256 + (h + 1) * 128] = value.astype(BF16)
            along = along + value * both[h]
        energy = energy + one[:, c : c + 1] * along
        if c % some == some - 1:
            leaving[c // some].start()
    energy_ref[...] = lax.dot_general(
        jnp.full((8, 128), 1.0, F32), energy, (((1,), (1,)), ((), ())), preferred_element_type=F32, precision=HIGHEST
    )[0:1]
    for copy in leaving:
        copy.wait()


def integral_kernel(*refs):
    *parts, integral_ref, out_ref = refs
    parts = [p[...] for p in parts]
    while len(parts) > 1:
        parts = [parts[i] + parts[i + 1] for i in range(0, len(parts), 2)]
    shape = (out_ref.shape[0], 128)
    total = jnp.where((iota(shape, 1) >> 4) == iota(shape, 0), parts[0], 0.0)
    out_ref[...] = dot_exact(total, integral_ref[...])


def call(kernel, outs, *args, name, apart=(), fetched=(), outs_apart=(), flops=0, scratch=()):
    moved = sum(int(np.prod(a.shape)) * a.dtype.itemsize for a in args) + sum(
        int(np.prod(o.shape)) * o.dtype.itemsize for o in outs
    )
    count = len(args) + len(outs) + len(scratch)
    pieces = {i: 4 if args[i].size * args[i].dtype.itemsize >= 2**18 else 1 for i in fetched}

    def fetching(*refs):
        refs, held, sems = list(refs[:count]), refs[count:-1], refs[-1]
        copies = []
        for i, buffer in zip(fetched, held, strict=True):
            rows = args[i].shape[0] // pieces[i]
            for k in range(pieces[i]):
                some = slice(k * rows, (k + 1) * rows)
                ends = (refs[i].at[some], buffer.at[some]) if pieces[i] > 1 else (refs[i], buffer)
                copies.append(pltpu.make_async_copy(*ends, sems.at[len(copies)]))
        for copy in copies:
            copy.start()
        for copy in copies:
            copy.wait()
        for i, buffer in zip(fetched, held, strict=True):
            refs[i] = buffer
        kernel(*refs)

    extra = []
    if fetched:
        extra = [pltpu.VMEM(args[i].shape, args[i].dtype) for i in fetched]
        extra.append(pltpu.SemaphoreType.DMA((sum(pieces.values()),)))
    outside = set(apart) | set(fetched)
    return pl.pallas_call(
        fetching if fetched else kernel,
        out_shape=outs,
        in_specs=[
            pl.BlockSpec(memory_space=pltpu.HBM if i in outside else pltpu.VMEM) for i in range(len(args))
        ],
        out_specs=[
            pl.BlockSpec(memory_space=pltpu.HBM if i in outs_apart else pltpu.VMEM) for i in range(len(outs))
        ],
        scratch_shapes=list(scratch) + extra,
        compiler_params=pltpu.CompilerParams(vmem_limit_bytes=VMEM_LIMIT),
        cost_estimate=pl.CostEstimate(flops=flops, bytes_accessed=moved, transcendentals=0),
        name=name,
    )(*(far(a) if i in outside else a for i, a in enumerate(args)))


def across(a, k):
    return lax.ppermute(a, "grp", [(i, i ^ k) for i in range(lax.axis_size("grp"))])


def far(a):
    return pltpu.with_memory_space_constraint(a, pltpu.HBM)


def shaped(shape, dtype=F32):
    return jax.ShapeDtypeStruct(shape, dtype)


def body(energies, triples, pair_surfaces, pair_slot, single_surfaces, modals, mode_slot):
    devices = lax.axis_size("dev")
    groups = lax.axis_size("grp")
    number = triples.shape[0]
    own = modals.shape[0]
    capacity = 3 * number // devices
    cos_wide = np.zeros((G, 128), np.float32)
    fit_wide = np.zeros((G, 128), np.float32)
    cos_block = np.zeros((128, own * G), np.float32)
    for m in range(own):
        cos_wide[:, m * 32 : m * 32 + KEEP] = COSINES.T
        fit_wide[:, m * 32 + KEEP : m * 32 + 2 * KEEP] = FITTER.T
        cos_block[m * KEEP : (m + 1) * KEEP, m * G : (m + 1) * G] = COSINES
    kron = np.einsum("dh,el->hlde", FITTER, FITTER).reshape(G * G, KEEP * KEEP)
    hi, lo = (jnp.asarray(x) for x in halves_np(kron))
    fit_rows = np.zeros((G, 128), np.float32)
    fit_rows[:, :KEEP] = FITTER.T
    wide = np.zeros((2, 32, G, G))
    wide[0, :KEEP] = FITTER[:, :, None]
    wide[1, :KEEP] = FITTER[:, None, :]
    wide = jnp.asarray(np.stack([h[p] for p in range(2) for h in halves_np(wide.reshape(2, 32, G * G))]))
    send, meta = call(
        ask_kernel,
        [shaped((devices, 2, 128)), shaped((3 * number, 128))],
        triples.T,
        pair_slot,
        mode_slot.reshape(1, -1),
        modals,
        single_surfaces,
        jnp.asarray(cos_wide),
        jnp.asarray(fit_wide),
        fetched=tuple(range(7)),
        name="ask",
    )
    came = lax.all_to_all(send, "dev", 0, 0, tiled=True)
    table = shaped((pair_surfaces.shape[0], 512), BF16)
    first_hi, first_lo = halves_np(np.kron(FITTER, np.eye(8)))
    first = jnp.asarray(np.concatenate([first_hi, first_lo], axis=0))
    table_hi, table_lo, integral = call(
        table_kernel,
        [table, table, shaped((128, S * S))],
        pair_surfaces,
        hi,
        lo,
        modals,
        jnp.asarray(cos_block),
        fetched=(0, 1, 2, 3, 4),
        name="table",
        flops=5 * 10**8,
    )
    each = 2 * capacity + 1
    answer, known = call(
        share_kernel,
        [shaped((devices * each, 128)), shaped((3 * number, 128))],
        came,
        table_hi,
        table_lo,
        energies,
        meta,
        jnp.asarray(fit_rows),
        wide,
        apart=(3, 5, 6),
        name="share",
        flops=10**9,
        scratch=[
            pltpu.VMEM((G, 128), F32),
            pltpu.VMEM((number, G * G), F32),
            pltpu.VMEM((number, G * G), F32),
            pltpu.VMEM((G, 16, 128), F32),
            pltpu.VMEM(energies.shape, BF16),
            pltpu.VMEM(fit_rows.shape, F32),
            pltpu.VMEM(wide.shape, BF16),
            pltpu.SemaphoreType.DMA((number // 16,)),
            pltpu.SemaphoreType.DMA((2,)),
        ],
    )
    terms = lax.all_to_all(
        answer.reshape(devices, each, 1, 128), "dev", 0, 0, tiled=True
    ).reshape(devices * each, 128)
    far_part = (KEEP - NEAR, number, KEEP**2)
    fitted = call(
        fit_kernel,
        [shaped((number, KEEP**2))] * NEAR + [pltpu.HBM(far_part, F32)],
        energies,
        hi,
        lo,
        first,
        apart=(0,),
        outs_apart=(NEAR,),
        scratch=[
            pltpu.VMEM(energies.shape, BF16),
            pltpu.VMEM(far_part, F32),
            pltpu.SemaphoreType.DMA((number // FIT_TILE, 4)),
            pltpu.SemaphoreType.DMA((number // FIT_TILE,)),
        ],
        name="fit",
        flops=5 * 10**9,
    )
    terms, fitted = lax.optimization_barrier((terms, fitted))
    (mine,) = call(own_kernel, [shaped((1, 128))], terms, name="own")
    mine = mine + across(mine, 1)
    mine, terms = lax.optimization_barrier((mine, terms))
    neighbour = across(mine, 2)
    (got,) = call(gather_kernel, [shaped((3 * number, KEEP**2))], terms, meta, name="gather", flops=3 * 10**8)
    neighbour, got = lax.optimization_barrier((neighbour, got))
    mine = mine + neighbour
    parts = [mine, across(mine, 4)]
    mine, known, got = lax.optimization_barrier((mine, known, got))
    coefficients, energy = call(
        face_kernel,
        [pltpu.HBM((number, KEEP**3), BF16), shaped((1, number))],
        *fitted,
        got,
        known,
        apart=(NEAR,),
        outs_apart=(0,),
        scratch=[
            pltpu.VMEM((number, KEEP**3), BF16),
            pltpu.VMEM(far_part, F32),
            pltpu.SemaphoreType.DMA((4,)),
            pltpu.SemaphoreType.DMA,
        ],
        name="faces",
        flops=10**9,
    )
    (mean_field,) = call(
        integral_kernel,
        [shaped((own, S * S))],
        *parts,
        integral,
        name="integrals",
    )
    return coefficients, energy.reshape(number), mean_field


def solution(mesh):
    in_specs = (
        P(("grp", "dev"), None),
        P(("grp", "dev"), None),
        P("dev", None),
        P(),
        P("dev", None),
        P("dev", None),
        P(),
    )
    out_specs = (P(("grp", "dev"), None), P(("grp", "dev")), P("dev", None))
    return jax.shard_map(body, mesh=mesh, in_specs=in_specs, out_specs=out_specs, check_vma=False)
```

```python
import numpy as np
import jax
import jax.numpy as jnp
from jax import lax
from jax.experimental import pallas as pl
from jax.experimental.pallas import tpu as pltpu
from jax.sharding import PartitionSpec as P

G = 32
KEEP = 16
S = 16
F32 = jnp.float32
BF16 = jnp.bfloat16
HIGHEST = lax.Precision.HIGHEST
VMEM_LIMIT = 24 * 2**20


def tables():
    orders = np.arange(KEEP, dtype=np.float64)
    points = np.arange(G, dtype=np.float64) + 0.5
    cosines = np.cos(np.pi * orders[:, None] * points[None, :] / G)
    weights = np.where(orders == 0, 1.0, 2.0) / G
    return cosines, weights[:, None] * cosines


COSINES, FITTER = tables()


def halves(a):
    hi = a.astype(BF16)
    return hi, (a - hi.astype(F32)).astype(BF16)


def halves_np(a):
    a = a.astype(np.float32)
    hi = a.astype(jnp.bfloat16)
    return hi, (a - hi.astype(np.float32)).astype(jnp.bfloat16)


def dot(a, b):
    return jnp.dot(a, b, preferred_element_type=F32)


def dot_exact(a, b):
    return jnp.dot(a, b, preferred_element_type=F32, precision=HIGHEST)


def iota(shape, dim):
    return lax.broadcasted_iota(jnp.int32, shape, dim)


def lane_sum(a):
    return jnp.sum(a, axis=1, keepdims=True)


def column(row):
    n = row.shape[1]
    return lane_sum(jnp.where(iota((n, n), 0) == iota((n, n), 1), row, 0.0))


def one_hot(column_f, width):
    return (iota((column_f.shape[0], width), 1).astype(F32) == column_f).astype(F32).astype(BF16)


def dot_two(a, b):
    hi, lo = halves(a)
    return dot(hi, b) + dot(lo, b)


def pick_two(pick, hi, lo):
    return dot(pick, hi) + dot(pick, lo)


def ask_kernel(tri_ref, pair_ref, slot_ref, modal_ref, single_ref, cos_ref, fit_ref, out_ref, meta_ref):
    modes = slot_ref.shape[1]
    tri = tri_ref[...].astype(F32)
    first, second, third = (column(tri[p : p + 1]) for p in range(3))
    lower = jnp.concatenate([first, first, second], axis=0)
    upper = jnp.concatenate([second, third, third], axis=0)
    each = jnp.concatenate([first, second, third], axis=0)
    rows = lower.shape[0]
    number = rows // 3
    lane = iota((rows, modes), 1).astype(F32)
    pair = pair_ref[...]
    high = (pair >> 8).astype(F32).astype(BF16)
    low = (pair & 255).astype(F32).astype(BF16)
    pick = (lane == lower).astype(F32).astype(BF16)
    at = lane == upper
    owner = lane_sum(jnp.where(at, dot(pick, high), 0.0))
    local = lane_sum(jnp.where(at, dot(pick, low), 0.0))
    slots = slot_ref[...]
    slots = ((slots & 3) * 32 + (slots >> 2)).astype(F32)
    slot = lane_sum(jnp.where(lane == each, slots, 0.0))
    wide = iota((rows, 128), 1)
    wide_f = wide.astype(F32)
    hit = wide_f == owner
    hit_b = hit.astype(F32).astype(BF16)
    earlier = (iota((rows, rows), 1) < iota((rows, rows), 0)).astype(F32).astype(BF16)
    rank = lane_sum(jnp.where(hit, dot(earlier, hit_b), 0.0))
    ordered = lower < upper
    is_first = iota((rows, 1), 0) < number
    turned = jnp.where(is_first, ordered.astype(F32), 1.0 - ordered.astype(F32))
    s1, s2, s3 = (slot[p * number : (p + 1) * number] for p in range(3))
    left = jnp.concatenate([s1, s1, s2], axis=0)
    right = jnp.concatenate([s2, s3, s3], axis=0)
    other = jnp.concatenate([s3, s2, s1], axis=0)
    small = jnp.where(ordered, left, right)
    large = jnp.where(ordered, right, left)
    off = wide_f - rank
    said = jnp.where(off == 0.0, local, 0.0)
    for k, value in enumerate((turned, small, large, other)):
        said = said + jnp.where(off == 16.0 * (k + 1), value, 0.0)
    asked = lax.dot_general(hit_b, said.astype(BF16), (((0,), (0,)), ((), ())), preferred_element_type=F32)
    square = modal_ref[...] * modal_ref[...]
    spread = jnp.broadcast_to(cos_ref[...][:, None, :], (G, S, 128)).reshape(G * S, 128)
    spread = jnp.where((iota((G * S, 128), 0) & 15) == 0, spread, 0.0)
    mine = dot_exact(square, spread) + dot_exact(single_ref[...], fit_ref[...])
    four = mine.shape
    mine = jnp.sum(jnp.where((iota(four, 1) >> 5) == iota(four, 0), mine, 0.0), axis=0, keepdims=True)
    peers = out_ref.shape[0]
    out_ref[:, 0, :] = jnp.broadcast_to(mine, (peers, 128))
    out_ref[:, 1, :] = asked[:peers]
    meta_ref[...] = jnp.where(wide == 0, owner * 25.0 + rank, jnp.where(wide == 1, slot, 0.0))


FIT_TILE = 32
NEAR = 10


def fit_some(energy_ref, hi_ref, lo_ref, first_ref, out_refs, start):
    cells = G * G
    few = 8
    rows = pl.ds(pl.multiple_of(start, FIT_TILE), FIT_TILE)
    stacked = jnp.concatenate([energy_ref[rows, g * cells : (g + 1) * cells] for g in range(G)], axis=0)
    two = dot(stacked, hi_ref[...]) + dot(stacked, lo_ref[...])
    half = first_ref.shape[0] // 2
    for h in range(FIT_TILE // few):
        at = h * few
        part = jnp.concatenate(
            [two[g * FIT_TILE + at : g * FIT_TILE + at + few] for g in range(G)], axis=0
        )
        p_hi, p_lo = halves(part)
        large = dot(first_ref[...], p_hi)
        all_three = large[:half] + large[half:] + dot(first_ref[:half], p_lo)
        some = pl.ds(pl.multiple_of(start + at, few), few)
        for c in range(KEEP):
            out_refs[c][some, :] = all_three[c * few : (c + 1) * few]


def table_kernel(
    pair_ref,
    hi_ref,
    lo_ref,
    modal_ref,
    cosine_ref,
    table_hi_ref,
    table_lo_ref,
    integral_ref,
):
    a_hi, a_lo = halves(pair_ref[...])
    k_hi, k_lo = hi_ref[...], lo_ref[...]
    terms = dot(a_hi, k_hi) + dot(a_hi, k_lo) + dot(a_lo, k_hi)
    square = (256, 256)
    i, j = iota(square, 0), iota(square, 1)
    turn = (((i & 15) == (j >> 4)) & ((i >> 4) == (j & 15))).astype(F32).astype(BF16)
    t_hi, t_lo = halves(terms)
    table_hi_ref[:, :256] = t_hi
    table_lo_ref[:, :256] = t_lo
    table_hi_ref[:, 256:] = dot(t_hi, turn).astype(BF16)
    table_lo_ref[:, 256:] = dot(t_lo, turn).astype(BF16)
    modal = modal_ref[...]
    own = modal.shape[0]
    row = iota((own * G, G * S), 0)
    lane = iota((own * G, G * S), 1)
    spread = jnp.zeros((own * G, G * S), F32)
    for m in range(own):
        spread = jnp.where((row >> 5) == m, modal[m : m + 1, :], spread)
    spread = jnp.where((lane >> 4) == (row & 31), spread, 0.0)
    k, n = iota((G * S, 256), 0), iota((G * S, 256), 1)
    hi, lo = halves(spread)
    to_left = ((k & 15) == (n >> 4)).astype(F32).astype(BF16)
    to_right = ((k & 15) == (n & 15)).astype(F32).astype(BF16)
    left = dot(hi, to_left) + dot(lo, to_left)
    right = dot(hi, to_right) + dot(lo, to_right)
    integral_ref[...] = dot_exact(cosine_ref[...], left * right)


def fit_kernel(source_ref, hi_ref, lo_ref, first_ref, *refs):
    near_refs = list(refs[:NEAR])
    far_ref, energy_ref, rest_ref, sems, out_sems = refs[NEAR:]
    tiles = energy_ref.shape[0] // FIT_TILE
    out_refs = near_refs + [rest_ref.at[c] for c in range(KEEP - NEAR)]

    def copies(r):
        few = FIT_TILE // 4
        for k in range(4):
            rows = pl.ds(pl.multiple_of(r * FIT_TILE + k * few, few), few)
            yield pltpu.make_async_copy(source_ref.at[rows], energy_ref.at[rows], sems.at[r, k])

    def copy_out(r):
        rows = pl.ds(pl.multiple_of(r * FIT_TILE, FIT_TILE), FIT_TILE)
        return pltpu.make_async_copy(rest_ref.at[:, rows], far_ref.at[:, rows], out_sems.at[r])

    for r in range(2):
        for copy in copies(r):
            copy.start()

    def over_rows(r, carry):
        for copy in copies(r):
            copy.wait()

        @pl.when(r + 2 < tiles)
        def _():
            for copy in copies(r + 2):
                copy.start()

        fit_some(energy_ref, hi_ref, lo_ref, first_ref, out_refs, r * FIT_TILE)
        copy_out(r).start()
        return carry

    lax.fori_loop(0, tiles, over_rows, 0)
    for r in range(tiles):
        copy_out(r).wait()


def share_kernel(
    came_ref,
    hi_ref,
    lo_ref,
    source_ref,
    meta_ref,
    fit_in,
    wide_in,
    out_ref,
    known_ref,
    w1_ref,
    w23_ref,
    lead_ref,
    along_ref,
    energy_ref,
    fit_ref,
    wide_ref,
    sems,
    more_sems,
):
    tile = 16
    tables_in = [
        pltpu.make_async_copy(fit_in, fit_ref, more_sems.at[0]),
        pltpu.make_async_copy(wide_in, wide_ref, more_sems.at[1]),
    ]
    for part in tables_in:
        part.start()

    def copy(r):
        rows_r = pl.ds(pl.multiple_of(r * tile, tile), tile)
        return pltpu.make_async_copy(source_ref.at[rows_r], energy_ref.at[rows_r], sems.at[r])

    tiles, ahead = energy_ref.shape[0] // tile, 4
    for r in range(ahead):
        copy(r).start()
    peers = came_ref.shape[0]
    number = energy_ref.shape[0]
    rows = 3 * number
    asked = came_ref[:, 1, :].astype(BF16)
    per = float(rows // peers)
    at = iota((rows, 1), 0).astype(F32)
    peer = jnp.floor((at + 0.5) * (1.0 / per))
    rank = at - per * peer
    seen = dot(one_hot(peer, peers), asked)
    off = iota((rows, 128), 1).astype(F32) - rank
    local, small, large, other = (
        lane_sum(jnp.where(off == 16.0 * k, seen, 0.0)) for k in (0, 2, 3, 4)
    )
    slot = jnp.concatenate([meta_ref[:, 1:2], small, large, other], axis=0)
    pick = one_hot(slot, 128)
    ground = came_ref[:, 0, :]
    spots = 128 // peers
    ground = jnp.concatenate([pltpu.roll(ground, 128 - 32 * j, 1) if j else ground for j in range(spots)], axis=0)
    ground = jnp.where(iota((128, 128), 1) < 32, ground, 0.0)
    ground = ground + pltpu.roll(ground, 32, 1)
    ground = ground + pltpu.roll(ground, 64, 1)
    known = pick_two(pick, *halves(ground))
    known_ref[...] = known[:rows]
    k, n = iota((128, 256), 0), iota((128, 256), 1)
    widen = (k == (n >> 4)).astype(F32).astype(BF16)
    k, n = iota((256, 128), 0), iota((256, 128), 1)
    to_high = ((k >> 4) == n).astype(F32).astype(BF16)
    to_low = ((k & 15) == n).astype(F32).astype(BF16)

    def repeated(a):
        part = jnp.where((iota(a.shape, 1) & 31) < 16, a, 0.0)
        return part + pltpu.roll(part, 16, 1)

    def twice(a):
        return jnp.concatenate([a, a], axis=1)

    terms = pick_two(one_hot(local, 256), hi_ref[:, :256], lo_ref[:, :256])
    g_small, g_large, g_other = (known[p * rows : (p + 1) * rows] for p in (1, 2, 3))
    of_small = dot_two(terms * twice(repeated(g_large)), to_high)
    of_large = dot_two(terms * dot_two(g_small, widen), to_low)
    norm = g_other[:, 0:1]
    of_other = lane_sum(of_small * g_small)
    lane = iota((rows, 128), 1)
    shares = [-norm * of_small, -norm * of_large, jnp.where(lane == 0, -of_other, 0.0)]
    one, two, three = (known[p * number : (p + 1) * number] for p in range(3))
    cells = G * G
    for part in tables_in:
        part.wait()
    w1_ref[...] = jnp.broadcast_to(lane_sum(fit_ref[...] * one[0:1]), w1_ref.shape)
    ways = [wide_ref[p] for p in range(4)]

    def weights(a, hi, lo):
        a_hi, a_lo = halves(a[:, :32])
        return dot(a_hi, hi) + dot(a_hi, lo) + dot(a_lo, hi)

    w2 = weights(two, ways[0], ways[1])
    w3 = weights(three, ways[2], ways[3])
    w23_ref[...] = w2 * w3
    lanes = cells // 128

    def over_rows(r, carry):
        copy(r).wait()

        @pl.when(r + ahead < tiles)
        def _():
            copy(r + ahead).start()

        rows_r = pl.ds(pl.multiple_of(r * tile, tile), tile)
        w23 = [w23_ref[rows_r, k * 128 : (k + 1) * 128] for k in range(lanes)]

        def over_points(g, lead):
            x = energy_ref[rows_r, pl.ds(pl.multiple_of(g * cells, cells), cells)].astype(F32)
            w1 = w1_ref[pl.ds(g, 1), :]
            fresh, along = [], None
            for k in range(lanes):
                part = x[:, k * 128 : (k + 1) * 128]
                fresh.append(lead[k] + w1 * part)
                term = part * w23[k]
                along = term if along is None else along + term
            along_ref[g] += along
            return tuple(fresh)

        none = jnp.zeros((tile, 128), F32)
        lead = lax.fori_loop(0, G, over_points, (none,) * lanes, unroll=16)
        for k in range(lanes):
            lead_ref[rows_r, k * 128 : (k + 1) * 128] = lead[k]
        return carry

    along_ref[...] = jnp.zeros_like(along_ref)
    lax.fori_loop(0, tiles, over_rows, 0)

    def back(a, hi, lo):
        a_hi, a_lo = halves(a)
        dims = (((1,), (1,)), ((), ()))
        total = lax.dot_general(a_hi, hi, dims, preferred_element_type=F32)
        total = total + lax.dot_general(a_hi, lo, dims, preferred_element_type=F32)
        total = total + lax.dot_general(a_lo, hi, dims, preferred_element_type=F32)
        return jnp.concatenate([total, jnp.zeros((number, 96), F32)], axis=1)

    sums = lane_sum(jnp.sum(along_ref[...], axis=1))
    field_first = jnp.sum(sums * fit_ref[...], axis=0, keepdims=True)
    field_first = jnp.where(iota((number, 128), 0) == 0, field_first, 0.0)
    field_second = back(lead_ref[...] * w3, ways[0], ways[1])
    field_third = back(lead_ref[...] * w2, ways[2], ways[3])
    own = known[:rows]
    lane = iota((rows, 128), 1)
    single = jnp.where(lane < 16, pltpu.roll(own, 112, 1), 0.0)
    along = lane_sum(single * own)
    norms = own[:, 0:1]
    n1, n2, n3 = (norms[p * number : (p + 1) * number] for p in range(3))
    q1, q2, q3 = (along[p * number : (p + 1) * number] for p in range(3))
    scale = jnp.concatenate([n2 * n3, n1 * n3, n1 * n2], axis=0)
    shift = jnp.concatenate([n3 * q2 + n2 * q3, n3 * q1 + n1 * q3, n2 * q1 + n1 * q2], axis=0)
    from_grid = jnp.concatenate([field_first, field_second, field_third], axis=0)
    from_grid = from_grid - scale * single - jnp.where(lane == 0, shift, 0.0)
    fields = jnp.concatenate([from_grid] + shares, axis=0)
    f_hi, f_lo = halves(fields)
    dims = (((0,), (0,)), ((), ()))
    part = lax.dot_general(pick, f_hi, dims, preferred_element_type=F32) + lax.dot_general(
        pick, f_lo, dims, preferred_element_type=F32
    )
    part = part[:peers] + sum(
        pltpu.roll(part[j * peers : (j + 1) * peers], 16 * j, 1) for j in range(1, spots)
    )
    slots = out_ref.shape[0]
    each = float(slots // peers)
    at = iota((slots, 1), 0).astype(F32)
    peer = jnp.floor((at + 0.5) * (1.0 / each))
    rest = at - each * peer
    late = rest >= per
    rank = rest - jnp.where(late, per, 0.0)
    from_peer = one_hot(peer, peers)
    seen = dot(from_peer, asked)
    off = iota((slots, 128), 1).astype(F32) - rank
    local = lane_sum(jnp.where(off == 0.0, seen, 0.0))
    turned = lane_sum(jnp.where(off == 16.0, seen, 0.0))
    terms = pick_two(one_hot(local, 256), hi_ref[...], lo_ref[...])
    terms = jnp.where(turned > 0.5, terms[:, 256:], terms[:, :256])
    terms = jnp.where(late, terms[:, 128:], terms[:, :128])
    p_hi, p_lo = halves(part)
    out_ref[...] = jnp.where(rest == 2.0 * per, pick_two(from_peer, p_hi, p_lo), terms)


def own_kernel(came_ref, out_ref):
    peers = came_ref.shape[0] // 25
    each = 25
    rows = came_ref[pl.ds(each - 1, peers, stride=each), :]
    out_ref[...] = jnp.sum(rows, axis=0, keepdims=True)


def face_kernel(*refs):
    far_ref, came_ref, known_ref, meta_ref, far_out, energy_ref, coef_ref, rest_ref, out_sems, sem = refs[NEAR:]
    fit_refs = list(refs[:NEAR]) + [rest_ref.at[c] for c in range(KEEP - NEAR)]
    coming = pltpu.make_async_copy(far_ref, rest_ref, sem)
    coming.start()
    number = coef_ref.shape[0]
    some = 4
    leaving = []
    for k in range(KEEP // some):
        cols = slice(k * some * 256, (k + 1) * some * 256)
        leaving.append(pltpu.make_async_copy(coef_ref.at[:, cols], far_out.at[:, cols], out_sems.at[k]))
    place = meta_ref[:, 0:1]
    known = known_ref[...]
    one, two, three = (known[p * number : (p + 1) * number] for p in range(3))
    hi, lo = halves(came_ref[...])
    slots = came_ref.shape[0]
    got = [pick_two(one_hot(place + 12.0 * h, slots), hi, lo) for h in range(2)]
    lane = iota((number, 128), 1)
    k, n = iota((128, 256), 0), iota((128, 256), 1)
    two_wide = dot_two(two, (k == (n >> 4)).astype(F32).astype(BF16))
    two_single = dot_two(two, ((k == (n >> 4) + 16) & ((n & 15) == 0)).astype(F32).astype(BF16))
    three_low = jnp.where((lane & 31) < 16, three, 0.0)
    three_wide = three_low + pltpu.roll(three_low, 16, 1)
    start = lane < 16
    first_pair = [g[:number] for g in got]
    first_pair[0] = first_pair[0] + jnp.where(start, pltpu.roll(one, 112, 1), 0.0)
    second_pair = [g[number : 2 * number] for g in got]
    third_pair = [g[2 * number :] for g in got]
    third_pair[0] = third_pair[0] + jnp.where(start, pltpu.roll(three, 112, 1), 0.0)
    third_pair = [t + two_single[:, h * 128 : (h + 1) * 128] for h, t in enumerate(third_pair)]
    both = [two_wide[:, h * 128 : (h + 1) * 128] * three_wide for h in range(2)]
    spaced = (lane & 15) == 0
    energy = jnp.zeros((number, 128), F32)
    for c in range(KEEP):
        if c == NEAR:
            coming.wait()
        along = jnp.zeros((number, 128), F32)
        for h in range(2):
            moved = pltpu.roll(first_pair[h], 128 - c, 1) if c else first_pair[h]
            value = fit_refs[c][:, h * 128 : (h + 1) * 128] - jnp.where(spaced, moved, 0.0)
            if h == 0:
                shift = (c % 8) * 16
                moved = second_pair[c // 8]
                moved = pltpu.roll(moved, 128 - shift, 1) if shift else moved
                value = value - jnp.where(start, moved, 0.0)
            if c == 0:
                value = value - third_pair[h]
            coef_ref[:, c * 256 + h * 128 : c * 256 + (h + 1) * 128] = value.astype(BF16)
            along = along + value * both[h]
        energy = energy + one[:, c : c + 1] * along
        if c % some == some - 1:
            leaving[c // some].start()
    energy_ref[...] = lax.dot_general(
        jnp.full((8, 128), 1.0, F32), energy, (((1,), (1,)), ((), ())), preferred_element_type=F32, precision=HIGHEST
    )[0:1]
    for copy in leaving:
        copy.wait()


def integral_kernel(*refs):
    *parts, integral_ref, out_ref = refs
    parts = [p[...] for p in parts]
    while len(parts) > 1:
        parts = [parts[i] + parts[i + 1] for i in range(0, len(parts), 2)]
    shape = (out_ref.shape[0], 128)
    total = jnp.where((iota(shape, 1) >> 4) == iota(shape, 0), parts[0], 0.0)
    out_ref[...] = dot_exact(total, integral_ref[...])


def call(kernel, outs, *args, name, apart=(), fetched=(), outs_apart=(), flops=0, scratch=()):
    moved = sum(int(np.prod(a.shape)) * a.dtype.itemsize for a in args) + sum(
        int(np.prod(o.shape)) * o.dtype.itemsize for o in outs
    )
    count = len(args) + len(outs) + len(scratch)
    pieces = {i: 4 if args[i].size * args[i].dtype.itemsize >= 2**18 else 1 for i in fetched}

    def fetching(*refs):
        refs, held, sems = list(refs[:count]), refs[count:-1], refs[-1]
        copies = []
        for i, buffer in zip(fetched, held, strict=True):
            rows = args[i].shape[0] // pieces[i]
            for k in range(pieces[i]):
                some = slice(k * rows, (k + 1) * rows)
                ends = (refs[i].at[some], buffer.at[some]) if pieces[i] > 1 else (refs[i], buffer)
                copies.append(pltpu.make_async_copy(*ends, sems.at[len(copies)]))
        for copy in copies:
            copy.start()
        for copy in copies:
            copy.wait()
        for i, buffer in zip(fetched, held, strict=True):
            refs[i] = buffer
        kernel(*refs)

    extra = []
    if fetched:
        extra = [pltpu.VMEM(args[i].shape, args[i].dtype) for i in fetched]
        extra.append(pltpu.SemaphoreType.DMA((sum(pieces.values()),)))
    outside = set(apart) | set(fetched)
    return pl.pallas_call(
        fetching if fetched else kernel,
        out_shape=outs,
        in_specs=[
            pl.BlockSpec(memory_space=pltpu.HBM if i in outside else pltpu.VMEM) for i in range(len(args))
        ],
        out_specs=[
            pl.BlockSpec(memory_space=pltpu.HBM if i in outs_apart else pltpu.VMEM) for i in range(len(outs))
        ],
        scratch_shapes=list(scratch) + extra,
        compiler_params=pltpu.CompilerParams(vmem_limit_bytes=VMEM_LIMIT),
        cost_estimate=pl.CostEstimate(flops=flops, bytes_accessed=moved, transcendentals=0),
        name=name,
    )(*(far(a) if i in outside else a for i, a in enumerate(args)))


def across(a, k):
    return lax.ppermute(a, "grp", [(i, i ^ k) for i in range(lax.axis_size("grp"))])


def far(a):
    return pltpu.with_memory_space_constraint(a, pltpu.HBM)


def shaped(shape, dtype=F32):
    return jax.ShapeDtypeStruct(shape, dtype)


def body(energies, triples, pair_surfaces, pair_slot, single_surfaces, modals, mode_slot):
    devices = lax.axis_size("dev")
    groups = lax.axis_size("grp")
    number = triples.shape[0]
    own = modals.shape[0]
    capacity = 3 * number // devices
    cos_wide = np.zeros((G, 128), np.float32)
    fit_wide = np.zeros((G, 128), np.float32)
    cos_block = np.zeros((128, own * G), np.float32)
    for m in range(own):
        cos_wide[:, m * 32 : m * 32 + KEEP] = COSINES.T
        fit_wide[:, m * 32 + KEEP : m * 32 + 2 * KEEP] = FITTER.T
        cos_block[m * KEEP : (m + 1) * KEEP, m * G : (m + 1) * G] = COSINES
    kron = np.einsum("dh,el->hlde", FITTER, FITTER).reshape(G * G, KEEP * KEEP)
    hi, lo = (jnp.asarray(x) for x in halves_np(kron))
    fit_rows = np.zeros((G, 128), np.float32)
    fit_rows[:, :KEEP] = FITTER.T
    wide = np.zeros((2, 32, G, G))
    wide[0, :KEEP] = FITTER[:, :, None]
    wide[1, :KEEP] = FITTER[:, None, :]
    wide = jnp.asarray(np.stack([h[p] for p in range(2) for h in halves_np(wide.reshape(2, 32, G * G))]))
    send, meta = call(
        ask_kernel,
        [shaped((devices, 2, 128)), shaped((3 * number, 128))],
        triples.T,
        pair_slot,
        mode_slot.reshape(1, -1),
        modals,
        single_surfaces,
        jnp.asarray(cos_wide),
        jnp.asarray(fit_wide),
        fetched=tuple(range(7)),
        name="ask",
    )
    came = lax.all_to_all(send, "dev", 0, 0, tiled=True)
    table = shaped((pair_surfaces.shape[0], 512), BF16)
    first_hi, first_lo = halves_np(np.kron(FITTER, np.eye(8)))
    first = jnp.asarray(np.concatenate([first_hi, first_lo], axis=0))
    table_hi, table_lo, integral = call(
        table_kernel,
        [table, table, shaped((128, S * S))],
        pair_surfaces,
        hi,
        lo,
        modals,
        jnp.asarray(cos_block),
        fetched=(0, 1, 2, 3, 4),
        name="table",
        flops=5 * 10**8,
    )
    each = 2 * capacity + 1
    answer, known = call(
        share_kernel,
        [shaped((devices * each, 128)), shaped((3 * number, 128))],
        came,
        table_hi,
        table_lo,
        energies,
        meta,
        jnp.asarray(fit_rows),
        wide,
        apart=(3, 5, 6),
        name="share",
        flops=10**9,
        scratch=[
            pltpu.VMEM((G, 128), F32),
            pltpu.VMEM((number, G * G), F32),
            pltpu.VMEM((number, G * G), F32),
            pltpu.VMEM((G, 16, 128), F32),
            pltpu.VMEM(energies.shape, BF16),
            pltpu.VMEM(fit_rows.shape, F32),
            pltpu.VMEM(wide.shape, BF16),
            pltpu.SemaphoreType.DMA((number // 16,)),
            pltpu.SemaphoreType.DMA((2,)),
        ],
    )
    terms = lax.all_to_all(
        answer.reshape(devices, each, 1, 128), "dev", 0, 0, tiled=True
    ).reshape(devices * each, 128)
    far_part = (KEEP - NEAR, number, KEEP**2)
    fitted = call(
        fit_kernel,
        [shaped((number, KEEP**2))] * NEAR + [pltpu.HBM(far_part, F32)],
        energies,
        hi,
        lo,
        first,
        apart=(0,),
        outs_apart=(NEAR,),
        scratch=[
            pltpu.VMEM(energies.shape, BF16),
            pltpu.VMEM(far_part, F32),
            pltpu.SemaphoreType.DMA((number // FIT_TILE, 4)),
            pltpu.SemaphoreType.DMA((number // FIT_TILE,)),
        ],
        name="fit",
        flops=5 * 10**9,
    )
    terms, fitted = lax.optimization_barrier((terms, fitted))
    (mine,) = call(own_kernel, [shaped((1, 128))], terms, name="own")
    mine = mine + across(mine, 1)
    parts = [mine] + [across(mine, k) for k in range(2, groups, 2)]
    mine, known = lax.optimization_barrier((mine, known))
    coefficients, energy = call(
        face_kernel,
        [pltpu.HBM((number, KEEP**3), BF16), shaped((1, number))],
        *fitted,
        terms,
        known,
        meta,
        apart=(NEAR,),
        outs_apart=(0,),
        scratch=[
            pltpu.VMEM((number, KEEP**3), BF16),
            pltpu.VMEM(far_part, F32),
            pltpu.SemaphoreType.DMA((4,)),
            pltpu.SemaphoreType.DMA,
        ],
        name="faces",
        flops=10**9,
    )
    (mean_field,) = call(
        integral_kernel,
        [shaped((own, S * S))],
        *parts,
        integral,
        name="integrals",
    )
    return coefficients, energy.reshape(number), mean_field


def solution(mesh):
    in_specs = (
        P(("grp", "dev"), None),
        P(("grp", "dev"), None),
        P("dev", None),
        P(),
        P("dev", None),
        P("dev", None),
        P(),
    )
    out_specs = (P(("grp", "dev"), None), P(("grp", "dev")), P("dev", None))
    return jax.shard_map(body, mesh=mesh, in_specs=in_specs, out_specs=out_specs, check_vma=False)
```

```python
import numpy as np
import jax
import jax.numpy as jnp
from jax import lax
from jax.experimental import pallas as pl
from jax.experimental.pallas import tpu as pltpu
from jax.sharding import PartitionSpec as P

G = 32
KEEP = 16
S = 16
F32 = jnp.float32
BF16 = jnp.bfloat16
HIGHEST = lax.Precision.HIGHEST
VMEM_LIMIT = 24 * 2**20


def tables():
    orders = np.arange(KEEP, dtype=np.float64)
    points = np.arange(G, dtype=np.float64) + 0.5
    cosines = np.cos(np.pi * orders[:, None] * points[None, :] / G)
    weights = np.where(orders == 0, 1.0, 2.0) / G
    return cosines, weights[:, None] * cosines


COSINES, FITTER = tables()


def halves(a):
    hi = a.astype(BF16)
    return hi, (a - hi.astype(F32)).astype(BF16)


def halves_np(a):
    a = a.astype(np.float32)
    hi = a.astype(jnp.bfloat16)
    return hi, (a - hi.astype(np.float32)).astype(jnp.bfloat16)


def dot(a, b):
    return jnp.dot(a, b, preferred_element_type=F32)


def dot_exact(a, b):
    return jnp.dot(a, b, preferred_element_type=F32, precision=HIGHEST)


def iota(shape, dim):
    return lax.broadcasted_iota(jnp.int32, shape, dim)


def lane_sum(a):
    return jnp.sum(a, axis=1, keepdims=True)


def column(row):
    n = row.shape[1]
    return lane_sum(jnp.where(iota((n, n), 0) == iota((n, n), 1), row, 0.0))


def one_hot(column_f, width):
    return (iota((column_f.shape[0], width), 1).astype(F32) == column_f).astype(F32).astype(BF16)


def dot_two(a, b):
    hi, lo = halves(a)
    return dot(hi, b) + dot(lo, b)


def pick_two(pick, hi, lo):
    return dot(pick, hi) + dot(pick, lo)


def ask_kernel(tri_ref, pair_ref, slot_ref, modal_ref, single_ref, cos_ref, fit_ref, out_ref, meta_ref):
    modes = slot_ref.shape[1]
    tri = tri_ref[...].astype(F32)
    first, second, third = (column(tri[p : p + 1]) for p in range(3))
    lower = jnp.concatenate([first, first, second], axis=0)
    upper = jnp.concatenate([second, third, third], axis=0)
    each = jnp.concatenate([first, second, third], axis=0)
    rows = lower.shape[0]
    number = rows // 3
    lane = iota((rows, modes), 1).astype(F32)
    pair = pair_ref[...]
    high = (pair >> 8).astype(F32).astype(BF16)
    low = (pair & 255).astype(F32).astype(BF16)
    pick = (lane == lower).astype(F32).astype(BF16)
    at = lane == upper
    owner = lane_sum(jnp.where(at, dot(pick, high), 0.0))
    local = lane_sum(jnp.where(at, dot(pick, low), 0.0))
    slots = slot_ref[...]
    slots = ((slots & 3) * 32 + (slots >> 2)).astype(F32)
    slot = lane_sum(jnp.where(lane == each, slots, 0.0))
    wide = iota((rows, 128), 1)
    wide_f = wide.astype(F32)
    hit = wide_f == owner
    hit_b = hit.astype(F32).astype(BF16)
    earlier = (iota((rows, rows), 1) < iota((rows, rows), 0)).astype(F32).astype(BF16)
    rank = lane_sum(jnp.where(hit, dot(earlier, hit_b), 0.0))
    ordered = lower < upper
    is_first = iota((rows, 1), 0) < number
    turned = jnp.where(is_first, ordered.astype(F32), 1.0 - ordered.astype(F32))
    s1, s2, s3 = (slot[p * number : (p + 1) * number] for p in range(3))
    left = jnp.concatenate([s1, s1, s2], axis=0)
    right = jnp.concatenate([s2, s3, s3], axis=0)
    other = jnp.concatenate([s3, s2, s1], axis=0)
    small = jnp.where(ordered, left, right)
    large = jnp.where(ordered, right, left)
    off = wide_f - rank
    said = jnp.where(off == 0.0, local, 0.0)
    for k, value in enumerate((turned, small, large, other)):
        said = said + jnp.where(off == 16.0 * (k + 1), value, 0.0)
    asked = lax.dot_general(hit_b, said.astype(BF16), (((0,), (0,)), ((), ())), preferred_element_type=F32)
    square = modal_ref[...] * modal_ref[...]
    spread = jnp.broadcast_to(cos_ref[...][:, None, :], (G, S, 128)).reshape(G * S, 128)
    spread = jnp.where((iota((G * S, 128), 0) & 15) == 0, spread, 0.0)
    mine = dot_exact(square, spread) + dot_exact(single_ref[...], fit_ref[...])
    four = mine.shape
    mine = jnp.sum(jnp.where((iota(four, 1) >> 5) == iota(four, 0), mine, 0.0), axis=0, keepdims=True)
    peers = out_ref.shape[0]
    out_ref[:, 0, :] = jnp.broadcast_to(mine, (peers, 128))
    out_ref[:, 1, :] = asked[:peers]
    meta_ref[...] = jnp.where(wide == 0, owner * 25.0 + rank, jnp.where(wide == 1, slot, 0.0))


FIT_TILE = 32
NEAR = 11


def fit_some(energy_ref, hi_ref, lo_ref, first_ref, out_refs, start):
    cells = G * G
    few = 8
    rows = pl.ds(pl.multiple_of(start, FIT_TILE), FIT_TILE)
    stacked = jnp.concatenate([energy_ref[rows, g * cells : (g + 1) * cells] for g in range(G)], axis=0)
    two = dot(stacked, hi_ref[...]) + dot(stacked, lo_ref[...])
    half = first_ref.shape[0] // 2
    for h in range(FIT_TILE // few):
        at = h * few
        part = jnp.concatenate(
            [two[g * FIT_TILE + at : g * FIT_TILE + at + few] for g in range(G)], axis=0
        )
        p_hi, p_lo = halves(part)
        large = dot(first_ref[...], p_hi)
        all_three = large[:half] + large[half:] + dot(first_ref[:half], p_lo)
        some = pl.ds(pl.multiple_of(start + at, few), few)
        for c in range(KEEP):
            out_refs[c][some, :] = all_three[c * few : (c + 1) * few]


def table_kernel(
    pair_ref,
    hi_ref,
    lo_ref,
    modal_ref,
    cosine_ref,
    table_hi_ref,
    table_lo_ref,
    integral_ref,
):
    a_hi, a_lo = halves(pair_ref[...])
    k_hi, k_lo = hi_ref[...], lo_ref[...]
    terms = dot(a_hi, k_hi) + dot(a_hi, k_lo) + dot(a_lo, k_hi)
    square = (256, 256)
    i, j = iota(square, 0), iota(square, 1)
    turn = (((i & 15) == (j >> 4)) & ((i >> 4) == (j & 15))).astype(F32).astype(BF16)
    t_hi, t_lo = halves(terms)
    table_hi_ref[:, :256] = t_hi
    table_lo_ref[:, :256] = t_lo
    table_hi_ref[:, 256:] = dot(t_hi, turn).astype(BF16)
    table_lo_ref[:, 256:] = dot(t_lo, turn).astype(BF16)
    modal = modal_ref[...]
    own = modal.shape[0]
    row = iota((own * G, G * S), 0)
    lane = iota((own * G, G * S), 1)
    spread = jnp.zeros((own * G, G * S), F32)
    for m in range(own):
        spread = jnp.where((row >> 5) == m, modal[m : m + 1, :], spread)
    spread = jnp.where((lane >> 4) == (row & 31), spread, 0.0)
    k, n = iota((G * S, 256), 0), iota((G * S, 256), 1)
    hi, lo = halves(spread)
    to_left = ((k & 15) == (n >> 4)).astype(F32).astype(BF16)
    to_right = ((k & 15) == (n & 15)).astype(F32).astype(BF16)
    left = dot(hi, to_left) + dot(lo, to_left)
    right = dot(hi, to_right) + dot(lo, to_right)
    integral_ref[...] = dot_exact(cosine_ref[...], left * right)


def fit_kernel(source_ref, hi_ref, lo_ref, first_ref, *refs):
    near_refs = list(refs[:NEAR])
    far_ref, energy_ref, rest_ref, sems, out_sems = refs[NEAR:]
    tiles = energy_ref.shape[0] // FIT_TILE
    out_refs = near_refs + [rest_ref.at[c] for c in range(KEEP - NEAR)]

    def copies(r):
        few = FIT_TILE // 4
        for k in range(4):
            rows = pl.ds(pl.multiple_of(r * FIT_TILE + k * few, few), few)
            yield pltpu.make_async_copy(source_ref.at[rows], energy_ref.at[rows], sems.at[r, k])

    def copy_out(r):
        rows = pl.ds(pl.multiple_of(r * FIT_TILE, FIT_TILE), FIT_TILE)
        return pltpu.make_async_copy(rest_ref.at[:, rows], far_ref.at[:, rows], out_sems.at[r])

    for r in range(2):
        for copy in copies(r):
            copy.start()

    def over_rows(r, carry):
        for copy in copies(r):
            copy.wait()

        @pl.when(r + 2 < tiles)
        def _():
            for copy in copies(r + 2):
                copy.start()

        fit_some(energy_ref, hi_ref, lo_ref, first_ref, out_refs, r * FIT_TILE)
        copy_out(r).start()
        return carry

    lax.fori_loop(0, tiles, over_rows, 0)
    for r in range(tiles):
        copy_out(r).wait()


def share_kernel(
    came_ref,
    hi_ref,
    lo_ref,
    source_ref,
    meta_ref,
    fit_in,
    wide_in,
    out_ref,
    known_ref,
    w1_ref,
    w23_ref,
    lead_ref,
    along_ref,
    energy_ref,
    fit_ref,
    wide_ref,
    sems,
    more_sems,
):
    tile = 16
    tables_in = [
        pltpu.make_async_copy(fit_in, fit_ref, more_sems.at[0]),
        pltpu.make_async_copy(wide_in, wide_ref, more_sems.at[1]),
    ]
    for part in tables_in:
        part.start()

    def copy(r):
        rows_r = pl.ds(pl.multiple_of(r * tile, tile), tile)
        return pltpu.make_async_copy(source_ref.at[rows_r], energy_ref.at[rows_r], sems.at[r])

    tiles, ahead = energy_ref.shape[0] // tile, 4
    for r in range(ahead):
        copy(r).start()
    peers = came_ref.shape[0]
    number = energy_ref.shape[0]
    rows = 3 * number
    asked = came_ref[:, 1, :].astype(BF16)
    per = float(rows // peers)
    at = iota((rows, 1), 0).astype(F32)
    peer = jnp.floor((at + 0.5) * (1.0 / per))
    rank = at - per * peer
    seen = dot(one_hot(peer, peers), asked)
    off = iota((rows, 128), 1).astype(F32) - rank
    local, small, large, other = (
        lane_sum(jnp.where(off == 16.0 * k, seen, 0.0)) for k in (0, 2, 3, 4)
    )
    slot = jnp.concatenate([meta_ref[:, 1:2], small, large, other], axis=0)
    pick = one_hot(slot, 128)
    ground = came_ref[:, 0, :]
    spots = 128 // peers
    ground = jnp.concatenate([pltpu.roll(ground, 128 - 32 * j, 1) if j else ground for j in range(spots)], axis=0)
    ground = jnp.where(iota((128, 128), 1) < 32, ground, 0.0)
    ground = ground + pltpu.roll(ground, 32, 1)
    ground = ground + pltpu.roll(ground, 64, 1)
    known = pick_two(pick, *halves(ground))
    known_ref[...] = known[:rows]
    k, n = iota((128, 256), 0), iota((128, 256), 1)
    widen = (k == (n >> 4)).astype(F32).astype(BF16)
    k, n = iota((256, 128), 0), iota((256, 128), 1)
    to_high = ((k >> 4) == n).astype(F32).astype(BF16)
    to_low = ((k & 15) == n).astype(F32).astype(BF16)

    def repeated(a):
        part = jnp.where((iota(a.shape, 1) & 31) < 16, a, 0.0)
        return part + pltpu.roll(part, 16, 1)

    def twice(a):
        return jnp.concatenate([a, a], axis=1)

    terms = pick_two(one_hot(local, 256), hi_ref[:, :256], lo_ref[:, :256])
    g_small, g_large, g_other = (known[p * rows : (p + 1) * rows] for p in (1, 2, 3))
    of_small = dot_two(terms * twice(repeated(g_large)), to_high)
    of_large = dot_two(terms * dot_two(g_small, widen), to_low)
    norm = g_other[:, 0:1]
    of_other = lane_sum(of_small * g_small)
    lane = iota((rows, 128), 1)
    shares = [-norm * of_small, -norm * of_large, jnp.where(lane == 0, -of_other, 0.0)]
    one, two, three = (known[p * number : (p + 1) * number] for p in range(3))
    cells = G * G
    for part in tables_in:
        part.wait()
    w1_ref[...] = jnp.broadcast_to(lane_sum(fit_ref[...] * one[0:1]), w1_ref.shape)
    ways = [wide_ref[p] for p in range(4)]

    def weights(a, hi, lo):
        a_hi, a_lo = halves(a[:, :32])
        return dot(a_hi, hi) + dot(a_hi, lo) + dot(a_lo, hi)

    w2 = weights(two, ways[0], ways[1])
    w3 = weights(three, ways[2], ways[3])
    w23_ref[...] = w2 * w3
    lanes = cells // 128

    def over_rows(r, carry):
        copy(r).wait()

        @pl.when(r + ahead < tiles)
        def _():
            copy(r + ahead).start()

        rows_r = pl.ds(pl.multiple_of(r * tile, tile), tile)
        w23 = [w23_ref[rows_r, k * 128 : (k + 1) * 128] for k in range(lanes)]

        def over_points(g, lead):
            x = energy_ref[rows_r, pl.ds(pl.multiple_of(g * cells, cells), cells)].astype(F32)
            w1 = w1_ref[pl.ds(g, 1), :]
            fresh, along = [], None
            for k in range(lanes):
                part = x[:, k * 128 : (k + 1) * 128]
                fresh.append(lead[k] + w1 * part)
                term = part * w23[k]
                along = term if along is None else along + term
            along_ref[g] += along
            return tuple(fresh)

        none = jnp.zeros((tile, 128), F32)
        lead = lax.fori_loop(0, G, over_points, (none,) * lanes, unroll=16)
        for k in range(lanes):
            lead_ref[rows_r, k * 128 : (k + 1) * 128] = lead[k]
        return carry

    along_ref[...] = jnp.zeros_like(along_ref)
    lax.fori_loop(0, tiles, over_rows, 0)

    def back(a, hi, lo):
        a_hi, a_lo = halves(a)
        dims = (((1,), (1,)), ((), ()))
        total = lax.dot_general(a_hi, hi, dims, preferred_element_type=F32)
        total = total + lax.dot_general(a_hi, lo, dims, preferred_element_type=F32)
        total = total + lax.dot_general(a_lo, hi, dims, preferred_element_type=F32)
        return jnp.concatenate([total, jnp.zeros((number, 96), F32)], axis=1)

    sums = lane_sum(jnp.sum(along_ref[...], axis=1))
    field_first = jnp.sum(sums * fit_ref[...], axis=0, keepdims=True)
    field_first = jnp.where(iota((number, 128), 0) == 0, field_first, 0.0)
    field_second = back(lead_ref[...] * w3, ways[0], ways[1])
    field_third = back(lead_ref[...] * w2, ways[2], ways[3])
    own = known[:rows]
    lane = iota((rows, 128), 1)
    single = jnp.where(lane < 16, pltpu.roll(own, 112, 1), 0.0)
    along = lane_sum(single * own)
    norms = own[:, 0:1]
    n1, n2, n3 = (norms[p * number : (p + 1) * number] for p in range(3))
    q1, q2, q3 = (along[p * number : (p + 1) * number] for p in range(3))
    scale = jnp.concatenate([n2 * n3, n1 * n3, n1 * n2], axis=0)
    shift = jnp.concatenate([n3 * q2 + n2 * q3, n3 * q1 + n1 * q3, n2 * q1 + n1 * q2], axis=0)
    from_grid = jnp.concatenate([field_first, field_second, field_third], axis=0)
    from_grid = from_grid - scale * single - jnp.where(lane == 0, shift, 0.0)
    fields = jnp.concatenate([from_grid] + shares, axis=0)
    f_hi, f_lo = halves(fields)
    dims = (((0,), (0,)), ((), ()))
    part = lax.dot_general(pick, f_hi, dims, preferred_element_type=F32) + lax.dot_general(
        pick, f_lo, dims, preferred_element_type=F32
    )
    part = part[:peers] + sum(
        pltpu.roll(part[j * peers : (j + 1) * peers], 16 * j, 1) for j in range(1, spots)
    )
    slots = out_ref.shape[0]
    each = float(slots // peers)
    at = iota((slots, 1), 0).astype(F32)
    peer = jnp.floor((at + 0.5) * (1.0 / each))
    rest = at - each * peer
    late = rest >= per
    rank = rest - jnp.where(late, per, 0.0)
    from_peer = one_hot(peer, peers)
    seen = dot(from_peer, asked)
    off = iota((slots, 128), 1).astype(F32) - rank
    local = lane_sum(jnp.where(off == 0.0, seen, 0.0))
    turned = lane_sum(jnp.where(off == 16.0, seen, 0.0))
    terms = pick_two(one_hot(local, 256), hi_ref[...], lo_ref[...])
    terms = jnp.where(turned > 0.5, terms[:, 256:], terms[:, :256])
    terms = jnp.where(late, terms[:, 128:], terms[:, :128])
    p_hi, p_lo = halves(part)
    out_ref[...] = jnp.where(rest == 2.0 * per, pick_two(from_peer, p_hi, p_lo), terms)


def own_kernel(came_ref, out_ref):
    peers = came_ref.shape[0] // 25
    each = 25
    rows = came_ref[pl.ds(each - 1, peers, stride=each), :]
    out_ref[...] = jnp.sum(rows, axis=0, keepdims=True)


def face_kernel(*refs):
    far_ref, came_ref, known_ref, meta_ref, far_out, energy_ref, coef_ref, rest_ref, out_sems, sem = refs[NEAR:]
    fit_refs = list(refs[:NEAR]) + [rest_ref.at[c] for c in range(KEEP - NEAR)]
    coming = pltpu.make_async_copy(far_ref, rest_ref, sem)
    coming.start()
    number = coef_ref.shape[0]
    some = 4
    leaving = []
    for k in range(KEEP // some):
        cols = slice(k * some * 256, (k + 1) * some * 256)
        leaving.append(pltpu.make_async_copy(coef_ref.at[:, cols], far_out.at[:, cols], out_sems.at[k]))
    place = meta_ref[:, 0:1]
    known = known_ref[...]
    one, two, three = (known[p * number : (p + 1) * number] for p in range(3))
    hi, lo = halves(came_ref[...])
    slots = came_ref.shape[0]
    got = [pick_two(one_hot(place + 12.0 * h, slots), hi, lo) for h in range(2)]
    lane = iota((number, 128), 1)
    k, n = iota((128, 256), 0), iota((128, 256), 1)
    two_wide = dot_two(two, (k == (n >> 4)).astype(F32).astype(BF16))
    two_single = dot_two(two, ((k == (n >> 4) + 16) & ((n & 15) == 0)).astype(F32).astype(BF16))
    three_low = jnp.where((lane & 31) < 16, three, 0.0)
    three_wide = three_low + pltpu.roll(three_low, 16, 1)
    start = lane < 16
    first_pair = [g[:number] for g in got]
    first_pair[0] = first_pair[0] + jnp.where(start, pltpu.roll(one, 112, 1), 0.0)
    second_pair = [g[number : 2 * number] for g in got]
    third_pair = [g[2 * number :] for g in got]
    third_pair[0] = third_pair[0] + jnp.where(start, pltpu.roll(three, 112, 1), 0.0)
    third_pair = [t + two_single[:, h * 128 : (h + 1) * 128] for h, t in enumerate(third_pair)]
    both = [two_wide[:, h * 128 : (h + 1) * 128] * three_wide for h in range(2)]
    spaced = (lane & 15) == 0
    energy = jnp.zeros((number, 128), F32)
    for c in range(KEEP):
        if c == NEAR:
            coming.wait()
        along = jnp.zeros((number, 128), F32)
        for h in range(2):
            moved = pltpu.roll(first_pair[h], 128 - c, 1) if c else first_pair[h]
            value = fit_refs[c][:, h * 128 : (h + 1) * 128] - jnp.where(spaced, moved, 0.0)
            if h == 0:
                shift = (c % 8) * 16
                moved = second_pair[c // 8]
                moved = pltpu.roll(moved, 128 - shift, 1) if shift else moved
                value = value - jnp.where(start, moved, 0.0)
            if c == 0:
                value = value - third_pair[h]
            coef_ref[:, c * 256 + h * 128 : c * 256 + (h + 1) * 128] = value.astype(BF16)
            along = along + value * both[h]
        energy = energy + one[:, c : c + 1] * along
        if c % some == some - 1:
            leaving[c // some].start()
    energy_ref[...] = lax.dot_general(
        jnp.full((8, 128), 1.0, F32), energy, (((1,), (1,)), ((), ())), preferred_element_type=F32, precision=HIGHEST
    )[0:1]
    for copy in leaving:
        copy.wait()


def integral_kernel(*refs):
    *parts, integral_ref, out_ref = refs
    parts = [p[...] for p in parts]
    while len(parts) > 1:
        parts = [parts[i] + parts[i + 1] for i in range(0, len(parts), 2)]
    shape = (out_ref.shape[0], 128)
    total = jnp.where((iota(shape, 1) >> 4) == iota(shape, 0), parts[0], 0.0)
    out_ref[...] = dot_exact(total, integral_ref[...])


def call(kernel, outs, *args, name, apart=(), fetched=(), outs_apart=(), flops=0, scratch=()):
    moved = sum(int(np.prod(a.shape)) * a.dtype.itemsize for a in args) + sum(
        int(np.prod(o.shape)) * o.dtype.itemsize for o in outs
    )
    count = len(args) + len(outs) + len(scratch)
    pieces = {i: 4 if args[i].size * args[i].dtype.itemsize >= 2**18 else 1 for i in fetched}

    def fetching(*refs):
        refs, held, sems = list(refs[:count]), refs[count:-1], refs[-1]
        copies = []
        for i, buffer in zip(fetched, held, strict=True):
            rows = args[i].shape[0] // pieces[i]
            for k in range(pieces[i]):
                some = slice(k * rows, (k + 1) * rows)
                ends = (refs[i].at[some], buffer.at[some]) if pieces[i] > 1 else (refs[i], buffer)
                copies.append(pltpu.make_async_copy(*ends, sems.at[len(copies)]))
        for copy in copies:
            copy.start()
        for copy in copies:
            copy.wait()
        for i, buffer in zip(fetched, held, strict=True):
            refs[i] = buffer
        kernel(*refs)

    extra = []
    if fetched:
        extra = [pltpu.VMEM(args[i].shape, args[i].dtype) for i in fetched]
        extra.append(pltpu.SemaphoreType.DMA((sum(pieces.values()),)))
    outside = set(apart) | set(fetched)
    return pl.pallas_call(
        fetching if fetched else kernel,
        out_shape=outs,
        in_specs=[
            pl.BlockSpec(memory_space=pltpu.HBM if i in outside else pltpu.VMEM) for i in range(len(args))
        ],
        out_specs=[
            pl.BlockSpec(memory_space=pltpu.HBM if i in outs_apart else pltpu.VMEM) for i in range(len(outs))
        ],
        scratch_shapes=list(scratch) + extra,
        compiler_params=pltpu.CompilerParams(vmem_limit_bytes=VMEM_LIMIT),
        cost_estimate=pl.CostEstimate(flops=flops, bytes_accessed=moved, transcendentals=0),
        name=name,
    )(*(far(a) if i in outside else a for i, a in enumerate(args)))


def across(a, k):
    return lax.ppermute(a, "grp", [(i, i ^ k) for i in range(lax.axis_size("grp"))])


def far(a):
    return pltpu.with_memory_space_constraint(a, pltpu.HBM)


def shaped(shape, dtype=F32):
    return jax.ShapeDtypeStruct(shape, dtype)


def body(energies, triples, pair_surfaces, pair_slot, single_surfaces, modals, mode_slot):
    devices = lax.axis_size("dev")
    groups = lax.axis_size("grp")
    number = triples.shape[0]
    own = modals.shape[0]
    capacity = 3 * number // devices
    cos_wide = np.zeros((G, 128), np.float32)
    fit_wide = np.zeros((G, 128), np.float32)
    cos_block = np.zeros((128, own * G), np.float32)
    for m in range(own):
        cos_wide[:, m * 32 : m * 32 + KEEP] = COSINES.T
        fit_wide[:, m * 32 + KEEP : m * 32 + 2 * KEEP] = FITTER.T
        cos_block[m * KEEP : (m + 1) * KEEP, m * G : (m + 1) * G] = COSINES
    kron = np.einsum("dh,el->hlde", FITTER, FITTER).reshape(G * G, KEEP * KEEP)
    hi, lo = (jnp.asarray(x) for x in halves_np(kron))
    fit_rows = np.zeros((G, 128), np.float32)
    fit_rows[:, :KEEP] = FITTER.T
    wide = np.zeros((2, 32, G, G))
    wide[0, :KEEP] = FITTER[:, :, None]
    wide[1, :KEEP] = FITTER[:, None, :]
    wide = jnp.asarray(np.stack([h[p] for p in range(2) for h in halves_np(wide.reshape(2, 32, G * G))]))
    send, meta = call(
        ask_kernel,
        [shaped((devices, 2, 128)), shaped((3 * number, 128))],
        triples.T,
        pair_slot,
        mode_slot.reshape(1, -1),
        modals,
        single_surfaces,
        jnp.asarray(cos_wide),
        jnp.asarray(fit_wide),
        fetched=tuple(range(7)),
        name="ask",
    )
    came = lax.all_to_all(send, "dev", 0, 0, tiled=True)
    table = shaped((pair_surfaces.shape[0], 512), BF16)
    first_hi, first_lo = halves_np(np.kron(FITTER, np.eye(8)))
    first = jnp.asarray(np.concatenate([first_hi, first_lo], axis=0))
    table_hi, table_lo, integral = call(
        table_kernel,
        [table, table, shaped((128, S * S))],
        pair_surfaces,
        hi,
        lo,
        modals,
        jnp.asarray(cos_block),
        fetched=(0, 1, 2, 3, 4),
        name="table",
        flops=5 * 10**8,
    )
    each = 2 * capacity + 1
    answer, known = call(
        share_kernel,
        [shaped((devices * each, 128)), shaped((3 * number, 128))],
        came,
        table_hi,
        table_lo,
        energies,
        meta,
        jnp.asarray(fit_rows),
        wide,
        apart=(3, 5, 6),
        name="share",
        flops=10**9,
        scratch=[
            pltpu.VMEM((G, 128), F32),
            pltpu.VMEM((number, G * G), F32),
            pltpu.VMEM((number, G * G), F32),
            pltpu.VMEM((G, 16, 128), F32),
            pltpu.VMEM(energies.shape, BF16),
            pltpu.VMEM(fit_rows.shape, F32),
            pltpu.VMEM(wide.shape, BF16),
            pltpu.SemaphoreType.DMA((number // 16,)),
            pltpu.SemaphoreType.DMA((2,)),
        ],
    )
    terms = lax.all_to_all(
        answer.reshape(devices, each, 1, 128), "dev", 0, 0, tiled=True
    ).reshape(devices * each, 128)
    far_part = (KEEP - NEAR, number, KEEP**2)
    fitted = call(
        fit_kernel,
        [shaped((number, KEEP**2))] * NEAR + [pltpu.HBM(far_part, F32)],
        energies,
        hi,
        lo,
        first,
        apart=(0,),
        outs_apart=(NEAR,),
        scratch=[
            pltpu.VMEM(energies.shape, BF16),
            pltpu.VMEM(far_part, F32),
            pltpu.SemaphoreType.DMA((number // FIT_TILE, 4)),
            pltpu.SemaphoreType.DMA((number // FIT_TILE,)),
        ],
        name="fit",
        flops=5 * 10**9,
    )
    terms, fitted = lax.optimization_barrier((terms, fitted))
    (mine,) = call(own_kernel, [shaped((1, 128))], terms, name="own")
    mine = mine + across(mine, 1)
    parts = [mine] + [across(mine, k) for k in range(2, groups, 2)]
    mine, known = lax.optimization_barrier((mine, known))
    coefficients, energy = call(
        face_kernel,
        [pltpu.HBM((number, KEEP**3), BF16), shaped((1, number))],
        *fitted,
        terms,
        known,
        meta,
        apart=(NEAR,),
        outs_apart=(0,),
        scratch=[
            pltpu.VMEM((number, KEEP**3), BF16),
            pltpu.VMEM(far_part, F32),
            pltpu.SemaphoreType.DMA((4,)),
            pltpu.SemaphoreType.DMA,
        ],
        name="faces",
        flops=10**9,
    )
    (mean_field,) = call(
        integral_kernel,
        [shaped((own, S * S))],
        *parts,
        integral,
        name="integrals",
    )
    return coefficients, energy.reshape(number), mean_field


def solution(mesh):
    in_specs = (
        P(("grp", "dev"), None),
        P(("grp", "dev"), None),
        P("dev", None),
        P(),
        P("dev", None),
        P("dev", None),
        P(),
    )
    out_specs = (P(("grp", "dev"), None), P(("grp", "dev")), P("dev", None))
    return jax.shard_map(body, mesh=mesh, in_specs=in_specs, out_specs=out_specs, check_vma=False)
```
